256 devices in a mesh: dp: 16 (over y, x_lo, core), segment: 2 (over x_hi), tensor: 8 (over z).
Axes of the slice: x: 4 (x_hi: 2, x_lo: 2; x = x_hi * 2 + x_lo), y: 4, z: 8, core: 2. Of those that a mesh axis runs over, the one named last changes fastest.
Arguments:
- segment_input: bfloat16 [2, 4096, 8192], P('segment', 'dp'), may hold values from -6 to 6
- attn_gain: float32 [2, 8192], P('segment'), may hold values from 0.5 to 1.5
- query_weight: bfloat16 [2, 8192, 4096], P('segment', 'dp', 'tensor'), may hold values from -1 to 1
- kv_weight: bfloat16 [2, 8192, 1024], P('segment', 'dp', 'tensor'), may hold values from -1 to 1
- out_weight: bfloat16 [2, 4096, 8192], P('segment', 'tensor', 'dp'), may hold values from -0.09375 to 0.09375
- fm_weight: float32 [2, 2, 32, 128, 128], P('segment', None, 'tensor'), may hold values from -0.5 to 0.5
- fm_bias: float32 [2, 2, 32, 128], P('segment', None, 'tensor'), may hold values from -3 to 3
Outputs:
- handoff: bfloat16 [2, 4096, 8192], P('segment', ('dp', 'tensor'))
- fm_grad: float32 [2, 2, 32, 128, 128], P('segment', None, 'tensor')
- bias_grad: float32 [2, 2, 32, 128], P('segment', None, 'tensor')
The draws below stay inside these ranges and needn't reach their ends.
All inputs are finite; a program needn't handle non-finite values.
Results may differ from the reference program's by a relative error of at most 0.025.
Values may be sent and summed in bfloat16 or wider, within the bound.
A program may use at most 128 MiB of HBM per device.

```python
import jax
import jax.numpy as jnp
from jax import lax

D = 8192
HEADS = 32
KV_HEADS = 4
HEAD_DIM = 128
FEAT = 128
SEQ = 256
TOKENS = 4096
N_DP = 16
N_SEGMENT = 2
N_TENSOR = 8


def draw_query_weight(key, part):
    base = jax.random.truncated_normal(jax.random.fold_in(key, 1), -6.0, 6.0, (N_SEGMENT, D, HEADS * HEAD_DIM), jnp.float32) * D ** (-0.5)
    return base.astype(jnp.bfloat16)


def draw_kv_weight(key, part):
    base = jax.random.truncated_normal(jax.random.fold_in(key, 2), -6.0, 6.0, (N_SEGMENT, D, 2 * KV_HEADS * HEAD_DIM), jnp.float32) * D ** (-0.5)
    return base.astype(jnp.bfloat16)


def block_levels(own_key, dims, cuts, low, high):
    loudness, own = 1.0, jax.random.fold_in(own_key, 6)
    for position, parts in cuts:
        steps = jnp.exp(jax.random.uniform(jax.random.fold_in(own, position), (parts,), jnp.float32, low / len(cuts), high / len(cuts)))
        loudness = loudness * jnp.repeat(steps, dims[position] // parts).reshape([-1 if axis == position else 1 for axis in range(len(dims))])
    return loudness


def bell_draw(key, shape, scale, bound, cuts=(), kind=jnp.bfloat16):
    level = block_levels(key, shape, cuts, -0.22, 0.18) if cuts else 1.0
    array = jax.random.normal(key, shape, jnp.float32) * scale * level
    return jnp.minimum(jnp.maximum(array, -bound), bound).astype(kind)


def setup_inputs(seed: int = 0) -> dict:
    seeds = jax.random.split(jax.random.key(seed), 8)
    segment_input = bell_draw(seeds[0], (N_SEGMENT, TOKENS, D), 1.0, 6.0, ((0, 2), (1, 16)))
    attn_gain = jnp.clip(1.0 + 0.1 * jax.random.normal(seeds[1], (N_SEGMENT, D), jnp.float32), 0.5, 1.5)
    query_weight = draw_query_weight(jax.random.fold_in(seeds[7], 71), 0)
    kv_weight = draw_kv_weight(jax.random.fold_in(seeds[7], 71), 0)
    out_weight = bell_draw(seeds[4], (N_SEGMENT, HEADS * HEAD_DIM, D), (HEADS * HEAD_DIM) ** -0.5, 0.09375, ((0, 2), (1, 8), (2, 16)))
    fm_weight = bell_draw(seeds[5], (N_SEGMENT, 2, HEADS, HEAD_DIM, FEAT), HEAD_DIM ** -0.5, 0.5, ((0, 2), (2, 8)), jnp.float32)
    fm_bias = bell_draw(seeds[6], (N_SEGMENT, 2, HEADS, FEAT), 0.5, 3.0, ((0, 2), (2, 8)), jnp.float32)
    return {"segment_input": segment_input, "attn_gain": attn_gain, "query_weight": query_weight, "kv_weight": kv_weight, "out_weight": out_weight, "fm_weight": fm_weight, "fm_bias": fm_bias}


EPSILON = 1e-05
ROPE_BASE = 500000.0

def rope_tables(length, head_size):
    half_dim = head_size // 2
    frequency = ROPE_BASE ** (-(jnp.arange(half_dim, dtype=jnp.float32) * (2.0 / head_size)))
    angles = jnp.arange(length, dtype=jnp.float32)[:, None] * frequency[None, :]
    return (jnp.cos(angles)[:, None, :], jnp.sin(angles)[:, None, :])

def rotate_pairs(values, cosine_table, sine_table):
    half_dim = values.shape[-1] // 2
    first_half = values[..., :half_dim]
    second_half = values[..., half_dim:]
    return jnp.concatenate([first_half * cosine_table - second_half * sine_table, second_half * cosine_table + first_half * sine_table], axis=-1)

def student_loss(params, queries, keys_rep, values_rep, target, total_tokens):
    map_weight, map_bias = params
    query_pre = jnp.einsum('ihd,hdf->ihf', queries.astype(jnp.float32), map_weight[0], precision=lax.Precision.HIGHEST) + map_bias[0]
    key_pre = jnp.einsum('ihd,hdf->ihf', keys_rep.astype(jnp.float32), map_weight[1], precision=lax.Precision.HIGHEST) + map_bias[1]
    query_feat = jax.nn.elu(query_pre) + 1.0
    key_feat = jax.nn.elu(key_pre) + 1.0
    length = queries.shape[0]
    causal = (jnp.arange(length)[:, None] >= jnp.arange(length)[None, :]).astype(query_feat.dtype)
    affinity = jnp.einsum('ihf,jhf->hij', query_feat, key_feat, precision=lax.Precision.HIGHEST) * causal
    numerator = jnp.einsum('hij,jhd->ihd', affinity, values_rep.astype(jnp.float32), precision=lax.Precision.HIGHEST)
    denominator = lax.optimization_barrier(jnp.sum(affinity, axis=-1))
    linear_out = numerator / jnp.transpose(denominator)[:, :, None]
    mismatch = linear_out - target.astype(jnp.float32)
    return jnp.sum(mismatch * mismatch) / total_tokens

def teacher_layer(inputs, gain, query_local, kv_local, out_local, map_weight, map_bias):
    group = HEADS // KV_HEADS
    residual = inputs.astype(jnp.float32)
    inv_rms = lax.rsqrt(lax.optimization_barrier(jnp.mean(residual * residual, axis=-1, keepdims=True)) + EPSILON)
    normed = (residual * inv_rms * gain).astype(jnp.bfloat16)
    query_proj = jnp.dot(normed, query_local, preferred_element_type=jnp.float32).reshape(SEQ, HEADS, HEAD_DIM)
    kv_flat = jnp.dot(normed, kv_local, preferred_element_type=jnp.float32).reshape(SEQ, 2, HEAD_DIM, KV_HEADS)
    kv_proj = jnp.transpose(kv_flat, (0, 3, 1, 2))
    cosine_table, sine_table = rope_tables(SEQ, HEAD_DIM)
    queries = rotate_pairs(query_proj, cosine_table, sine_table).astype(jnp.bfloat16)
    keys = rotate_pairs(kv_proj[:, :, 0], cosine_table, sine_table).astype(jnp.bfloat16)
    values = kv_proj[:, :, 1].astype(jnp.bfloat16)
    keys_rep = jnp.repeat(keys, group, axis=1)
    values_rep = jnp.repeat(values, group, axis=1)
    scores = jnp.einsum('ihd,jhd->hij', queries.astype(jnp.float32), keys_rep.astype(jnp.float32), precision=lax.Precision.HIGHEST) * HEAD_DIM ** (-0.5)
    causal_keep = jnp.arange(SEQ)[:, None] >= jnp.arange(SEQ)[None, :]
    scores = jnp.where(causal_keep, scores, -jnp.inf)
    row_peak = lax.optimization_barrier(jnp.max(scores, axis=-1, keepdims=True))
    lifted = jnp.exp(scores - row_peak)
    probability = (lifted / lax.optimization_barrier(jnp.sum(lifted, axis=-1, keepdims=True))).astype(jnp.bfloat16)
    attended = jnp.einsum('hij,jhd->ihd', probability.astype(jnp.float32), values_rep.astype(jnp.float32), precision=lax.Precision.HIGHEST).astype(jnp.bfloat16)
    flat = attended.reshape(SEQ, N_TENSOR, HEADS * HEAD_DIM // N_TENSOR)
    out_groups = out_local.reshape(N_TENSOR, HEADS * HEAD_DIM // N_TENSOR, D)
    mixture = jnp.zeros((SEQ, D), jnp.float32)
    for tensor_num in range(N_TENSOR):
        partial_value = jnp.dot(flat[:, tensor_num], out_groups[tensor_num], preferred_element_type=jnp.float32).astype(jnp.bfloat16)
        mixture = mixture + lax.optimization_barrier(partial_value).astype(jnp.float32)
    output = (residual + mixture).astype(jnp.bfloat16)
    gradients = jax.grad(student_loss)((map_weight, map_bias), queries, keys_rep, values_rep, attended, TOKENS)
    return (output, gradients[0], gradients[1])

def reference(segment_input, attn_gain, query_weight, kv_weight, out_weight, fm_weight, fm_bias):
    outputs = []
    weight_grads = []
    bias_grads = []
    for segment_num in range(N_SEGMENT):
        sequences = segment_input[segment_num].reshape(N_DP, SEQ, D)

        def per_replica(inputs, segment_num=segment_num):
            return teacher_layer(inputs, attn_gain[segment_num], query_weight[segment_num], kv_weight[segment_num], out_weight[segment_num], fm_weight[segment_num], fm_bias[segment_num])
        output, weight_grad, bias_grad = lax.map(per_replica, sequences)
        outputs.append(output.reshape(TOKENS, D))
        weight_grads.append(lax.optimization_barrier(jnp.sum(weight_grad, axis=0)))
        bias_grads.append(lax.optimization_barrier(jnp.sum(bias_grad, axis=0)))
    handoff = jnp.stack([outputs[(segment_num - 1) % N_SEGMENT] for segment_num in range(N_SEGMENT)])
    return (handoff, jnp.stack(weight_grads), jnp.stack(bias_grads))
```

```python
import functools

import jax
import jax.numpy as jnp
import numpy as np
from jax import lax
from jax.experimental import pallas as pl
from jax.experimental.pallas import tpu as pltpu
from jax.sharding import PartitionSpec as P

MESH = pl.DeviceIdType.MESH
F32 = jnp.float32
BF16 = jnp.bfloat16
D = 8192
SEQ = 256
TOKENS = 4096
EPSILON = 1e-05
ROPE_BASE = 500000.0
SCALE = 128 ** (-0.5)

R1A = [("yp", 0, 0, 0, 2), ("ym", 0, 0, 2, 4)]
R1B = [("yp", 0, 0, 2, 4), ("ym", 0, 0, 0, 2)]
R1X = [("x", 0, 0, 1, 3)]
R1S = [("s", 0, 0, 0, 4)]
R2A = [("yp", -1, 0, 0, 2), ("ym", 1, 0, 2, 4)]
R2B = [("yp", 0, 1, 1, 3), ("ym", 0, 1, 1, 3)]
R2X = [
    ("x", 0, 0, 0, 1),
    ("x", 0, 0, 3, 4),
    ("x", -1, 0, 0, 1),
    ("x", 1, 0, 3, 4),
    ("x", -1, 0, 3, 4),
    ("x", 1, 0, 0, 1),
]
R2S = [("s", -1, 0, 0, 4), ("s", 1, 0, 0, 4)]
R3Y = [("yp", -1, 1, 1, 2), ("ym", 1, 1, 2, 3)]
R3X = [("x", 2, 0, 0, 1), ("x", 2, 0, 3, 4)]
R3S = [("s", 2, 0, 0, 4), ("s", 0, 1, 0, 4), ("s", -1, 1, 0, 4), ("s", 1, 1, 0, 4)]
R4S = [("s", 2, 1, 0, 4)]
STAGES = {}
MOVES = []
for _name, _list in (
    ("1a", R1A),
    ("1b", R1B),
    ("1x", R1X),
    ("1s", R1S),
    ("2a", R2A),
    ("2b", R2B),
    ("2x", R2X),
    ("2s", R2S),
    ("3y", R3Y),
    ("3x", R3X),
    ("3s", R3S),
    ("4s", R4S),
):
    STAGES[_name] = list(range(len(MOVES), len(MOVES) + len(_list)))
    MOVES.extend(_list)
N_MOVES = len(MOVES)
CUTS = (0, 112, 256, 400, 512)


def rope_tables():
    half = 64
    frequency = ROPE_BASE ** (-(np.arange(half, dtype=np.float64) * (2.0 / 128)))
    angles = np.arange(SEQ, dtype=np.float64)[:, None] * frequency[None, :]
    return np.cos(angles).astype(np.float32), np.sin(angles).astype(np.float32)


def mm(a, b):
    return jnp.dot(a, b, preferred_element_type=F32)


def mm_nt(a, b):
    return lax.dot_general(a, b, (((1,), (1,)), ((), ())), preferred_element_type=F32)


def mm_tn(a, b):
    return lax.dot_general(a, b, (((0,), (0,)), ((), ())), preferred_element_type=F32)


def kernel(
    x_hbm,
    gain_ref,
    wq_hbm,
    wkv_hbm,
    wo_hbm,
    fmw_ref,
    fmb_ref,
    cos_ref,
    sin_ref,
    cost_ref,
    sint_ref,
    hand_ref,
    fg_ref,
    bg_ref,
    x_ref,
    nrm,
    wkv,
    wqa,
    wqb,
    wo,
    kvacc,
    qacc,
    kvs,
    kvt,
    k_ref,
    kt_ref,
    v_ref,
    qrot,
    attb,
    stage,
    rx,
    gf,
    gs0,
    gr0,
    gs1,
    gr1,
    gy,
    ga,
    gall,
    loc_sem,
    g_send,
    g_recv,
    wz_send,
    wz_recv,
    kz_send,
    kz_recv,
    ag_send,
    ag_recv,
    gr_send,
    gr_recv,
    o_send,
    o_recv,
):
    dp = lax.axis_index("dp")
    seg = lax.axis_index("segment")
    t = lax.axis_index("tensor")
    core = dp % 2
    chip = dp // 2
    xl = chip % 2
    y = chip // 2
    sib = chip * 2 + (1 - core)
    xp = (y * 2 + (1 - xl)) * 2 + core
    yp = (dp + 4) % 16
    ym = (dp + 12) % 16
    y2 = (dp + 8) % 16
    peer = {"yp": yp, "ym": ym, "x": xp, "s": sib}

    pending = []

    def remote(src, dst, ssem, rsem, dev):
        return pltpu.make_async_remote_copy(
            src_ref=src,
            dst_ref=dst,
            send_sem=ssem,
            recv_sem=rsem,
            device_id=dev,
            device_id_type=MESH,
        )

    x_copy = pltpu.make_async_copy(x_hbm, x_ref, loc_sem.at[0])
    x_copy.start()
    locals_ = [
        pltpu.make_async_copy(wkv_hbm, wkv.at[dp], loc_sem.at[1]),
        pltpu.make_async_copy(wq_hbm.at[:, pl.ds(0, 256)], wqa.at[dp], loc_sem.at[2]),
        pltpu.make_async_copy(wq_hbm.at[:, pl.ds(256, 256)], wqb.at[dp], loc_sem.at[3]),
    ]
    for c in locals_:
        c.start()

    barrier = pltpu.get_barrier_semaphore()
    peers = [{"dp": p} for p in (sib, xp, yp, ym, y2)]
    for d in range(1, 8):
        peers.append({"tensor": (t + d) % 8})
    for d in range(1, 8):
        peers.append({"dp": sib, "tensor": (t + d) % 8})
    for d in range(8):
        peers.append({"segment": 1 - seg, "tensor": (t + d) % 8})
    for p in peers:
        pl.semaphore_signal(barrier, inc=1, device_id=p, device_id_type=MESH)
    pl.semaphore_wait(barrier, len(peers))

    def slot_of(dy, dx, c):
        return (((y + dy + 4) % 4) * 2 + (xl + dx) % 2) * 2 + c

    kinds = {
        "kv": (0, wkv, lambda lo, hi: wkv_hbm.at[pl.ds(lo, hi - lo)], 1),
        "qa": (1, wqa, lambda lo, hi: wq_hbm.at[pl.ds(lo, hi - lo), pl.ds(0, 256)], 1),
        "qb": (2, wqb, lambda lo, hi: wq_hbm.at[pl.ds(lo, hi - lo), pl.ds(256, 256)], 1),
        "o": (3, wo, None, 4),
    }

    def move(kind, k):
        index, buf, own, mult = kinds[kind]
        direction, dy, dx, lo, hi = MOVES[k]
        lo, hi = CUTS[lo] * mult, CUTS[hi] * mult
        slot = slot_of(dy, dx, core)
        dst = buf.at[slot, pl.ds(lo, hi - lo)]
        src = own(lo, hi) if (own is not None and dy == 0 and dx == 0) else dst
        return remote(
            src, dst, g_send.at[index, k], g_recv.at[index, k], {"dp": peer[direction]}
        )

    def send(kind, *names):
        for name in names:
            for k in STAGES[name]:
                c = move(kind, k)
                c.start()
                pending.append(c)

    def recv(kind, *names):
        for name in names:
            for k in STAGES[name]:
                move(kind, k).wait_recv()

    def wz(p, k):
        dst_dp = chip * 2 + k
        return remote(
            wo_hbm.at[pl.ds(k * 256, 256), pl.ds(p * 128, 128)],
            wo.at[dst_dp, pl.ds(pl.multiple_of(t * 256, 256), 256)],
            wz_send.at[p * 2 + k],
            wz_recv.at[t],
            {"dp": dst_dp, "tensor": 2 * p + core},
        )

    def wz_local(p, k):
        return pltpu.make_async_copy(
            wo_hbm.at[pl.ds(k * 256, 256), pl.ds(p * 128, 128)],
            wo.at[chip * 2 + k, pl.ds(pl.multiple_of(t * 256, 256), 256)],
            loc_sem.at[4],
        )

    def is_self(p, k):
        return jnp.logical_and(t == 2 * p + core, core == k)

    send("kv", "1a", "1x", "1b", "1s")
    for p in range(4):
        for k in range(2):

            @pl.when(jnp.logical_not(is_self(p, k)))
            def _(p=p, k=k):
                wz(p, k).start()

            @pl.when(is_self(p, k))
            def _(p=p, k=k):
                wz_local(p, k).start()

    send("qa", "1a", "1x", "1s")

    def norm_rows(r, carry):
        rows = pl.ds(pl.multiple_of(r * 16, 16), 16)
        total = jnp.zeros((16, 512), F32)
        for j in range(16):
            v = x_ref[rows, j * 512 : (j + 1) * 512].astype(F32)
            total = total + v * v
        inv = lax.rsqrt(jnp.sum(total, axis=-1, keepdims=True) * (1.0 / D) + EPSILON)
        for j in range(16):
            v = x_ref[rows, j * 512 : (j + 1) * 512].astype(F32)
            nrm[j, rows, :] = (v * inv * gain_ref[:, j * 512 : (j + 1) * 512]).astype(BF16)
        return carry

    x_copy.wait()
    lax.fori_loop(0, 6, norm_rows, 0)

    recv("kv", "1a")
    send("kv", "2a")
    recv("kv", "1x")
    send("kv", "2b")
    recv("kv", "1b")
    send("kv", "2x", "2s")
    send("qa", "1b")

    lax.fori_loop(6, 16, norm_rows, 0)

    recv("kv", "2a", "2b", "2x")
    send("kv", "3y", "3x", "3s")
    recv("qa", "1a")
    send("qa", "2a")
    send("qb", "1a", "1x", "1s")
    for c in locals_:
        c.wait()

    def eat(acc, buf, cols, first, wave):
        width = cols[1] - cols[0]

        def add(i, carry):
            c = jnp.where(i % 2 == 0, core, 1 - core)
            n = i // 2
            if wave == 1:
                dy, dx = n + 3, 0
            elif wave == 2:
                dy, dx = n + 3, 1 - n // 3
            else:
                dy, dx = n + 2, 1
            slot = slot_of(dy, dx, c)
            acc[:, cols[0] : cols[1]] += mm(nrm[slot], buf[slot])
            return carry

        if first:
            acc[:, cols[0] : cols[1]] = jnp.zeros((SEQ, width), F32)
        lax.fori_loop(0, {1: 6, 2: 8, 3: 2}[wave], add, 0)

    recv("kv", "1s", "2s")
    eat(kvacc, wkv, (0, 128), True, 1)
    recv("qa", "1x")
    send("qa", "2b")
    recv("qa", "1b")
    send("qa", "2x", "2s")
    send("qb", "1b")
    recv("kv", "3s")
    eat(kvacc, wkv, (0, 128), False, 2)
    recv("kv", "3y", "3x")
    send("kv", "4s")
    recv("kv", "4s")
    eat(kvacc, wkv, (0, 128), False, 3)

    r_i = lax.broadcasted_iota(jnp.int32, (128, 128), 0)
    c_i = lax.broadcasted_iota(jnp.int32, (128, 128), 1)
    pick = (c_i == (r_i & 31) * 4 + (r_i >> 5)).astype(BF16)
    kvs[...] = mm_nt(pick, kvacc[...].astype(BF16)).astype(BF16)

    def kz(d):
        dest = (t + d) % 8
        return remote(
            kvs.at[pl.ds(pl.multiple_of((dest // 2) * 32, 32), 32)],
            kvt.at[t],
            kz_send.at[d],
            kz_recv.at[d],
            {"tensor": dest},
        )

    for d in range(1, 8):
        c = kz(d)
        c.start()
        pending.append(c)
    kvt[t] = kvs[pl.ds(pl.multiple_of((t // 2) * 32, 32), 32), :]

    recv("qa", "1s", "2s")
    eat(qacc, wqa, (0, 256), True, 1)
    recv("qa", "2a", "2b", "2x")
    send("qa", "3y", "3x", "3s")
    recv("qb", "1a")
    send("qb", "2a")
    recv("qb", "1x")
    send("qb", "2b")
    recv("qb", "1b")
    send("qb", "2x", "2s")

    for ts in range(8):
        here = jnp.logical_and(t == ts, core == t % 2)

        @pl.when(jnp.logical_not(here))
        def _(ts=ts):
            remote(
                wo_hbm.at[pl.ds(0, 256), pl.ds(0, 128)],
                wo.at[dp, pl.ds(ts * 256, 256)],
                wz_send.at[0],
                wz_recv.at[ts],
                {"dp": sib},
            ).wait_recv()

        @pl.when(here)
        def _():
            wz_local(0, 0).wait()

    send("o", "1a", "1x", "1s")
    recv("qa", "3s")
    eat(qacc, wqa, (0, 256), False, 2)

    for d in range(1, 8):
        kz(d).wait_recv()
    kall = kvt[0:4].reshape(128, SEQ).astype(F32)
    k1, k2 = kall[0:64], kall[64:128]
    ct, st = cost_ref[...], sint_ref[...]
    krot = jnp.concatenate([k1 * ct - k2 * st, k2 * ct + k1 * st], axis=0)
    kt_ref[...] = krot.astype(BF16)
    k_ref[...] = krot.T.astype(BF16)
    v_ref[...] = kvt[4:8].reshape(128, SEQ).astype(F32).T.astype(BF16)

    recv("qa", "3y", "3x")
    send("qa", "4s")
    recv("qa", "4s")
    eat(qacc, wqa, (0, 256), False, 3)

    row_i = lax.broadcasted_iota(jnp.int32, (SEQ, SEQ), 0)
    col_i = lax.broadcasted_iota(jnp.int32, (SEQ, SEQ), 1)

    def attend(h):
        q = qacc[:, h * 128 : (h + 1) * 128]
        q = (q * cos_ref[...] + pltpu.roll(q, 64, 1) * sin_ref[...]).astype(BF16)
        qrot[h] = q
        scores = mm(q, kt_ref[...]) * SCALE
        scores = jnp.where(row_i >= col_i, scores, -jnp.inf)
        lifted = jnp.exp(scores - jnp.max(scores, axis=-1, keepdims=True))
        prob = (lifted / jnp.sum(lifted, axis=-1, keepdims=True)).astype(BF16)
        c0 = (h % 2) * 128
        attb[h // 2, t, :, c0 : c0 + 128] = mm(prob, v_ref[...]).astype(BF16)

    def ag(k, m):
        up, lo, n = [
            (True, 0, None),
            (False, 0, None),
            (True, -1, None),
            (False, 1, None),
            (True, -2, None),
            (False, 2, None),
            (True, -3, 0),
            (False, 3, 128),
        ][m]
        slot = (t + lo + 8) % 8
        ref = attb.at[k, slot] if n is None else attb.at[k, slot, pl.ds(n, 128)]
        dest = (t + 1) % 8 if up else (t + 7) % 8
        return remote(ref, ref, ag_send.at[k, m], ag_recv.at[k, m], {"tensor": dest})

    def ag_step(k, s):
        for m in (2 * s, 2 * s + 1):
            if s > 0:
                ag(k, m - 2).wait_recv()
            c = ag(k, m)
            c.start()
            pending.append(c)

    attend(0)
    attend(1)
    ag_step(0, 0)

    recv("qb", "1s", "2s")
    eat(qacc, wqb, (256, 512), True, 1)
    recv("qb", "2a", "2b", "2x")
    send("qb", "3y", "3x", "3s")
    send("o", "1b")
    ag_step(0, 1)
    recv("qb", "3s")
    eat(qacc, wqb, (256, 512), False, 2)
    recv("qb", "3y", "3x")
    send("qb", "4s")
    ag_step(0, 2)
    recv("qb", "4s")
    eat(qacc, wqb, (256, 512), False, 3)
    attend(2)
    attend(3)
    ag_step(1, 0)
    ag_step(0, 3)

    mask = row_i >= col_i
    lead = (lax.broadcasted_iota(jnp.int32, (16, 128), 0) == 0).astype(F32)

    def feature(z):
        e = jnp.exp(jnp.minimum(z, 0.0))
        pos = z > 0
        return jnp.where(pos, z + 1.0, e).astype(BF16), jnp.where(pos, 1.0, e)

    def pre(a, m, h):
        w = fmw_ref[m, h]
        hi = w.astype(BF16)
        low = (w - hi.astype(F32)).astype(BF16)
        return mm(a, hi) + mm(a, low) + fmb_ref[m, pl.ds(h, 1), :]

    def student(h):
        q, k, v = qrot[h], k_ref[...], v_ref[...]
        att = attb[h // 2, t, :, (h % 2) * 128 : (h % 2) * 128 + 128].astype(F32)
        qf, qd = feature(pre(q, 0, h))
        kf, kd = feature(pre(k, 1, h))
        aff = jnp.where(mask, mm_nt(qf, kf), 0.0)
        den = jnp.sum(aff, axis=-1, keepdims=True)
        out = mm(aff.astype(BF16), v) / den
        dnum = ((out - att) * (2.0 / TOKENS) / den).astype(BF16)
        dden = jnp.sum(dnum.astype(F32) * out, axis=-1, keepdims=True)
        daff = jnp.where(mask, mm_nt(dnum, v) - dden, 0.0).astype(BF16)
        dzq = mm(daff, kf) * qd
        dzk = mm_tn(daff, qf) * kd
        gf[0, h, 0:128, :] = mm_tn(q, dzq.astype(BF16))
        gf[1, h, 0:128, :] = mm_tn(k, dzk.astype(BF16))
        gf[0, h, 128:144, :] = jnp.sum(dzq, axis=0, keepdims=True) * lead
        gf[1, h, 128:144, :] = jnp.sum(dzk, axis=0, keepdims=True) * lead

    student(0)
    recv("o", "1a")
    send("o", "2a")
    recv("o", "1x")
    send("o", "2b")
    ag_step(1, 1)
    student(1)
    recv("o", "1b")
    send("o", "2x", "2s")
    ag_step(1, 2)
    student(2)
    ag_step(1, 3)
    student(3)

    def grad_move(n, src, dst, dev):
        return remote(src, dst, gr_send.at[n], gr_recv.at[n], {"dp": dev})

    g0 = grad_move(0, gs0, gr0, sib)
    gs0[...] = gf[1 - core].astype(BF16)
    g0.start()
    pending.append(g0)

    recv("o", "2a", "2b", "2x")
    send("o", "3y", "3x", "3s")

    g0.wait_recv()
    mine = pl.ds(2 * xl, 2)
    theirs = pl.ds(2 * (1 - xl), 2)
    gs1[...] = (gf[core, theirs] + gr0[theirs].astype(F32)).astype(BF16)
    g1 = grad_move(1, gs1, gr1, xp)
    g1.start()
    pending.append(g1)

    for k in range(2):
        for m in (6, 7) if k == 0 else (6, 7):
            ag(k, m).wait_recv()

    def column(plane, c):
        return pl.multiple_of((2 * c + plane % 2) * 512 + (plane // 2) * 128, 128)

    def project(n, carry):
        c = slot_of(jnp.where(n < 6, n % 3 + 3, 2), jnp.where(n < 6, n // 3, n - 6), 0) // 2
        total = x_ref[:, pl.ds(column(t, c), 128)].astype(F32)
        acc = jnp.zeros((SEQ, 128), F32)
        for k in range(2):
            for ts in range(8):
                acc = acc + mm(attb[k, ts], wo[2 * c + k, ts * 256 : (ts + 1) * 256, :])
        stage[n] = (total + acc).astype(BF16)
        return carry

    def ship(w, n0, n1):
        def out(d):
            dest = (t + d) % 8
            return remote(
                stage.at[pl.ds(n0, n1 - n0), pl.ds(pl.multiple_of(dest * 32, 32), 32)],
                rx.at[t, pl.ds(n0, n1 - n0)],
                o_send.at[w, d],
                o_recv.at[w, d],
                {"segment": 1 - seg, "tensor": dest},
            )

        return [out(d) for d in range(8)]

    waves = [ship(0, 0, 3), ship(1, 3, 7), ship(2, 7, 8)]

    def go(w):
        for c in waves[w]:
            c.start()
            pending.append(c)

    recv("o", "1s", "2s")
    lax.fori_loop(0, 3, project, 0)
    go(0)

    g1.wait_recv()
    gy[y] = (gf[core, mine] + gr0[mine].astype(F32) + gr1[...].astype(F32)).astype(BF16)
    gys = [grad_move(2 + d, gy.at[y], gy.at[y], (dp + 4 * d) % 16) for d in (1, 2, 3)]
    for c in gys:
        c.start()
        pending.append(c)

    recv("o", "3s")
    lax.fori_loop(3, 7, project, 0)
    go(1)

    for c in gys:
        c.wait_recv()
    total = gy[0].astype(F32)
    for j in range(1, 4):
        total = total + gy[j].astype(F32)
    ga[mine] = total.astype(BF16)
    g5 = grad_move(6, ga.at[mine], ga.at[mine], xp)
    g5.start()
    pending.append(g5)

    recv("o", "3y", "3x")
    send("o", "4s")
    g5.wait_recv()
    g6 = grad_move(7, ga, gall, sib)
    g6.start()
    pending.append(g6)

    recv("o", "4s")
    lax.fori_loop(7, 8, project, 0)
    go(2)

    g6.wait_recv()
    own, other = ga[...].astype(F32), gall[...].astype(F32)
    fg_ref[core] = own[:, 0:128, :]
    fg_ref[1 - core] = other[:, 0:128, :]
    for h in range(4):
        bg_ref[core, h : h + 1, :] = own[h, 128:129, :]
        bg_ref[1 - core, h : h + 1, :] = other[h, 128:129, :]

    for w in range(3):
        for c in waves[w]:
            c.wait_recv()

    def place(i, carry):
        plane, n = i // 8, i % 8
        c = slot_of(jnp.where(n < 6, n % 3 + 3, 2), jnp.where(n < 6, n // 3, n - 6), 0) // 2
        hand_ref[:, pl.ds(column(plane, c), 128)] = rx[plane, n]
        return carry

    lax.fori_loop(0, 64, place, 0)

    for p in range(4):
        for k in range(2):

            @pl.when(jnp.logical_not(is_self(p, k)))
            def _(p=p, k=k):
                wz(p, k).wait_send()

    for c in pending:
        c.wait_send()


def body(segment_input, attn_gain, query_weight, kv_weight, out_weight, fm_weight, fm_bias):
    cos, sin = rope_tables()
    cos2 = jnp.asarray(np.concatenate([cos, cos], axis=1))
    sin2 = jnp.asarray(np.concatenate([-sin, sin], axis=1))
    cost, sint = jnp.asarray(cos.T.copy()), jnp.asarray(sin.T.copy())
    anywhere = pl.BlockSpec(memory_space=pl.ANY)
    vmem = pl.BlockSpec(memory_space=pltpu.VMEM)
    dma = pltpu.SemaphoreType.DMA
    handoff, fg, bg = pl.pallas_call(
        kernel,
        out_shape=(
            jax.ShapeDtypeStruct((32, D), BF16),
            jax.ShapeDtypeStruct((2, 4, 128, 128), F32),
            jax.ShapeDtypeStruct((2, 4, 128), F32),
        ),
        in_specs=[anywhere, vmem, anywhere, anywhere, anywhere] + [vmem] * 6,
        out_specs=(vmem, vmem, vmem),
        scratch_shapes=[
            pltpu.VMEM((SEQ, D), BF16),
            pltpu.VMEM((16, SEQ, 512), BF16),
            pltpu.VMEM((16, 512, 128), BF16),
            pltpu.VMEM((16, 512, 256), BF16),
            pltpu.VMEM((16, 512, 256), BF16),
            pltpu.VMEM((16, 2048, 128), BF16),
            pltpu.VMEM((SEQ, 128), F32),
            pltpu.VMEM((SEQ, 512), F32),
            pltpu.VMEM((128, SEQ), BF16),
            pltpu.VMEM((8, 32, SEQ), BF16),
            pltpu.VMEM((SEQ, 128), BF16),
            pltpu.VMEM((128, SEQ), BF16),
            pltpu.VMEM((SEQ, 128), BF16),
            pltpu.VMEM((4, SEQ, 128), BF16),
            pltpu.VMEM((2, 8, SEQ, 256), BF16),
            pltpu.VMEM((8, SEQ, 128), BF16),
            pltpu.VMEM((8, 8, 32, 128), BF16),
            pltpu.VMEM((2, 4, 144, 128), F32),
            pltpu.VMEM((4, 144, 128), BF16),
            pltpu.VMEM((4, 144, 128), BF16),
            pltpu.VMEM((2, 144, 128), BF16),
            pltpu.VMEM((2, 144, 128), BF16),
            pltpu.VMEM((4, 2, 144, 128), BF16),
            pltpu.VMEM((4, 144, 128), BF16),
            pltpu.VMEM((4, 144, 128), BF16),
            dma((5,)),
            dma((4, N_MOVES)),
            dma((4, N_MOVES)),
            dma((8,)),
            dma((8,)),
            dma((8,)),
            dma((8,)),
            dma((2, 8)),
            dma((2, 8)),
            dma((8,)),
            dma((8,)),
            dma((3, 8)),
            dma((3, 8)),
        ],
        compiler_params=pltpu.CompilerParams(
            collective_id=0,
            has_side_effects=True,
            vmem_limit_bytes=60 * 1024 * 1024,
        ),
    )(
        segment_input[0],
        attn_gain,
        query_weight[0],
        kv_weight[0],
        out_weight[0],
        fm_weight[0],
        fm_bias[0],
        cos2,
        sin2,
        cost,
        sint,
    )
    return handoff[None], fg[None], bg[None]


def solution(mesh):
    placed = (
        P("segment", "dp", None),
        P("segment", None),
        P("segment", "dp", "tensor"),
        P("segment", "dp", "tensor"),
        P("segment", "tensor", "dp"),
        P("segment", None, "tensor", None, None),
        P("segment", None, "tensor", None),
    )
    return jax.shard_map(
        body,
        mesh=mesh,
        in_specs=placed,
        out_specs=(
            P("segment", ("dp", "tensor"), None),
            P("segment", None, "tensor", None, None),
            P("segment", None, "tensor", None),
        ),
        check_vma=False,
    )
```

```python
import jax
import jax.numpy as jnp
import numpy as np
from jax import lax
from jax.experimental import pallas as pl
from jax.experimental.pallas import tpu as pltpu
from jax.sharding import PartitionSpec as P

MESH = pl.DeviceIdType.MESH
F32 = jnp.float32
BF16 = jnp.bfloat16
D = 8192
SEQ = 256
TOKENS = 4096
EPSILON = 1e-05
ROPE_BASE = 500000.0
SCALE = 128 ** (-0.5)

STAGE_MOVES = {
    "1a": [("yp", 0, 0, 0, 2), ("ym", 0, 0, 2, 4)],
    "1b": [("yp", 0, 0, 2, 4), ("ym", 0, 0, 0, 2)],
    "1x": [("x", 0, 0, 1, 3)],
    "1o": [("x", 0, 0, 0, 1), ("x", 0, 0, 3, 4)],
    "1s": [("s", 0, 0, 0, 4)],
    "2a": [("yp", -1, 0, 0, 2), ("ym", 1, 0, 2, 4)],
    "2b": [("yp", 0, 1, 1, 2), ("ym", 0, 1, 2, 3)],
    "2c": [("yp", 0, 1, 2, 3), ("ym", 0, 1, 1, 2)],
    "2xa": [("x", -1, 0, 0, 1), ("x", 1, 0, 3, 4)],
    "2xb": [("x", -1, 0, 3, 4), ("x", 1, 0, 0, 1)],
    "2s": [("s", -1, 0, 0, 4), ("s", 1, 0, 0, 4)],
    "3y": [("yp", -1, 1, 1, 2), ("ym", 1, 1, 2, 3)],
    "3x": [("x", 2, 0, 0, 1), ("x", 2, 0, 3, 4)],
    "3sa": [("s", 0, 1, 0, 4)],
    "3sb": [("s", 2, 0, 0, 4)],
    "3sc": [("s", -1, 1, 0, 4), ("s", 1, 1, 0, 4)],
    "4s": [("s", 2, 1, 0, 4)],
}
STAGES = {}
MOVES = []
for _name, _list in STAGE_MOVES.items():
    STAGES[_name] = list(range(len(MOVES), len(MOVES) + len(_list)))
    MOVES.extend(_list)
N_MOVES = len(MOVES)
CUTS = (0, 112, 256, 400, 512)


def rope_tables():
    half = 64
    frequency = ROPE_BASE ** (-(np.arange(half, dtype=np.float64) * (2.0 / 128)))
    angles = np.arange(SEQ, dtype=np.float64)[:, None] * frequency[None, :]
    return np.cos(angles).astype(np.float32), np.sin(angles).astype(np.float32)


def mm(a, b):
    return jnp.dot(a, b, preferred_element_type=F32)


def mm_nt(a, b):
    return lax.dot_general(a, b, (((1,), (1,)), ((), ())), preferred_element_type=F32)


def mm_tn(a, b):
    return lax.dot_general(a, b, (((0,), (0,)), ((), ())), preferred_element_type=F32)


def kernel(
    x_hbm,
    gain_hbm,
    wq_hbm,
    wkv_hbm,
    wo_hbm,
    fmw_hbm,
    fmb_hbm,
    cos_hbm,
    sin_hbm,
    cost_hbm,
    sint_hbm,
    hand_hbm,
    gfin,
    x_ref,
    gain_ref,
    fmw_ref,
    fmb_ref,
    cos_ref,
    sin_ref,
    cost_ref,
    sint_ref,
    nrm,
    wkv,
    wqa,
    wqb,
    wo,
    kvacc,
    qacc,
    kvs,
    kvt,
    k_ref,
    kt_ref,
    v_ref,
    qrot,
    attb,
    stage,
    gf,
    gs0,
    gr0,
    gs1,
    gr1,
    ga,
    gall,
    loc_sem,
    g_send,
    g_recv,
    wz_send,
    wz_recv,
    kz_send,
    kz_recv,
    ag_send,
    ag_recv,
    gr_send,
    gr_recv,
    o_send,
    o_recv,
):
    dp = lax.axis_index("dp")
    seg = lax.axis_index("segment")
    t = lax.axis_index("tensor")
    core = dp % 2
    chip = dp // 2
    xl = chip % 2
    y = chip // 2
    sib = chip * 2 + (1 - core)
    xp = (y * 2 + (1 - xl)) * 2 + core
    yp = (dp + 4) % 16
    ym = (dp + 12) % 16
    peer = {"yp": yp, "ym": ym, "x": xp, "s": sib}

    pending = []

    def scope(name):
        return jax.named_scope(name)

    def remote(src, dst, ssem, rsem, dev):
        return pltpu.make_async_remote_copy(
            src_ref=src,
            dst_ref=dst,
            send_sem=ssem,
            recv_sem=rsem,
            device_id=dev,
            device_id_type=MESH,
        )

    def launch(c):
        c.start()
        pending.append(c)

    local = {}
    for n, (name, src, dst) in enumerate(
        (
            ("x", x_hbm, x_ref),
            ("gain", gain_hbm, gain_ref),
            ("kv", wkv_hbm, wkv.at[dp]),
            ("qa", wq_hbm.at[:, pl.ds(0, 256)], wqa.at[dp]),
            ("qb", wq_hbm.at[:, pl.ds(256, 256)], wqb.at[dp]),
            ("cos", cos_hbm, cos_ref),
            ("sin", sin_hbm, sin_ref),
            ("cost", cost_hbm, cost_ref),
            ("sint", sint_hbm, sint_ref),
            ("fmw", fmw_hbm, fmw_ref),
            ("fmb", fmb_hbm, fmb_ref),
        )
    ):
        local[name] = pltpu.make_async_copy(src, dst, loc_sem.at[n])
        local[name].start()

    def chip_at(dy, dx):
        return ((y + dy + 4) % 4) * 2 + (xl + dx) % 2

    def slot_of(dy, dx, c):
        return chip_at(dy, dx) * 2 + c

    barrier = pltpu.get_barrier_semaphore()
    peers = [{"dp": sib}]
    for n in range(1, 8):
        peers.append({"dp": slot_of(n % 4, n // 4, core)})
    for d in range(1, 8):
        peers.append({"tensor": (t + d) % 8})
    for d in range(1, 8):
        peers.append({"dp": sib, "tensor": (t + d) % 8})
    for d in range(8):
        peers.append({"segment": 1 - seg, "tensor": (t + d) % 8})
    for p in peers:
        pl.semaphore_signal(barrier, inc=1, device_id=p, device_id_type=MESH)
    with scope("barrier"):
        pl.semaphore_wait(barrier, len(peers))

    kinds = {
        "kv": (0, wkv, lambda lo, hi: wkv_hbm.at[pl.ds(lo, hi - lo)], 1),
        "qa": (1, wqa, lambda lo, hi: wq_hbm.at[pl.ds(lo, hi - lo), pl.ds(0, 256)], 1),
        "qb": (2, wqb, lambda lo, hi: wq_hbm.at[pl.ds(lo, hi - lo), pl.ds(256, 256)], 1),
        "o": (3, wo, None, 4),
    }

    def move(kind, k):
        index, buf, own, mult = kinds[kind]
        direction, dy, dx, lo, hi = MOVES[k]
        lo, hi = CUTS[lo] * mult, CUTS[hi] * mult
        slot = slot_of(dy, dx, core)
        dst = buf.at[slot, pl.ds(lo, hi - lo)]
        src = own(lo, hi) if (own is not None and dy == 0 and dx == 0) else dst
        return remote(
            src, dst, g_send.at[index, k], g_recv.at[index, k], {"dp": peer[direction]}
        )

    def send(kind, *names):
        for name in names:
            for k in STAGES[name]:
                launch(move(kind, k))

    def recv(kind, *names):
        with scope("W_%s_%s" % (kind, "_".join(names))):
            for name in names:
                for k in STAGES[name]:
                    move(kind, k).wait_recv()

    def first(kind):
        send(kind, "1a", "1x", "1b", "1o", "1s")

    def second(kind):
        recv(kind, "1a")
        send(kind, "2a", "2xa")
        recv(kind, "1x")
        send(kind, "2b", "2c")
        recv(kind, "1b")
        send(kind, "2xb", "2s")

    def wz(p, k):
        dst_dp = chip * 2 + k
        return remote(
            wo_hbm.at[pl.ds(k * 256, 256), pl.ds(p * 128, 128)],
            wo.at[dst_dp, pl.ds(pl.multiple_of(t * 256, 256), 256)],
            wz_send.at[p * 2 + k],
            wz_recv.at[t],
            {"dp": dst_dp, "tensor": 2 * p + core},
        )

    def wz_local(p, k):
        return pltpu.make_async_copy(
            wo_hbm.at[pl.ds(k * 256, 256), pl.ds(p * 128, 128)],
            wo.at[chip * 2 + k, pl.ds(pl.multiple_of(t * 256, 256), 256)],
            loc_sem.at[11],
        )

    def is_self(p, k):
        return jnp.logical_and(t == 2 * p + core, core == k)

    first("kv")
    for p in range(4):
        for k in range(2):

            @pl.when(jnp.logical_not(is_self(p, k)))
            def _(p=p, k=k):
                wz(p, k).start()

            @pl.when(is_self(p, k))
            def _(p=p, k=k):
                wz_local(p, k).start()

    def norm_rows(r, carry):
        rows = pl.ds(pl.multiple_of(r * 16, 16), 16)
        total = jnp.zeros((16, 512), F32)
        for j in range(16):
            v = x_ref[rows, j * 512 : (j + 1) * 512].astype(F32)
            total = total + v * v
        inv = lax.rsqrt(jnp.sum(total, axis=-1, keepdims=True) * (1.0 / D) + EPSILON)
        for j in range(16):
            v = x_ref[rows, j * 512 : (j + 1) * 512].astype(F32)
            nrm[j, rows, :] = (v * inv * gain_ref[:, j * 512 : (j + 1) * 512]).astype(BF16)
        return carry

    local["x"].wait()
    local["gain"].wait()
    with scope("norm1"):
        lax.fori_loop(0, 8, norm_rows, 0)
    second("kv")
    with scope("norm2"):
        lax.fori_loop(8, 16, norm_rows, 0)

    def eat(name, acc, buf, cols, start, wave):
        def add(i, carry):
            c = jnp.where(i % 2 == 0, core, 1 - core)
            n = i // 2
            if wave == 1:
                dy, dx = n + 3, 0
            elif wave == 2:
                dy, dx = n + 3, 1 - n // 3
            else:
                dy, dx = n + 2, 1
            slot = slot_of(dy, dx, c)
            acc[:, cols[0] : cols[1]] += mm(nrm[slot], buf[slot])
            return carry

        with scope("eat_%s%d" % (name, wave)):
            if start:
                acc[:, cols[0] : cols[1]] = jnp.zeros((SEQ, cols[1] - cols[0]), F32)
            lax.fori_loop(0, {1: 6, 2: 8, 3: 2}[wave], add, 0)

    def third(kind, then=None):
        recv(kind, "2a")
        send(kind, "3x")
        recv(kind, "2b")
        send(kind, "3y")
        if then is not None:
            first(then)
        send(kind, "3sb")
        recv(kind, "1o")
        send(kind, "3sa")
        recv(kind, "2c", "2xa", "2xb")
        send(kind, "3sc")

    def fourth(kind):
        recv(kind, "3y", "3x")
        send(kind, "4s")

    third("kv", "qa")
    local["kv"].wait()
    recv("kv", "1s", "2s")
    eat("kv", kvacc, wkv, (0, 128), True, 1)
    fourth("kv")
    second("qa")
    recv("kv", "3sa", "3sb", "3sc")
    eat("kv", kvacc, wkv, (0, 128), False, 2)
    recv("kv", "4s")
    eat("kv", kvacc, wkv, (0, 128), False, 3)

    r_i = lax.broadcasted_iota(jnp.int32, (128, 128), 0)
    c_i = lax.broadcasted_iota(jnp.int32, (128, 128), 1)
    pick = (c_i == (r_i & 31) * 4 + (r_i >> 5)).astype(BF16)
    kvs[...] = mm_nt(pick, kvacc[...].astype(BF16)).astype(BF16)

    def kz(d):
        dest = (t + d) % 8
        return remote(
            kvs.at[pl.ds(pl.multiple_of((dest // 2) * 32, 32), 32)],
            kvt.at[t],
            kz_send.at[d],
            kz_recv.at[d],
            {"tensor": dest},
        )

    for d in range(1, 8):
        launch(kz(d))
    kvt[t] = kvs[pl.ds(pl.multiple_of((t // 2) * 32, 32), 32), :]

    local["qa"].wait()
    recv("qa", "1s", "2s")
    eat("qa", qacc, wqa, (0, 256), True, 1)
    third("qa", "qb")

    for name in ("cos", "sin", "cost", "sint"):
        local[name].wait()
    with scope("Wkz"):
        for d in range(1, 8):
            kz(d).wait_recv()
    kall = kvt[0:4].reshape(128, SEQ).astype(F32)
    k1, k2 = kall[0:64], kall[64:128]
    ct, st = cost_ref[...], sint_ref[...]
    krot = jnp.concatenate([k1 * ct - k2 * st, k2 * ct + k1 * st], axis=0)
    kt_ref[...] = krot.astype(BF16)
    k_ref[...] = krot.T.astype(BF16)
    v_ref[...] = kvt[4:8].reshape(128, SEQ).astype(F32).T.astype(BF16)

    fourth("qa")
    recv("qa", "3sa", "3sb", "3sc")
    eat("qa", qacc, wqa, (0, 256), False, 2)
    second("qb")
    recv("qa", "4s")
    eat("qa", qacc, wqa, (0, 256), False, 3)

    row_i = lax.broadcasted_iota(jnp.int32, (SEQ, SEQ), 0)
    col_i = lax.broadcasted_iota(jnp.int32, (SEQ, SEQ), 1)
    mask = row_i >= col_i

    def attend(h):
        with scope("attend%d" % h):
            q = qacc[:, h * 128 : (h + 1) * 128]
            q = (q * cos_ref[...] + pltpu.roll(q, 64, 1) * sin_ref[...]).astype(BF16)
            qrot[h] = q
            scores = mm(q, kt_ref[...]) * SCALE
            scores = jnp.where(mask, scores, -jnp.inf)
            lifted = jnp.exp(scores - jnp.max(scores, axis=-1, keepdims=True))
            prob = (lifted / jnp.sum(lifted, axis=-1, keepdims=True)).astype(BF16)
            c0 = (h % 2) * 128
            attb[h // 2, t, :, c0 : c0 + 128] = mm(prob, v_ref[...]).astype(BF16)

    def ag(k, s, up, half):
        slot = (t + 8 - s) % 8 if up else (t + s) % 8
        ref = attb.at[k, slot, pl.ds(half * 128, 128)]
        dest = (t + 1) % 8 if up else (t + 7) % 8
        n = s * 4 + (0 if up else 2) + half
        return remote(ref, ref, ag_send.at[k, n], ag_recv.at[k, n], {"tensor": dest})

    def ag_step(k, s, half):
        if s > 0:
            with scope("Wag%d_%d_%d" % (k, s, half)):
                ag(k, s - 1, True, half).wait_recv()
                ag(k, s - 1, False, half).wait_recv()
        if s < 3 or half == 0:
            launch(ag(k, s, True, half))
        if s < 3 or half == 1:
            launch(ag(k, s, False, half))

    def ag_end(k):
        with scope("Wag%d_end" % k):
            ag(k, 3, True, 0).wait_recv()
            ag(k, 3, False, 1).wait_recv()

    lead = (lax.broadcasted_iota(jnp.int32, (16, 128), 0) == 0).astype(F32)

    def feature(z):
        e = jnp.exp(jnp.minimum(z, 0.0))
        pos = z > 0
        return jnp.where(pos, z + 1.0, e).astype(BF16), jnp.where(pos, 1.0, e)

    def pre(a, m, h):
        w = fmw_ref[m, h]
        hi = w.astype(BF16)
        low = (w - hi.astype(F32)).astype(BF16)
        return mm(a, hi) + mm(a, low) + fmb_ref[m, pl.ds(h, 1), :]

    def put(m, h, weight, bias):
        gf[m, 2 * h, 0:64, :] = weight[0:64]
        gf[m, 2 * h + 1, 0:64, :] = weight[64:128]
        gf[m, 2 * h, 64:80, :] = bias * lead
        gf[m, 2 * h + 1, 64:80, :] = jnp.zeros((16, 128), F32)

    def student(h):
        with scope("student%d" % h):
            q, k, v = qrot[h], k_ref[...], v_ref[...]
            att = attb[h // 2, t, :, (h % 2) * 128 : (h % 2) * 128 + 128].astype(F32)
            qf, qd = feature(pre(q, 0, h))
            kf, kd = feature(pre(k, 1, h))
            aff = jnp.where(mask, mm_nt(qf, kf), 0.0)
            den = jnp.sum(aff, axis=-1, keepdims=True)
            out = mm(aff.astype(BF16), v) / den
            dnum = ((out - att) * (2.0 / TOKENS) / den).astype(BF16)
            dden = jnp.sum(dnum.astype(F32) * out, axis=-1, keepdims=True)
            daff = jnp.where(mask, mm_nt(dnum, v) - dden, 0.0).astype(BF16)
            dzq = mm(daff, kf) * qd
            dzk = mm_tn(daff, qf) * kd
            put(0, h, mm_tn(q, dzq.astype(BF16)), jnp.sum(dzq, axis=0, keepdims=True))
            put(1, h, mm_tn(k, dzk.astype(BF16)), jnp.sum(dzk, axis=0, keepdims=True))

    attend(0)
    attend(1)
    ag_step(0, 0, 0)
    ag_step(0, 0, 1)

    local["qb"].wait()
    recv("qb", "1s", "2s")
    eat("qb", qacc, wqb, (256, 512), True, 1)

    for ts in range(8):
        here = jnp.logical_and(t == ts, core == t % 2)

        @pl.when(jnp.logical_not(here))
        def _(ts=ts):
            remote(
                wo_hbm.at[pl.ds(0, 256), pl.ds(0, 128)],
                wo.at[dp, pl.ds(ts * 256, 256)],
                wz_send.at[0],
                wz_recv.at[ts],
                {"dp": sib},
            ).wait_recv()

        @pl.when(here)
        def _():
            wz_local(0, 0).wait()

    third("qb", "o")
    ag_step(0, 1, 0)
    ag_step(0, 1, 1)
    local["fmw"].wait()
    local["fmb"].wait()
    fourth("qb")
    recv("qb", "3sa", "3sb", "3sc")
    eat("qb", qacc, wqb, (256, 512), False, 2)
    ag_step(0, 2, 0)
    ag_step(0, 2, 1)
    recv("qb", "4s")
    eat("qb", qacc, wqb, (256, 512), False, 3)
    attend(2)
    attend(3)
    ag_step(1, 0, 0)
    ag_step(1, 0, 1)
    ag_step(0, 3, 0)
    ag_step(0, 3, 1)

    def grad_move(n, src, dst, dev):
        return remote(src, dst, gr_send.at[n], gr_recv.at[n], {"dp": dev})

    student(0)
    recv("o", "1a")
    send("o", "2a", "2xa")
    recv("o", "1x")
    send("o", "2b", "2c")
    student(1)
    ag_step(1, 1, 0)
    student(2)
    ag_step(1, 1, 1)
    student(3)
    gs0[...] = gf[1 - core].astype(BF16)
    g0 = grad_move(0, gs0, gr0, sib)
    launch(g0)
    ag_step(1, 2, 0)
    recv("o", "1b")
    send("o", "2xb", "2s")
    ag_step(1, 2, 1)
    with scope("Wg0"):
        g0.wait_recv()
    gf[core] = gf[core] + gr0[...].astype(F32)
    gs1[...] = gf[core].astype(BF16)

    def chip_n(n):
        return chip_at(n % 4, n // 4)

    scatter = [
        grad_move(n, gs1.at[chip_n(n)], gr1.at[chip], chip_n(n) * 2 + core) for n in range(1, 8)
    ]
    for c in scatter:
        launch(c)
    recv("o", "1o")
    send("o", "3sa")
    ag_step(1, 3, 0)
    ag_step(1, 3, 1)
    ag_end(0)
    ag_end(1)

    def column(plane, c):
        return pl.multiple_of((2 * c + plane % 2) * 512 + (plane // 2) * 128, 128)

    def ship(n, dy, dx, d):
        dest = (t + d) % 8
        return remote(
            stage.at[n, pl.ds(pl.multiple_of(dest * 32, 32), 32)],
            hand_hbm.at[:, pl.ds(column(t, chip_at(dy, dx)), 128)],
            o_send.at[n, d],
            o_recv.at[n, d],
            {"segment": 1 - seg, "tensor": dest},
        )

    shipped = []

    def project(n, dy, dx):
        with scope("proj%d" % n):
            c = chip_at(dy, dx)

            def add(ts, acc):
                rows = pl.ds(pl.multiple_of(ts * 256, 256), 256)
                return (
                    acc
                    + mm(attb[0, ts], wo[2 * c, rows, :])
                    + mm(attb[1, ts], wo[2 * c + 1, rows, :])
                )

            acc = lax.fori_loop(0, 8, add, jnp.zeros((SEQ, 128), F32), unroll=2)
            stage[n] = (x_ref[:, pl.ds(column(t, c), 128)].astype(F32) + acc).astype(BF16)
            for d in (4, 3, 5, 2, 6, 1, 7, 0):
                c = ship(n, dy, dx, d)
                launch(c)
                shipped.append(c)

    recv("o", "1s", "2s")
    project(0, 0, 0)
    recv("o", "2a")
    send("o", "3x", "3sb")
    project(1, 1, 0)
    recv("o", "2b")
    send("o", "3y")
    project(2, -1, 0)
    recv("o", "3sa")
    project(3, 0, 1)

    with scope("Wgs"):
        for c in scatter:
            c.wait_recv()
    total = gf[core, chip]
    for n in range(1, 8):
        total = total + gr1[chip_n(n)].astype(F32)
    ga[chip] = total.astype(BF16)
    spread = [grad_move(7 + n, ga.at[chip], ga.at[chip], chip_n(n) * 2 + core) for n in range(1, 8)]
    for c in spread:
        launch(c)

    recv("o", "2c", "2xa", "2xb")
    send("o", "3sc")
    recv("o", "3sb")
    project(4, 2, 0)
    fourth("o")
    recv("o", "3sc")
    project(5, 1, 1)
    project(6, -1, 1)
    recv("o", "4s")
    project(7, 2, 1)

    with scope("Wga"):
        for c in spread:
            c.wait_recv()
    g6 = grad_move(15, ga, gall, sib)
    launch(g6)
    with scope("Wg6"):
        g6.wait_recv()
    gfin[core] = ga[...]
    gfin[1 - core] = gall[...]

    with scope("Wship"):
        for c in shipped:
            c.wait_recv()

    for p in range(4):
        for k in range(2):

            @pl.when(jnp.logical_not(is_self(p, k)))
            def _(p=p, k=k):
                wz(p, k).wait_send()

    with scope("Wsend"):
        for c in pending:
            c.wait_send()


def finish(hand_in, g_in, hand_ref, fg_ref, bg_ref):
    hand_ref[...] = hand_in[...]
    for m in range(2):
        for h in range(4):
            fg_ref[m, h, 0:64, :] = g_in[m, 2 * h, 0:64, :].astype(F32)
            fg_ref[m, h, 64:128, :] = g_in[m, 2 * h + 1, 0:64, :].astype(F32)
            bg_ref[m, h : h + 1, :] = g_in[m, 2 * h, 64:80, :].astype(F32)[0:1]


def body(segment_input, attn_gain, query_weight, kv_weight, out_weight, fm_weight, fm_bias):
    cos, sin = rope_tables()
    cos2 = jnp.asarray(np.concatenate([cos, cos], axis=1))
    sin2 = jnp.asarray(np.concatenate([-sin, sin], axis=1))
    cost, sint = jnp.asarray(cos.T.copy()), jnp.asarray(sin.T.copy())
    anywhere = pl.BlockSpec(memory_space=pl.ANY)
    vmem = pl.BlockSpec(memory_space=pltpu.VMEM)
    dma = pltpu.SemaphoreType.DMA
    hand, grads = pl.pallas_call(
        kernel,
        out_shape=(
            jax.ShapeDtypeStruct((32, D), BF16),
            jax.ShapeDtypeStruct((2, 8, 80, 128), BF16),
        ),
        in_specs=[anywhere] * 11,
        out_specs=(anywhere, vmem),
        scratch_shapes=[
            pltpu.VMEM((SEQ, D), BF16),
            pltpu.VMEM((1, D), F32),
            pltpu.VMEM((2, 4, 128, 128), F32),
            pltpu.VMEM((2, 4, 128), F32),
            pltpu.VMEM((SEQ, 128), F32),
            pltpu.VMEM((SEQ, 128), F32),
            pltpu.VMEM((64, SEQ), F32),
            pltpu.VMEM((64, SEQ), F32),
            pltpu.VMEM((16, SEQ, 512), BF16),
            pltpu.VMEM((16, 512, 128), BF16),
            pltpu.VMEM((16, 512, 256), BF16),
            pltpu.VMEM((16, 512, 256), BF16),
            pltpu.VMEM((16, 2048, 128), BF16),
            pltpu.VMEM((SEQ, 128), F32),
            pltpu.VMEM((SEQ, 512), F32),
            pltpu.VMEM((128, SEQ), BF16),
            pltpu.VMEM((8, 32, SEQ), BF16),
            pltpu.VMEM((SEQ, 128), BF16),
            pltpu.VMEM((128, SEQ), BF16),
            pltpu.VMEM((SEQ, 128), BF16),
            pltpu.VMEM((4, SEQ, 128), BF16),
            pltpu.VMEM((2, 8, SEQ, 256), BF16),
            pltpu.VMEM((8, SEQ, 128), BF16),
            pltpu.VMEM((2, 8, 80, 128), F32),
            pltpu.VMEM((8, 80, 128), BF16),
            pltpu.VMEM((8, 80, 128), BF16),
            pltpu.VMEM((8, 80, 128), BF16),
            pltpu.VMEM((8, 80, 128), BF16),
            pltpu.VMEM((8, 80, 128), BF16),
            pltpu.VMEM((8, 80, 128), BF16),
            dma((12,)),
            dma((4, N_MOVES)),
            dma((4, N_MOVES)),
            dma((8,)),
            dma((8,)),
            dma((8,)),
            dma((8,)),
            dma((2, 16)),
            dma((2, 16)),
            dma((16,)),
            dma((16,)),
            dma((8, 8)),
            dma((8, 8)),
        ],
        compiler_params=pltpu.CompilerParams(
            collective_id=0,
            has_side_effects=True,
            vmem_limit_bytes=60 * 1024 * 1024,
        ),
    )(
        segment_input[0],
        attn_gain,
        query_weight[0],
        kv_weight[0],
        out_weight[0],
        fm_weight[0],
        fm_bias[0],
        cos2,
        sin2,
        cost,
        sint,
    )
    handoff, fg, bg = pl.pallas_call(
        finish,
        out_shape=(
            jax.ShapeDtypeStruct((32, D), BF16),
            jax.ShapeDtypeStruct((2, 4, 128, 128), F32),
            jax.ShapeDtypeStruct((2, 4, 128), F32),
        ),
        in_specs=[vmem, vmem],
        out_specs=(vmem, vmem, vmem),
    )(hand, grads)
    return handoff[None], fg[None], bg[None]


def solution(mesh):
    placed = (
        P("segment", "dp", None),
        P("segment", None),
        P("segment", "dp", "tensor"),
        P("segment", "dp", "tensor"),
        P("segment", "tensor", "dp"),
        P("segment", None, "tensor", None, None),
        P("segment", None, "tensor", None),
    )
    return jax.shard_map(
        body,
        mesh=mesh,
        in_specs=placed,
        out_specs=(
            P("segment", ("dp", "tensor"), None),
            P("segment", None, "tensor", None, None),
            P("segment", None, "tensor", None),
        ),
        check_vma=False,
    )
```

```python
import jax
import jax.numpy as jnp
import numpy as np
from jax import lax
from jax.experimental import pallas as pl
from jax.experimental.pallas import tpu as pltpu
from jax.sharding import PartitionSpec as P

MESH = pl.DeviceIdType.MESH
F32 = jnp.float32
BF16 = jnp.bfloat16
D = 8192
SEQ = 256
TOKENS = 4096
EPSILON = 1e-05
ROPE_BASE = 500000.0
SCALE = 128 ** (-0.5)

STAGE_MOVES = {
    "1a": [("yp", 0, 0, 0, 2), ("ym", 0, 0, 2, 4)],
    "1b": [("yp", 0, 0, 2, 4), ("ym", 0, 0, 0, 2)],
    "1x": [("x", 0, 0, 1, 3)],
    "1o": [("x", 0, 0, 0, 1), ("x", 0, 0, 3, 4)],
    "1s": [("s", 0, 0, 0, 4)],
    "2a": [("yp", -1, 0, 0, 2), ("ym", 1, 0, 2, 4)],
    "2b": [("yp", 0, 1, 1, 2), ("ym", 0, 1, 2, 3)],
    "2c": [("yp", 0, 1, 2, 3), ("ym", 0, 1, 1, 2)],
    "2xa": [("x", -1, 0, 0, 1), ("x", 1, 0, 3, 4)],
    "2xb": [("x", -1, 0, 3, 4), ("x", 1, 0, 0, 1)],
    "2s": [("s", -1, 0, 0, 4), ("s", 1, 0, 0, 4)],
    "3y": [("yp", -1, 1, 1, 2), ("ym", 1, 1, 2, 3)],
    "3x": [("x", 2, 0, 0, 1), ("x", 2, 0, 3, 4)],
    "3sa": [("s", 0, 1, 0, 4)],
    "3sb": [("s", 2, 0, 0, 4)],
    "3sc": [("s", -1, 1, 0, 4), ("s", 1, 1, 0, 4)],
    "4s": [("s", 2, 1, 0, 4)],
}
STAGE_INDEX = {name: n for n, name in enumerate(STAGE_MOVES)}
CUTS = (0, 112, 256, 400, 512)


def rope_tables():
    half = 64
    frequency = ROPE_BASE ** (-(np.arange(half, dtype=np.float64) * (2.0 / 128)))
    angles = np.arange(SEQ, dtype=np.float64)[:, None] * frequency[None, :]
    return np.cos(angles).astype(np.float32), np.sin(angles).astype(np.float32)


def mm(a, b):
    return jnp.dot(a, b, preferred_element_type=F32)


def mm_nt(a, b):
    return lax.dot_general(a, b, (((1,), (1,)), ((), ())), preferred_element_type=F32)


def mm_tn(a, b):
    return lax.dot_general(a, b, (((0,), (0,)), ((), ())), preferred_element_type=F32)


def kernel(
    x_hbm,
    gain_hbm,
    wq_hbm,
    wkv_hbm,
    wo_hbm,
    fmw_hbm,
    fmb_hbm,
    tab_hbm,
    hand_hbm,
    gfin,
    x_ref,
    gain_ref,
    fmw_ref,
    fmb_ref,
    tab_ref,
    nrm,
    wkv,
    wqa,
    wqb,
    wo,
    kvacc,
    qacc,
    kvs,
    kvt,
    k_ref,
    kt_ref,
    v_ref,
    qrot,
    attb,
    part,
    stage,
    gf,
    gs0,
    gr0,
    gs1,
    gr1,
    ga,
    loc_sem,
    idle_sem,
    g_send,
    g_recv,
    wz_send,
    wz_recv,
    kz_send,
    kz_recv,
    ag_send,
    ag_recv,
    gr_send,
    gr_recv,
    o_send,
    o_recv,
):
    dp = lax.axis_index("dp")
    seg = lax.axis_index("segment")
    t = lax.axis_index("tensor")
    core = dp % 2
    chip = dp // 2
    xl = chip % 2
    y = chip // 2
    sib = chip * 2 + (1 - core)
    xp = (y * 2 + (1 - xl)) * 2 + core
    yp = (dp + 4) % 16
    ym = (dp + 12) % 16
    peer = {"yp": yp, "ym": ym, "x": xp, "s": sib}

    def scope(name):
        return jax.named_scope(name)

    def remote(src, dst, ssem, rsem, dev):
        return pltpu.make_async_remote_copy(
            src_ref=src,
            dst_ref=dst,
            send_sem=ssem,
            recv_sem=rsem,
            device_id=dev,
            device_id_type=MESH,
        )

    def landed(ref, sem):
        remote(ref, ref, idle_sem, sem, {"dp": sib}).wait_recv()

    def left(ref, sem):
        remote(ref, ref, sem, idle_sem, {"dp": sib}).wait_send()

    local = {}
    for n, (name, src, dst) in enumerate(
        (
            ("x", x_hbm, x_ref),
            ("gain", gain_hbm, gain_ref),
            ("kv", wkv_hbm, wkv.at[dp]),
            ("qa", wq_hbm.at[:, pl.ds(0, 256)], wqa.at[dp]),
            ("qb", wq_hbm.at[:, pl.ds(256, 256)], wqb.at[dp]),
            ("tab", tab_hbm, tab_ref),
            ("fmw", fmw_hbm, fmw_ref),
            ("fmb", fmb_hbm, fmb_ref),
        )
    ):
        local[name] = pltpu.make_async_copy(src, dst, loc_sem.at[n])
        local[name].start()

    def chip_at(dy, dx):
        return ((y + dy + 4) % 4) * 2 + (xl + dx) % 2

    def slot_of(dy, dx, c):
        return chip_at(dy, dx) * 2 + c

    barrier = pltpu.get_barrier_semaphore()
    peers = []
    for d in (4, 3, 5, 2, 6, 1, 7, 0):
        peers.append({"segment": 1 - seg, "tensor": (t + d) % 8})
    for d in (4, 3, 5, 2, 6, 1, 7):
        peers.append({"tensor": (t + d) % 8})
        peers.append({"dp": sib, "tensor": (t + d) % 8})
    for n in (6, 5, 7, 2, 4, 1, 3):
        peers.append({"dp": slot_of(n % 4, n // 4, core)})
    peers.append({"dp": sib})
    for p in peers:
        pl.semaphore_signal(barrier, inc=1, device_id=p, device_id_type=MESH)
    with scope("barrier"):
        pl.semaphore_wait(barrier, len(peers))

    kinds = {
        "kv": (0, wkv, lambda lo, hi: wkv_hbm.at[pl.ds(lo, hi - lo)], 1),
        "qa": (1, wqa, lambda lo, hi: wq_hbm.at[pl.ds(lo, hi - lo), pl.ds(0, 256)], 1),
        "qb": (2, wqb, lambda lo, hi: wq_hbm.at[pl.ds(lo, hi - lo), pl.ds(256, 256)], 1),
        "o": (3, wo, None, 4),
    }

    def move(kind, stage_name, which):
        index, buf, own, mult = kinds[kind]
        direction, dy, dx, lo, hi = STAGE_MOVES[stage_name][which]
        lo, hi = CUTS[lo] * mult, CUTS[hi] * mult
        slot = slot_of(dy, dx, core)
        dst = buf.at[slot, pl.ds(lo, hi - lo)]
        src = own(lo, hi) if (own is not None and dy == 0 and dx == 0) else dst
        recv_sem = g_recv.at[index, STAGE_INDEX[stage_name]]
        return remote(src, dst, g_send.at[index], recv_sem, {"dp": peer[direction]})

    def send(kind, *names):
        for name in names:
            for which in range(len(STAGE_MOVES[name])):
                move(kind, name, which).start()

    def recv(kind, *names):
        index, buf, _, mult = kinds[kind]
        with scope("W_%s_%s" % (kind, "_".join(names))):
            for name in names:
                rows = sum(CUTS[m[4]] - CUTS[m[3]] for m in STAGE_MOVES[name])
                ref = buf.at[pl.ds(0, 2)] if rows > 512 else buf.at[0, pl.ds(0, rows * mult)]
                landed(ref, g_recv.at[index, STAGE_INDEX[name]])

    def first(kind):
        send(kind, "1a", "1x", "1b", "1o", "1s")

    def wz(p, k):
        dst_dp = chip * 2 + k
        return remote(
            wo_hbm.at[pl.ds(k * 256, 256), pl.ds(p * 128, 128)],
            wo.at[dst_dp, pl.ds(pl.multiple_of(t * 256, 256), 256)],
            wz_send,
            wz_recv,
            {"dp": dst_dp, "tensor": 2 * p + core},
        )

    def wz_local(p, k):
        return pltpu.make_async_copy(
            wo_hbm.at[pl.ds(k * 256, 256), pl.ds(p * 128, 128)],
            wo.at[chip * 2 + k, pl.ds(pl.multiple_of(t * 256, 256), 256)],
            loc_sem.at[8],
        )

    def is_self(p, k):
        return jnp.logical_and(t == 2 * p + core, core == k)

    first("kv")
    first("qa")
    for p in range(4):
        for k in range(2):

            @pl.when(jnp.logical_not(is_self(p, k)))
            def _(p=p, k=k):
                wz(p, k).start()

            @pl.when(is_self(p, k))
            def _(p=p, k=k):
                wz_local(p, k).start()

    def norm_rows(r, carry):
        rows = pl.ds(pl.multiple_of(r * 16, 16), 16)
        total = jnp.zeros((16, 512), F32)
        for j in range(16):
            v = x_ref[rows, j * 512 : (j + 1) * 512].astype(F32)
            total = total + v * v
        inv = lax.rsqrt(jnp.sum(total, axis=-1, keepdims=True) * (1.0 / D) + EPSILON)
        for j in range(16):
            v = x_ref[rows, j * 512 : (j + 1) * 512].astype(F32)
            nrm[j, rows, :] = (v * inv * gain_ref[:, j * 512 : (j + 1) * 512]).astype(BF16)
        return carry

    local["x"].wait()
    local["gain"].wait()
    with scope("norm1"):
        lax.fori_loop(0, 8, norm_rows, 0)
    recv("kv", "1a")
    send("kv", "2a", "2xa")
    recv("kv", "1x")
    send("kv", "2b", "2c")
    with scope("norm2"):
        lax.fori_loop(8, 16, norm_rows, 0)
    recv("kv", "1b")
    send("kv", "2xb", "2s")
    recv("qa", "1a")
    send("qa", "2a", "2xa")
    recv("qa", "1x")
    send("qa", "2b")

    def eat(name, acc, buf, cols, start, wave):
        def add(i, carry):
            c = jnp.where(i % 2 == 0, core, 1 - core)
            n = i // 2
            if wave == 1:
                dy, dx = n + 3, 0
            elif wave == 2:
                dy, dx = n + 3, 1 - n // 3
            else:
                dy, dx = n + 2, 1
            slot = slot_of(dy, dx, c)
            acc[:, cols[0] : cols[1]] += mm(nrm[slot], buf[slot])
            return carry

        with scope("eat_%s%d" % (name, wave)):
            if start:
                acc[:, cols[0] : cols[1]] = jnp.zeros((SEQ, cols[1] - cols[0]), F32)
            lax.fori_loop(0, {1: 6, 2: 8, 3: 2}[wave], add, 0)

    def fourth(kind):
        recv(kind, "3y", "3x")
        send(kind, "4s")

    def done2(kind):
        recv(kind, "2c", "2xa", "2xb", "1o")
        send(kind, "3sb", "3sa", "3sc")

    recv("kv", "2a")
    send("kv", "3x")
    recv("kv", "2b")
    send("kv", "3y")
    send("qa", "2c")
    recv("qa", "1b")
    send("qa", "2xb", "2s")
    send("qb", "1a", "1x")
    done2("kv")
    local["kv"].wait()
    recv("kv", "1s", "2s")
    eat("kv", kvacc, wkv, (0, 128), True, 1)
    fourth("kv")
    recv("kv", "3sa", "3sb", "3sc")
    eat("kv", kvacc, wkv, (0, 128), False, 2)
    recv("qa", "2a")
    send("qa", "3x")
    recv("qa", "2b")
    send("qa", "3y")
    send("qb", "1b", "1o", "1s")
    recv("kv", "4s")
    eat("kv", kvacc, wkv, (0, 128), False, 3)

    r_i = lax.broadcasted_iota(jnp.int32, (128, 128), 0)
    c_i = lax.broadcasted_iota(jnp.int32, (128, 128), 1)
    pick = (c_i == (r_i & 31) * 4 + (r_i >> 5)).astype(BF16)
    kvs[...] = mm_nt(pick, kvacc[...].astype(BF16)).astype(BF16)

    def kz(d):
        dest = (t + d) % 8
        return remote(
            kvs.at[pl.ds(pl.multiple_of((dest // 2) * 32, 32), 32)],
            kvt.at[t],
            kz_send,
            kz_recv,
            {"tensor": dest},
        )

    for d in range(1, 8):
        kz(d).start()
    kvt[t] = kvs[pl.ds(pl.multiple_of((t // 2) * 32, 32), 32), :]

    done2("qa")
    recv("qb", "1a")
    send("qb", "2a", "2xa")
    recv("qb", "1x")
    send("qb", "2b", "2c")
    local["qa"].wait()
    recv("qa", "1s", "2s")
    eat("qa", qacc, wqa, (0, 256), True, 1)
    fourth("qa")
    recv("qb", "1b")
    send("qb", "2xb", "2s")

    own_column = core == t % 2

    with scope("Wwz"):

        @pl.when(own_column)
        def _():
            wz_local(0, 0).wait()
            landed(wo.at[0, pl.ds(0, 7 * 256)], wz_recv)

        @pl.when(jnp.logical_not(own_column))
        def _():
            landed(wo.at[0], wz_recv)

    send("o", "1a", "1x")
    recv("qa", "3sa", "3sb", "3sc")
    eat("qa", qacc, wqa, (0, 256), False, 2)

    local["tab"].wait()
    with scope("Wkz"):
        landed(kvt.at[pl.ds(0, 7)], kz_recv)
    kall = kvt[0:4].reshape(128, SEQ).astype(F32)
    k1, k2 = kall[0:64], kall[64:128]
    ct, st = tab_ref[0].T[0:64], tab_ref[1].T[64:128]
    krot = jnp.concatenate([k1 * ct - k2 * st, k2 * ct + k1 * st], axis=0)
    kt_ref[...] = krot.astype(BF16)
    k_ref[...] = krot.T.astype(BF16)
    v_ref[...] = kvt[4:8].reshape(128, SEQ).astype(F32).T.astype(BF16)

    recv("qa", "4s")
    eat("qa", qacc, wqa, (0, 256), False, 3)
    recv("qb", "2a")
    send("qb", "3x")

    row_i = lax.broadcasted_iota(jnp.int32, (SEQ, SEQ), 0)
    col_i = lax.broadcasted_iota(jnp.int32, (SEQ, SEQ), 1)
    mask = row_i >= col_i

    def attend(h):
        with scope("attend%d" % h):
            q = qacc[:, h * 128 : (h + 1) * 128]
            q = (q * tab_ref[0] + pltpu.roll(q, 64, 1) * tab_ref[1]).astype(BF16)
            qrot[h] = q
            scores = mm(q, kt_ref[...]) * SCALE
            scores = jnp.where(mask, scores, -jnp.inf)
            lifted = jnp.exp(scores - jnp.max(scores, axis=-1, keepdims=True))
            prob = (lifted / jnp.sum(lifted, axis=-1, keepdims=True)).astype(BF16)
            c0 = (h % 2) * 128
            cols = pl.ds(pl.multiple_of(t * 256 + c0, 128), 128)
            attb[h // 2, :, cols] = mm(prob, v_ref[...]).astype(BF16)

    def ag(k, s, up, half):
        slot = (t + 8 - s) % 8 if up else (t + s) % 8
        ref = attb.at[k, pl.ds(half * 128, 128), pl.ds(pl.multiple_of(slot * 256, 256), 256)]
        dest = (t + 1) % 8 if up else (t + 7) % 8
        return remote(ref, ref, ag_send.at[k], ag_recv.at[k, 2 * s + half], {"tensor": dest})

    def ag_step(k, s, half):
        if s > 0:
            with scope("Wag%d_%d_%d" % (k, s, half)):
                landed(attb.at[k, :, pl.ds(0, 256)], ag_recv.at[k, 2 * s - 2 + half])
        if s < 3 or half == 0:
            ag(k, s, True, half).start()
        if s < 3 or half == 1:
            ag(k, s, False, half).start()

    def ag_end(k):
        with scope("Wag%d_end" % k):
            for half in range(2):
                landed(attb.at[k, pl.ds(0, 128), pl.ds(0, 256)], ag_recv.at[k, 6 + half])

    lead = (lax.broadcasted_iota(jnp.int32, (16, 128), 0) == 0).astype(F32)

    def feature(z):
        e = jnp.exp(jnp.minimum(z, 0.0))
        pos = z > 0
        return jnp.where(pos, z + 1.0, e).astype(BF16), jnp.where(pos, 1.0, e)

    def pre(a, m, h):
        w = fmw_ref[m, h]
        hi = w.astype(BF16)
        low = (w - hi.astype(F32)).astype(BF16)
        return mm(a, hi) + mm(a, low) + fmb_ref[m, pl.ds(h, 1), :]

    def put(m, h, weight, bias):
        gf[m, 2 * h, 0:64, :] = weight[0:64]
        gf[m, 2 * h + 1, 0:64, :] = weight[64:128]
        gf[m, 2 * h, 64:80, :] = bias * lead
        gf[m, 2 * h + 1, 64:80, :] = jnp.zeros((16, 128), F32)

    def student(h):
        with scope("student%d" % h):
            q, k, v = qrot[h], k_ref[...], v_ref[...]
            cols = pl.ds(pl.multiple_of(t * 256 + (h % 2) * 128, 128), 128)
            att = attb[h // 2, :, cols].astype(F32)
            qf, qd = feature(pre(q, 0, h))
            kf, kd = feature(pre(k, 1, h))
            aff = jnp.where(mask, mm_nt(qf, kf), 0.0)
            den = jnp.sum(aff, axis=-1, keepdims=True)
            out = mm(aff.astype(BF16), v) / den
            dnum = ((out - att) * (2.0 / TOKENS) / den).astype(BF16)
            dden = jnp.sum(dnum.astype(F32) * out, axis=-1, keepdims=True)
            daff = jnp.where(mask, mm_nt(dnum, v) - dden, 0.0).astype(BF16)
            dzq = mm(daff, kf) * qd
            dzk = mm_tn(daff, qf) * kd
            put(0, h, mm_tn(q, dzq.astype(BF16)), jnp.sum(dzq, axis=0, keepdims=True))
            put(1, h, mm_tn(k, dzk.astype(BF16)), jnp.sum(dzk, axis=0, keepdims=True))

    attend(0)
    attend(1)
    ag_step(0, 0, 0)
    ag_step(0, 0, 1)
    recv("qb", "2b")
    send("qb", "3y")
    send("o", "1b", "1o", "1s")

    def column(plane, c):
        return pl.multiple_of((2 * c + plane % 2) * 512 + (plane // 2) * 128, 128)

    def ship(n, dy, dx, d):
        dest = (t + d) % 8
        return remote(
            stage.at[n, pl.ds(pl.multiple_of(dest * 32, 32), 32)],
            hand_hbm.at[:, pl.ds(column(t, chip_at(dy, dx)), 128)],
            o_send,
            o_recv,
            {"segment": 1 - seg, "tensor": dest},
        )

    def early(n, dy, dx):
        with scope("early%d" % n):
            c = chip_at(dy, dx)
            part[n] = x_ref[:, pl.ds(column(t, c), 128)].astype(F32) + mm(attb[0], wo[2 * c])

    def late(n, dy, dx):
        with scope("late%d" % n):
            c = chip_at(dy, dx)
            stage[n] = (part[n] + mm(attb[1], wo[2 * c + 1])).astype(BF16)
            for d in (4, 3, 5, 2, 6, 1, 7, 0):
                ship(n, dy, dx, d).start()

    def grad_move(n, src, dst, dev):
        return remote(src, dst, gr_send.at[n], gr_recv.at[n], {"dp": dev})

    def chip_n(n):
        return chip_at(n % 4, n // 4)

    done2("qb")
    local["qb"].wait()
    recv("qb", "1s", "2s")
    eat("qb", qacc, wqb, (256, 512), True, 1)
    ag_step(0, 1, 0)
    ag_step(0, 1, 1)
    fourth("qb")
    local["fmw"].wait()
    local["fmb"].wait()
    recv("o", "1a")
    send("o", "2a", "2xa")
    recv("o", "1x")
    send("o", "2b", "2c")
    recv("qb", "3sa", "3sb", "3sc")
    eat("qb", qacc, wqb, (256, 512), False, 2)
    ag_step(0, 2, 0)
    ag_step(0, 2, 1)
    recv("qb", "4s")
    eat("qb", qacc, wqb, (256, 512), False, 3)
    attend(2)
    attend(3)
    ag_step(1, 0, 0)
    ag_step(1, 0, 1)
    student(0)
    ag_step(0, 3, 0)
    ag_step(0, 3, 1)
    recv("o", "1b")
    send("o", "2xb", "2s")
    student(1)
    ag_step(1, 1, 0)
    student(2)
    ag_step(1, 1, 1)
    recv("o", "1o")
    send("o", "3sa")
    student(3)
    gs0[...] = gf[1 - core].astype(BF16)
    g0 = grad_move(0, gs0, gr0, sib)
    g0.start()
    ag_step(1, 2, 0)
    recv("o", "2a")
    send("o", "3x", "3sb")
    ag_step(1, 2, 1)
    ag_end(0)
    recv("o", "1s", "2s")
    early(0, 0, 0)
    early(1, 1, 0)
    ag_step(1, 3, 0)
    early(2, -1, 0)
    ag_step(1, 3, 1)
    recv("o", "2b")
    send("o", "3y")
    with scope("Wg0"):
        g0.wait_recv()
    gf[core] = gf[core] + gr0[...].astype(F32)
    gs1[...] = gf[core].astype(BF16)
    for n in range(1, 8):
        grad_move(1, gs1.at[chip_n(n)], gr1.at[n - 1], chip_n(n) * 2 + core).start()
    recv("o", "3sa")
    early(3, 0, 1)
    ag_end(1)
    late(0, 0, 0)
    late(1, 1, 0)
    late(2, -1, 0)
    late(3, 0, 1)
    recv("o", "2c", "2xa", "2xb")
    send("o", "3sc")
    recv("o", "3sb")
    early(4, 2, 0)
    late(4, 2, 0)
    fourth("o")
    recv("o", "3sc")
    early(5, 1, 1)
    late(5, 1, 1)
    early(6, -1, 1)
    late(6, -1, 1)
    recv("o", "4s")
    early(7, 2, 1)
    late(7, 2, 1)

    with scope("Wgs"):
        landed(gr1, gr_recv.at[1])
    total = gf[core, chip]
    for n in range(1, 8):
        total = total + gr1[n - 1].astype(F32)
    ga[chip] = total.astype(BF16)
    for n in range(1, 8):
        grad_move(2, ga.at[chip], ga.at[chip], chip_n(n) * 2 + core).start()

    with scope("Wga"):
        landed(ga.at[pl.ds(0, 7)], gr_recv.at[2])
    g6 = grad_move(3, ga, gfin.at[core], sib)
    g6.start()
    keep = pltpu.make_async_copy(ga, gfin.at[core], loc_sem.at[8])
    keep.start()
    with scope("Wg6"):
        landed(ga, gr_recv.at[3])
    with scope("Wship"):
        landed(stage, o_recv)

    with scope("Wsend"):

        @pl.when(own_column)
        def _():
            left(wo.at[0, pl.ds(0, 7 * 256)], wz_send)

        @pl.when(jnp.logical_not(own_column))
        def _():
            left(wo.at[0], wz_send)

        for index, buf, _, _ in kinds.values():
            left(buf.at[pl.ds(0, 15)], g_send.at[index])
        left(kvt.at[pl.ds(0, 7)], kz_send)
        for k in range(2):
            left(attb.at[k, :, pl.ds(0, 7 * 256)], ag_send.at[k])
        for n, ref in enumerate((gs0, gs1.at[pl.ds(0, 7)], gs1.at[pl.ds(0, 7)], ga)):
            left(ref, gr_send.at[n])
        left(stage, o_send)
        keep.wait()


def finish(hand_in, g_in, hand_ref, fg_ref, bg_ref):
    hand_ref[...] = hand_in[...]
    for m in range(2):
        for h in range(4):
            fg_ref[m, h, 0:64, :] = g_in[m, 2 * h, 0:64, :].astype(F32)
            fg_ref[m, h, 64:128, :] = g_in[m, 2 * h + 1, 0:64, :].astype(F32)
            bg_ref[m, h : h + 1, :] = g_in[m, 2 * h, 64:80, :].astype(F32)[0:1]


def body(segment_input, attn_gain, query_weight, kv_weight, out_weight, fm_weight, fm_bias):
    cos, sin = rope_tables()
    cos2, sin2 = np.concatenate([cos, cos], axis=1), np.concatenate([-sin, sin], axis=1)
    tables = jnp.asarray(np.stack([cos2, sin2]))
    anywhere = pl.BlockSpec(memory_space=pl.ANY)
    vmem = pl.BlockSpec(memory_space=pltpu.VMEM)
    dma = pltpu.SemaphoreType.DMA
    hand, grads = pl.pallas_call(
        kernel,
        out_shape=(
            jax.ShapeDtypeStruct((32, D), BF16),
            jax.ShapeDtypeStruct((2, 8, 80, 128), BF16),
        ),
        in_specs=[anywhere] * 8,
        out_specs=(anywhere, anywhere),
        scratch_shapes=[
            pltpu.VMEM((SEQ, D), BF16),
            pltpu.VMEM((1, D), F32),
            pltpu.VMEM((2, 4, 128, 128), F32),
            pltpu.VMEM((2, 4, 128), F32),
            pltpu.VMEM((2, SEQ, 128), F32),
            pltpu.VMEM((16, SEQ, 512), BF16),
            pltpu.VMEM((16, 512, 128), BF16),
            pltpu.VMEM((16, 512, 256), BF16),
            pltpu.VMEM((16, 512, 256), BF16),
            pltpu.VMEM((16, 2048, 128), BF16),
            pltpu.VMEM((SEQ, 128), F32),
            pltpu.VMEM((SEQ, 512), F32),
            pltpu.VMEM((128, SEQ), BF16),
            pltpu.VMEM((8, 32, SEQ), BF16),
            pltpu.VMEM((SEQ, 128), BF16),
            pltpu.VMEM((128, SEQ), BF16),
            pltpu.VMEM((SEQ, 128), BF16),
            pltpu.VMEM((4, SEQ, 128), BF16),
            pltpu.VMEM((2, SEQ, 2048), BF16),
            pltpu.VMEM((8, SEQ, 128), F32),
            pltpu.VMEM((8, SEQ, 128), BF16),
            pltpu.VMEM((2, 8, 80, 128), F32),
            pltpu.VMEM((8, 80, 128), BF16),
            pltpu.VMEM((8, 80, 128), BF16),
            pltpu.VMEM((8, 80, 128), BF16),
            pltpu.VMEM((7, 80, 128), BF16),
            pltpu.VMEM((8, 80, 128), BF16),
            dma((9,)),
            dma(()),
            dma((4,)),
            dma((4, len(STAGE_MOVES))),
            dma(()),
            dma(()),
            dma(()),
            dma(()),
            dma((2,)),
            dma((2, 8)),
            dma((4,)),
            dma((4,)),
            dma(()),
            dma(()),
        ],
        compiler_params=pltpu.CompilerParams(
            collective_id=0,
            has_side_effects=True,
            vmem_limit_bytes=60 * 1024 * 1024,
        ),
    )(
        segment_input[0],
        attn_gain,
        query_weight[0],
        kv_weight[0],
        out_weight[0],
        fm_weight[0],
        fm_bias[0],
        tables,
    )
    handoff, fg, bg = pl.pallas_call(
        finish,
        out_shape=(
            jax.ShapeDtypeStruct((32, D), BF16),
            jax.ShapeDtypeStruct((2, 4, 128, 128), F32),
            jax.ShapeDtypeStruct((2, 4, 128), F32),
        ),
        in_specs=[vmem, vmem],
        out_specs=(vmem, vmem, vmem),
    )(hand, grads)
    return handoff[None], fg[None], bg[None]


def solution(mesh):
    placed = (
        P("segment", "dp", None),
        P("segment", None),
        P("segment", "dp", "tensor"),
        P("segment", "dp", "tensor"),
        P("segment", "tensor", "dp"),
        P("segment", None, "tensor", None, None),
        P("segment", None, "tensor", None),
    )
    return jax.shard_map(
        body,
        mesh=mesh,
        in_specs=placed,
        out_specs=(
            P("segment", ("dp", "tensor"), None),
            P("segment", None, "tensor", None, None),
            P("segment", None, "tensor", None),
        ),
        check_vma=False,
    )
```

```python
import jax
import jax.numpy as jnp
import numpy as np
from jax import lax
from jax.experimental import pallas as pl
from jax.experimental.pallas import tpu as pltpu
from jax.sharding import PartitionSpec as P

MESH = pl.DeviceIdType.MESH
F32 = jnp.float32
BF16 = jnp.bfloat16
D = 8192
SEQ = 256
TOKENS = 4096
EPSILON = 1e-05
ROPE_BASE = 500000.0
SCALE = 128 ** (-0.5)

STAGE_MOVES = {
    "1a": [("yp", 0, 0, 0, 2), ("ym", 0, 0, 2, 4)],
    "1b": [("yp", 0, 0, 2, 4), ("ym", 0, 0, 0, 2)],
    "1x": [("x", 0, 0, 1, 3)],
    "1o": [("x", 0, 0, 0, 1), ("x", 0, 0, 3, 4)],
    "1s": [("s", 0, 0, 0, 4)],
    "2a": [("yp", -1, 0, 0, 2), ("ym", 1, 0, 2, 4)],
    "2b": [("yp", 0, 1, 1, 2), ("ym", 0, 1, 2, 3)],
    "2c": [("yp", 0, 1, 2, 3), ("ym", 0, 1, 1, 2)],
    "2xa": [("x", -1, 0, 0, 1), ("x", 1, 0, 3, 4)],
    "2xb": [("x", -1, 0, 3, 4), ("x", 1, 0, 0, 1)],
    "2s": [("s", -1, 0, 0, 4), ("s", 1, 0, 0, 4)],
    "3y": [("yp", -1, 1, 1, 2), ("ym", 1, 1, 2, 3)],
    "3x": [("x", 2, 0, 0, 1), ("x", 2, 0, 3, 4)],
    "3sa": [("s", 0, 1, 0, 4)],
    "3sb": [("s", 2, 0, 0, 4)],
    "3sc": [("s", -1, 1, 0, 4), ("s", 1, 1, 0, 4)],
    "4s": [("s", 2, 1, 0, 4)],
}
STAGE_INDEX = {name: n for n, name in enumerate(STAGE_MOVES)}
CUTS = (0, 112, 256, 400, 512)
CUTS_OUT = (0, 288, 1024, 1760, 2048)


def rope_tables():
    half = 64
    frequency = ROPE_BASE ** (-(np.arange(half, dtype=np.float64) * (2.0 / 128)))
    angles = np.arange(SEQ, dtype=np.float64)[:, None] * frequency[None, :]
    return np.cos(angles).astype(np.float32), np.sin(angles).astype(np.float32)


def mm(a, b):
    return jnp.dot(a, b, preferred_element_type=F32)


def mm_nt(a, b):
    return lax.dot_general(a, b, (((1,), (1,)), ((), ())), preferred_element_type=F32)


def mm_tn(a, b):
    return lax.dot_general(a, b, (((0,), (0,)), ((), ())), preferred_element_type=F32)


def kernel(
    x_hbm,
    gain_hbm,
    wq_hbm,
    wkv_hbm,
    wo_hbm,
    fmw_hbm,
    fmb_hbm,
    tab_hbm,
    hand_hbm,
    gfin,
    x_ref,
    gain_ref,
    fmw_ref,
    fmb_ref,
    tab_ref,
    nrm,
    wkv,
    wqa,
    wqb,
    wo,
    kvacc,
    qacc,
    kvs,
    kvt,
    k_ref,
    kt_ref,
    v_ref,
    qrot,
    attb,
    part,
    stage,
    gf,
    gs0,
    gr0,
    gs1,
    gr1,
    ga,
    loc_sem,
    idle_sem,
    g_send,
    g_recv,
    wz_send,
    wz_recv,
    kz_send,
    kz_recv,
    ag_send,
    ag_recv,
    gr_send,
    gr_recv,
    o_send,
    o_recv,
):
    dp = lax.axis_index("dp")
    seg = lax.axis_index("segment")
    t = lax.axis_index("tensor")
    core = dp % 2
    chip = dp // 2
    xl = chip % 2
    y = chip // 2
    sib = chip * 2 + (1 - core)
    xp = (y * 2 + (1 - xl)) * 2 + core
    yp = (dp + 4) % 16
    ym = (dp + 12) % 16
    peer = {"yp": yp, "ym": ym, "x": xp, "s": sib}

    def scope(name):
        return jax.named_scope(name)

    def remote(src, dst, ssem, rsem, dev):
        return pltpu.make_async_remote_copy(
            src_ref=src,
            dst_ref=dst,
            send_sem=ssem,
            recv_sem=rsem,
            device_id=dev,
            device_id_type=MESH,
        )

    def landed(ref, sem):
        remote(ref, ref, idle_sem, sem, {"dp": sib}).wait_recv()

    def left(ref, sem):
        remote(ref, ref, sem, idle_sem, {"dp": sib}).wait_send()

    local = {}
    for n, (name, src, dst) in enumerate(
        (
            ("x", x_hbm, x_ref),
            ("gain", gain_hbm, gain_ref),
            ("kv", wkv_hbm, wkv.at[dp]),
            ("qa", wq_hbm.at[:, pl.ds(0, 256)], wqa.at[dp]),
            ("qb", wq_hbm.at[:, pl.ds(256, 256)], wqb.at[dp]),
            ("tab", tab_hbm, tab_ref),
            ("fmw", fmw_hbm, fmw_ref),
            ("fmb", fmb_hbm, fmb_ref),
        )
    ):
        local[name] = pltpu.make_async_copy(src, dst, loc_sem.at[n])
        local[name].start()

    def chip_at(dy, dx):
        return ((y + dy + 4) % 4) * 2 + (xl + dx) % 2

    def slot_of(dy, dx, c):
        return chip_at(dy, dx) * 2 + c

    barrier = pltpu.get_barrier_semaphore()
    peers = []
    for d in (4, 3, 5, 2, 6, 1, 7, 0):
        peers.append({"segment": 1 - seg, "tensor": (t + d) % 8})
    for d in (4, 3, 5, 2, 6, 1, 7):
        peers.append({"tensor": (t + d) % 8})
        peers.append({"dp": sib, "tensor": (t + d) % 8})
    for n in (6, 5, 7, 2, 4, 1, 3):
        peers.append({"dp": slot_of(n % 4, n // 4, core)})
    peers.append({"dp": sib})
    for p in peers:
        pl.semaphore_signal(barrier, inc=1, device_id=p, device_id_type=MESH)
    with scope("barrier"):
        pl.semaphore_wait(barrier, len(peers))

    kinds = {
        "kv": (0, wkv, lambda lo, hi: wkv_hbm.at[pl.ds(lo, hi - lo)], CUTS),
        "qa": (1, wqa, lambda lo, hi: wq_hbm.at[pl.ds(lo, hi - lo), pl.ds(0, 256)], CUTS),
        "qb": (2, wqb, lambda lo, hi: wq_hbm.at[pl.ds(lo, hi - lo), pl.ds(256, 256)], CUTS),
        "o": (3, wo, None, CUTS_OUT),
    }

    def move(kind, stage_name, which):
        index, buf, own, cuts = kinds[kind]
        direction, dy, dx, lo, hi = STAGE_MOVES[stage_name][which]
        lo, hi = cuts[lo], cuts[hi]
        slot = slot_of(dy, dx, core)
        dst = buf.at[slot, pl.ds(lo, hi - lo)]
        src = own(lo, hi) if (own is not None and dy == 0 and dx == 0) else dst
        recv_sem = g_recv.at[index, STAGE_INDEX[stage_name]]
        return remote(src, dst, g_send.at[index], recv_sem, {"dp": peer[direction]})

    def send(kind, *names):
        for name in names:
            for which in range(len(STAGE_MOVES[name])):
                move(kind, name, which).start()

    def recv(kind, *names):
        index, buf, _, cuts = kinds[kind]
        with scope("W_%s_%s" % (kind, "_".join(names))):
            for name in names:
                rows = sum(cuts[m[4]] - cuts[m[3]] for m in STAGE_MOVES[name])
                ref = buf.at[pl.ds(0, 2)] if rows > cuts[4] else buf.at[0, pl.ds(0, rows)]
                landed(ref, g_recv.at[index, STAGE_INDEX[name]])

    def first(kind):
        send(kind, "1a", "1x", "1b", "1o", "1s")

    def wz(p, k):
        dst_dp = chip * 2 + k
        return remote(
            wo_hbm.at[pl.ds(k * 256, 256), pl.ds(p * 128, 128)],
            wo.at[dst_dp, pl.ds(pl.multiple_of(t * 256, 256), 256)],
            wz_send,
            wz_recv,
            {"dp": dst_dp, "tensor": 2 * p + core},
        )

    def wz_local(p, k):
        return pltpu.make_async_copy(
            wo_hbm.at[pl.ds(k * 256, 256), pl.ds(p * 128, 128)],
            wo.at[chip * 2 + k, pl.ds(pl.multiple_of(t * 256, 256), 256)],
            loc_sem.at[8],
        )

    def is_self(p, k):
        return jnp.logical_and(t == 2 * p + core, core == k)

    first("kv")
    first("qa")
    for p in range(4):
        for k in range(2):

            @pl.when(jnp.logical_not(is_self(p, k)))
            def _(p=p, k=k):
                wz(p, k).start()

            @pl.when(is_self(p, k))
            def _(p=p, k=k):
                wz_local(p, k).start()

    def norm_rows(r, carry):
        rows = pl.ds(pl.multiple_of(r * 16, 16), 16)
        total = jnp.zeros((16, 512), F32)
        for j in range(16):
            v = x_ref[rows, j * 512 : (j + 1) * 512].astype(F32)
            total = total + v * v
        inv = lax.rsqrt(jnp.sum(total, axis=-1, keepdims=True) * (1.0 / D) + EPSILON)
        for j in range(16):
            v = x_ref[rows, j * 512 : (j + 1) * 512].astype(F32)
            nrm[j, rows, :] = (v * inv * gain_ref[:, j * 512 : (j + 1) * 512]).astype(BF16)
        return carry

    local["x"].wait()
    local["gain"].wait()
    with scope("norm1"):
        lax.fori_loop(0, 8, norm_rows, 0)
    recv("kv", "1a")
    send("kv", "2a", "2xa")
    recv("kv", "1x")
    send("kv", "2b", "2c")
    with scope("norm2"):
        lax.fori_loop(8, 16, norm_rows, 0)
    recv("kv", "1b")
    send("kv", "2xb", "2s")
    recv("qa", "1a")
    send("qa", "2a", "2xa")
    recv("qa", "1x")
    send("qa", "2b")

    def eat(name, acc, buf, cols, start, wave):
        def add(n, carry):
            if wave == 1:
                dy, dx = n + 3, 0
            elif wave == 2:
                dy, dx = n + 3, 1 - n // 3
            else:
                dy, dx = n + 2, 1
            slot = slot_of(dy, dx, 0)
            acc[:, cols[0] : cols[1]] += mm(nrm[slot], buf[slot]) + mm(nrm[slot + 1], buf[slot + 1])
            return carry

        with scope("eat_%s%d" % (name, wave)):
            if start:
                acc[:, cols[0] : cols[1]] = jnp.zeros((SEQ, cols[1] - cols[0]), F32)
            lax.fori_loop(0, {1: 3, 2: 4, 3: 1}[wave], add, 0)

    def fourth(kind):
        recv(kind, "3y", "3x")
        send(kind, "4s")

    def done2(kind):
        recv(kind, "2c", "2xa", "2xb", "1o")
        send(kind, "3sb", "3sa", "3sc")

    recv("kv", "2a")
    send("kv", "3x")
    recv("kv", "2b")
    send("kv", "3y")
    send("qa", "2c")
    recv("qa", "1b")
    send("qa", "2xb", "2s")
    send("qb", "1a", "1x")
    done2("kv")
    local["kv"].wait()
    recv("kv", "1s", "2s")
    eat("kv", kvacc, wkv, (0, 128), True, 1)
    recv("qa", "2a")
    send("qa", "3x")
    recv("qa", "2b")
    send("qa", "3y")
    fourth("kv")
    recv("kv", "3sa", "3sb", "3sc")
    eat("kv", kvacc, wkv, (0, 128), False, 2)
    done2("qa")
    send("qb", "1b", "1o", "1s")
    recv("kv", "4s")
    eat("kv", kvacc, wkv, (0, 128), False, 3)

    r_i = lax.broadcasted_iota(jnp.int32, (128, 128), 0)
    c_i = lax.broadcasted_iota(jnp.int32, (128, 128), 1)
    pick = (c_i == (r_i & 31) * 4 + (r_i >> 5)).astype(BF16)
    kvs[...] = mm_nt(pick, kvacc[...].astype(BF16)).astype(BF16)

    def kz(d):
        dest = (t + d) % 8
        return remote(
            kvs.at[pl.ds(pl.multiple_of((dest // 2) * 32, 32), 32)],
            kvt.at[t],
            kz_send,
            kz_recv,
            {"tensor": dest},
        )

    for d in range(1, 8):
        kz(d).start()
    kvt[t] = kvs[pl.ds(pl.multiple_of((t // 2) * 32, 32), 32), :]

    recv("qb", "1a")
    send("qb", "2a", "2xa")
    recv("qb", "1x")
    send("qb", "2b", "2c")
    local["qa"].wait()
    recv("qa", "1s", "2s")
    eat("qa", qacc, wqa, (0, 256), True, 1)
    fourth("qa")
    recv("qa", "3sa", "3sb", "3sc")
    eat("qa", qacc, wqa, (0, 256), False, 2)
    recv("qb", "1b")
    send("qb", "2xb", "2s")

    local["tab"].wait()
    with scope("Wkz"):
        landed(kvt.at[pl.ds(0, 7)], kz_recv)
    kall = kvt[0:4].reshape(128, SEQ).astype(F32)
    k1, k2 = kall[0:64], kall[64:128]
    ct, st = tab_ref[0].T[0:64], tab_ref[1].T[64:128]
    krot = jnp.concatenate([k1 * ct - k2 * st, k2 * ct + k1 * st], axis=0)
    kt_ref[...] = krot.astype(BF16)
    k_ref[...] = krot.T.astype(BF16)
    v_ref[...] = kvt[4:8].reshape(128, SEQ).astype(F32).T.astype(BF16)

    recv("qa", "4s")
    eat("qa", qacc, wqa, (0, 256), False, 3)

    row_i = lax.broadcasted_iota(jnp.int32, (SEQ, SEQ), 0)
    col_i = lax.broadcasted_iota(jnp.int32, (SEQ, SEQ), 1)
    mask = row_i >= col_i

    def attend(h):
        with scope("attend%d" % h):
            q = qacc[:, h * 128 : (h + 1) * 128]
            q = (q * tab_ref[0] + pltpu.roll(q, 64, 1) * tab_ref[1]).astype(BF16)
            qrot[h] = q
            scores = mm(q, kt_ref[...]) * SCALE
            scores = jnp.where(mask, scores, -jnp.inf)
            lifted = jnp.exp(scores - jnp.max(scores, axis=-1, keepdims=True))
            prob = (lifted / jnp.sum(lifted, axis=-1, keepdims=True)).astype(BF16)
            c0 = (h % 2) * 128
            cols = pl.ds(pl.multiple_of(t * 256 + c0, 128), 128)
            attb[h // 2, :, cols] = mm(prob, v_ref[...]).astype(BF16)

    def ag(k, s, up, half):
        slot = (t + 8 - s) % 8 if up else (t + s) % 8
        ref = attb.at[k, pl.ds(half * 128, 128), pl.ds(pl.multiple_of(slot * 256, 256), 256)]
        dest = (t + 1) % 8 if up else (t + 7) % 8
        return remote(ref, ref, ag_send.at[k], ag_recv.at[k, 2 * s + half], {"tensor": dest})

    def ag_step(k, s, half):
        if s > 0:
            with scope("Wag%d_%d_%d" % (k, s, half)):
                landed(attb.at[k, :, pl.ds(0, 256)], ag_recv.at[k, 2 * s - 2 + half])
        if s < 3 or half == 0:
            ag(k, s, True, half).start()
        if s < 3 or half == 1:
            ag(k, s, False, half).start()

    def ag_end(k):
        with scope("Wag%d_end" % k):
            for half in range(2):
                landed(attb.at[k, pl.ds(0, 128), pl.ds(0, 256)], ag_recv.at[k, 6 + half])

    lead = (lax.broadcasted_iota(jnp.int32, (16, 128), 0) == 0).astype(F32)

    def feature(z):
        e = jnp.exp(jnp.minimum(z, 0.0))
        pos = z > 0
        return jnp.where(pos, z + 1.0, e).astype(BF16), jnp.where(pos, 1.0, e)

    def pre(a, m, h):
        w = fmw_ref[m, h]
        hi = w.astype(BF16)
        low = (w - hi.astype(F32)).astype(BF16)
        return mm(a, hi) + mm(a, low) + fmb_ref[m, pl.ds(h, 1), :]

    def put(m, h, weight, bias):
        gf[m, 2 * h, 0:64, :] = weight[0:64]
        gf[m, 2 * h + 1, 0:64, :] = weight[64:128]
        gf[m, 2 * h, 64:80, :] = bias * lead
        gf[m, 2 * h + 1, 64:80, :] = jnp.zeros((16, 128), F32)

    def student(h):
        with scope("student%d" % h):
            q, k, v = qrot[h], k_ref[...], v_ref[...]
            cols = pl.ds(pl.multiple_of(t * 256 + (h % 2) * 128, 128), 128)
            att = attb[h // 2, :, cols].astype(F32)
            qf, qd = feature(pre(q, 0, h))
            kf, kd = feature(pre(k, 1, h))
            aff = jnp.where(mask, mm_nt(qf, kf), 0.0)
            den = jnp.sum(aff, axis=-1, keepdims=True)
            out = mm(aff.astype(BF16), v) / den
            dnum = ((out - att) * (2.0 / TOKENS) / den).astype(BF16)
            dden = jnp.sum(dnum.astype(F32) * out, axis=-1, keepdims=True)
            daff = jnp.where(mask, mm_nt(dnum, v) - dden, 0.0).astype(BF16)
            dzq = mm(daff, kf) * qd
            dzk = mm_tn(daff, qf) * kd
            put(0, h, mm_tn(q, dzq.astype(BF16)), jnp.sum(dzq, axis=0, keepdims=True))
            put(1, h, mm_tn(k, dzk.astype(BF16)), jnp.sum(dzk, axis=0, keepdims=True))

    attend(0)
    attend(1)
    ag_step(0, 0, 0)
    ag_step(0, 0, 1)
    recv("qb", "2a")
    send("qb", "3x")
    recv("qb", "2b")
    send("qb", "3y")

    own_column = core == t % 2

    with scope("Wwz"):

        @pl.when(own_column)
        def _():
            wz_local(0, 0).wait()
            landed(wo.at[0, pl.ds(0, 7 * 256)], wz_recv)

        @pl.when(jnp.logical_not(own_column))
        def _():
            landed(wo.at[0], wz_recv)

    def column(plane, c):
        return pl.multiple_of((2 * c + plane % 2) * 512 + (plane // 2) * 128, 128)

    def ship(n, dy, dx, d):
        dest = (t + d) % 8
        return remote(
            stage.at[n, pl.ds(pl.multiple_of(dest * 32, 32), 32)],
            hand_hbm.at[:, pl.ds(column(t, chip_at(dy, dx)), 128)],
            o_send,
            o_recv,
            {"segment": 1 - seg, "tensor": dest},
        )

    def early(n, dy, dx):
        with scope("early%d" % n):
            c = chip_at(dy, dx)
            part[n] = x_ref[:, pl.ds(column(t, c), 128)].astype(F32) + mm(attb[0], wo[2 * c])

    def late(n, dy, dx):
        with scope("late%d" % n):
            c = chip_at(dy, dx)
            stage[n] = (part[n] + mm(attb[1], wo[2 * c + 1])).astype(BF16)
            for d in (4, 3, 5, 2, 6, 1, 7, 0):
                ship(n, dy, dx, d).start()

    def grad_move(n, src, dst, dev):
        return remote(src, dst, gr_send.at[n], gr_recv.at[n], {"dp": dev})

    def chip_n(n):
        return chip_at(n % 4, n // 4)

    done2("qb")
    local["qb"].wait()
    recv("qb", "1s", "2s")
    eat("qb", qacc, wqb, (256, 512), True, 1)
    send("o", "1a", "1x", "1b", "1o", "1s")
    ag_step(0, 1, 0)
    ag_step(0, 1, 1)
    fourth("qb")
    recv("qb", "3sa", "3sb", "3sc")
    eat("qb", qacc, wqb, (256, 512), False, 2)
    recv("qb", "4s")
    eat("qb", qacc, wqb, (256, 512), False, 3)
    attend(2)
    attend(3)
    ag_step(0, 2, 0)
    ag_step(1, 0, 0)
    ag_step(0, 2, 1)
    ag_step(1, 0, 1)
    recv("o", "1a")
    send("o", "2a", "2xa")
    recv("o", "1x")
    send("o", "2b", "2c")
    local["fmw"].wait()
    local["fmb"].wait()
    student(0)
    ag_step(1, 1, 0)
    ag_step(0, 3, 0)
    student(1)
    ag_step(1, 1, 1)
    ag_step(0, 3, 1)
    recv("o", "1b")
    send("o", "2xb", "2s")
    student(2)
    ag_step(1, 2, 0)
    student(3)
    gs0[...] = gf[1 - core].astype(BF16)
    g0 = grad_move(0, gs0, gr0, sib)
    g0.start()
    ag_step(1, 2, 1)
    recv("o", "1o")
    send("o", "3sa")
    ag_end(0)
    recv("o", "1s", "2s")
    early(0, 0, 0)
    with scope("Wg0"):
        g0.wait_recv()
    gf[core] = gf[core] + gr0[...].astype(F32)
    gs1[...] = gf[core].astype(BF16)
    for n in range(1, 8):
        grad_move(1, gs1.at[chip_n(n)], gr1.at[n - 1], chip_n(n) * 2 + core).start()
    ag_step(1, 3, 0)
    recv("o", "2a")
    send("o", "3x", "3sb")
    early(1, 1, 0)
    ag_step(1, 3, 1)
    early(2, -1, 0)
    recv("o", "3sa")
    early(3, 0, 1)
    recv("o", "2b")
    send("o", "3y")
    ag_end(1)
    late(0, 0, 0)
    late(1, 1, 0)
    late(2, -1, 0)
    late(3, 0, 1)

    with scope("Wgs"):
        landed(gr1, gr_recv.at[1])
    total = gf[core, chip]
    for n in range(1, 8):
        total = total + gr1[n - 1].astype(F32)
    ga[chip] = total.astype(BF16)
    for n in range(1, 8):
        grad_move(2, ga.at[chip], ga.at[chip], chip_n(n) * 2 + core).start()

    recv("o", "2c", "2xa", "2xb")
    send("o", "3sc")
    recv("o", "3sb")
    early(4, 2, 0)
    late(4, 2, 0)
    fourth("o")
    recv("o", "3sc")
    early(5, 1, 1)
    late(5, 1, 1)
    early(6, -1, 1)
    late(6, -1, 1)
    recv("o", "4s")
    early(7, 2, 1)
    late(7, 2, 1)

    with scope("Wga"):
        landed(ga.at[pl.ds(0, 7)], gr_recv.at[2])
    g6 = grad_move(3, ga, gfin.at[core], sib)
    g6.start()
    keep = pltpu.make_async_copy(ga, gfin.at[core], loc_sem.at[8])
    keep.start()
    with scope("Wg6"):
        landed(ga, gr_recv.at[3])
    with scope("Wship"):
        landed(stage, o_recv)

    with scope("Wsend"):

        @pl.when(own_column)
        def _():
            left(wo.at[0, pl.ds(0, 7 * 256)], wz_send)

        @pl.when(jnp.logical_not(own_column))
        def _():
            left(wo.at[0], wz_send)

        for index, buf, _, _ in kinds.values():
            left(buf.at[pl.ds(0, 15)], g_send.at[index])
        left(kvt.at[pl.ds(0, 7)], kz_send)
        for k in range(2):
            left(attb.at[k, :, pl.ds(0, 7 * 256)], ag_send.at[k])
        for n, ref in enumerate((gs0, gs1.at[pl.ds(0, 7)], gs1.at[pl.ds(0, 7)], ga)):
            left(ref, gr_send.at[n])
        left(stage, o_send)
        keep.wait()


def finish(hand_in, g_in, hand_ref, fg_ref, bg_ref):
    hand_ref[...] = hand_in[...]
    for m in range(2):
        for h in range(4):
            fg_ref[m, h, 0:64, :] = g_in[m, 2 * h, 0:64, :].astype(F32)
            fg_ref[m, h, 64:128, :] = g_in[m, 2 * h + 1, 0:64, :].astype(F32)
            bg_ref[m, h : h + 1, :] = g_in[m, 2 * h, 64:80, :].astype(F32)[0:1]


def body(segment_input, attn_gain, query_weight, kv_weight, out_weight, fm_weight, fm_bias):
    cos, sin = rope_tables()
    cos2, sin2 = np.concatenate([cos, cos], axis=1), np.concatenate([-sin, sin], axis=1)
    tables = jnp.asarray(np.stack([cos2, sin2]))
    anywhere = pl.BlockSpec(memory_space=pl.ANY)
    vmem = pl.BlockSpec(memory_space=pltpu.VMEM)
    dma = pltpu.SemaphoreType.DMA
    hand, grads = pl.pallas_call(
        kernel,
        out_shape=(
            jax.ShapeDtypeStruct((32, D), BF16),
            jax.ShapeDtypeStruct((2, 8, 80, 128), BF16),
        ),
        in_specs=[anywhere] * 8,
        out_specs=(anywhere, anywhere),
        scratch_shapes=[
            pltpu.VMEM((SEQ, D), BF16),
            pltpu.VMEM((1, D), F32),
            pltpu.VMEM((2, 4, 128, 128), F32),
            pltpu.VMEM((2, 4, 128), F32),
            pltpu.VMEM((2, SEQ, 128), F32),
            pltpu.VMEM((16, SEQ, 512), BF16),
            pltpu.VMEM((16, 512, 128), BF16),
            pltpu.VMEM((16, 512, 256), BF16),
            pltpu.VMEM((16, 512, 256), BF16),
            pltpu.VMEM((16, 2048, 128), BF16),
            pltpu.VMEM((SEQ, 128), F32),
            pltpu.VMEM((SEQ, 512), F32),
            pltpu.VMEM((128, SEQ), BF16),
            pltpu.VMEM((8, 32, SEQ), BF16),
            pltpu.VMEM((SEQ, 128), BF16),
            pltpu.VMEM((128, SEQ), BF16),
            pltpu.VMEM((SEQ, 128), BF16),
            pltpu.VMEM((4, SEQ, 128), BF16),
            pltpu.VMEM((2, SEQ, 2048), BF16),
            pltpu.VMEM((8, SEQ, 128), F32),
            pltpu.VMEM((8, SEQ, 128), BF16),
            pltpu.VMEM((2, 8, 80, 128), F32),
            pltpu.VMEM((8, 80, 128), BF16),
            pltpu.VMEM((8, 80, 128), BF16),
            pltpu.VMEM((8, 80, 128), BF16),
            pltpu.VMEM((7, 80, 128), BF16),
            pltpu.VMEM((8, 80, 128), BF16),
            dma((9,)),
            dma(()),
            dma((4,)),
            dma((4, len(STAGE_MOVES))),
            dma(()),
            dma(()),
            dma(()),
            dma(()),
            dma((2,)),
            dma((2, 8)),
            dma((4,)),
            dma((4,)),
            dma(()),
            dma(()),
        ],
        compiler_params=pltpu.CompilerParams(
            collective_id=0,
            has_side_effects=True,
            vmem_limit_bytes=60 * 1024 * 1024,
        ),
    )(
        segment_input[0],
        attn_gain,
        query_weight[0],
        kv_weight[0],
        out_weight[0],
        fm_weight[0],
        fm_bias[0],
        tables,
    )
    handoff, fg, bg = pl.pallas_call(
        finish,
        out_shape=(
            jax.ShapeDtypeStruct((32, D), BF16),
            jax.ShapeDtypeStruct((2, 4, 128, 128), F32),
            jax.ShapeDtypeStruct((2, 4, 128), F32),
        ),
        in_specs=[vmem, vmem],
        out_specs=(vmem, vmem, vmem),
    )(hand, grads)
    return handoff[None], fg[None], bg[None]


def solution(mesh):
    placed = (
        P("segment", "dp", None),
        P("segment", None),
        P("segment", "dp", "tensor"),
        P("segment", "dp", "tensor"),
        P("segment", "tensor", "dp"),
        P("segment", None, "tensor", None, None),
        P("segment", None, "tensor", None),
    )
    return jax.shard_map(
        body,
        mesh=mesh,
        in_specs=placed,
        out_specs=(
            P("segment", ("dp", "tensor"), None),
            P("segment", None, "tensor", None, None),
            P("segment", None, "tensor", None),
        ),
        check_vma=False,
    )
```

```python
import jax
import jax.numpy as jnp
import numpy as np
from jax import lax
from jax.experimental import pallas as pl
from jax.experimental.pallas import tpu as pltpu
from jax.sharding import PartitionSpec as P

MESH = pl.DeviceIdType.MESH
F32 = jnp.float32
BF16 = jnp.bfloat16
D = 8192
SEQ = 256
TOKENS = 4096
EPSILON = 1e-05
ROPE_BASE = 500000.0
SCALE = 128 ** (-0.5)

STAGE_MOVES = {
    "1a": [("yp", 0, 0, 0, 2), ("ym", 0, 0, 2, 4)],
    "1b": [("yp", 0, 0, 2, 4), ("ym", 0, 0, 0, 2)],
    "1x": [("x", 0, 0, 1, 3)],
    "1o": [("x", 0, 0, 0, 1), ("x", 0, 0, 3, 4)],
    "1s": [("s", 0, 0, 0, 4)],
    "2a": [("yp", -1, 0, 0, 2), ("ym", 1, 0, 2, 4)],
    "2b": [("yp", 0, 1, 1, 2), ("ym", 0, 1, 2, 3)],
    "2c": [("yp", 0, 1, 2, 3), ("ym", 0, 1, 1, 2)],
    "2xa": [("x", -1, 0, 0, 1), ("x", 1, 0, 3, 4)],
    "2xb": [("x", -1, 0, 3, 4), ("x", 1, 0, 0, 1)],
    "2s": [("s", -1, 0, 0, 4), ("s", 1, 0, 0, 4)],
    "3y": [("yp", -1, 1, 1, 2), ("ym", 1, 1, 2, 3)],
    "3x": [("x", 2, 0, 0, 1), ("x", 2, 0, 3, 4)],
    "3sa": [("s", 0, 1, 0, 4)],
    "3sb": [("s", 2, 0, 0, 4)],
    "3sc": [("s", -1, 1, 0, 4), ("s", 1, 1, 0, 4)],
    "4s": [("s", 2, 1, 0, 4)],
}
STAGE_INDEX = {name: n for n, name in enumerate(STAGE_MOVES)}
CUTS = (0, 112, 256, 400, 512)
CUTS_OUT = (0, 288, 1024, 1760, 2048)


def rope_tables():
    half = 64
    frequency = ROPE_BASE ** (-(np.arange(half, dtype=np.float64) * (2.0 / 128)))
    angles = np.arange(SEQ, dtype=np.float64)[:, None] * frequency[None, :]
    return np.cos(angles).astype(np.float32), np.sin(angles).astype(np.float32)


def mm(a, b):
    return jnp.dot(a, b, preferred_element_type=F32)


def mm_nt(a, b):
    return lax.dot_general(a, b, (((1,), (1,)), ((), ())), preferred_element_type=F32)


def mm_tn(a, b):
    return lax.dot_general(a, b, (((0,), (0,)), ((), ())), preferred_element_type=F32)


def kernel(
    x_hbm,
    gain_hbm,
    wq_hbm,
    wkv_hbm,
    wo_hbm,
    fmw_hbm,
    fmb_hbm,
    tab_hbm,
    hand_hbm,
    gfin,
    x_ref,
    gain_ref,
    fmw_ref,
    fmb_ref,
    tab_ref,
    nrm,
    wkv,
    wqa,
    wqb,
    wo,
    kvacc,
    qacc,
    kvs,
    kvt,
    k_ref,
    kt_ref,
    v_ref,
    qrot,
    attb,
    part,
    stage,
    gf,
    gs0,
    gr0,
    gs1,
    gr1,
    ga,
    here_sem,
    loc_sem,
    idle_sem,
    g_send,
    g_recv,
    wz_send,
    wz_recv,
    kz_send,
    kz_recv,
    ag_send,
    ag_recv,
    gr_send,
    gr_recv,
    o_send,
    o_recv,
):
    dp = lax.axis_index("dp")
    seg = lax.axis_index("segment")
    t = lax.axis_index("tensor")
    core = dp % 2
    chip = dp // 2
    xl = chip % 2
    y = chip // 2
    sib = chip * 2 + (1 - core)
    xp = (y * 2 + (1 - xl)) * 2 + core
    yp = (dp + 4) % 16
    ym = (dp + 12) % 16
    peer = {"yp": yp, "ym": ym, "x": xp, "s": sib}

    def scope(name):
        return jax.named_scope(name)

    def remote(src, dst, ssem, rsem, dev):
        return pltpu.make_async_remote_copy(
            src_ref=src,
            dst_ref=dst,
            send_sem=ssem,
            recv_sem=rsem,
            device_id=dev,
            device_id_type=MESH,
        )

    def landed(ref, sem):
        remote(ref, ref, idle_sem, sem, {"dp": sib}).wait_recv()

    def left(ref, sem):
        remote(ref, ref, sem, idle_sem, {"dp": sib}).wait_send()

    barrier = pltpu.get_barrier_semaphore()
    above, below = {"tensor": (t + 1) % 8}, {"tensor": (t + 7) % 8}
    peers = [{"segment": 1 - seg, "dp": xp}, above, below, {"dp": yp}, {"dp": ym}, {"dp": xp}]
    peers.append({"dp": sib})
    for p in peers:
        pl.semaphore_signal(barrier, inc=1, device_id=p, device_id_type=MESH)

    local = {}
    for n, (name, src, dst) in enumerate(
        (
            ("x", x_hbm, x_ref),
            ("gain", gain_hbm, gain_ref),
            ("kv", wkv_hbm, wkv.at[dp]),
            ("qa", wq_hbm.at[:, pl.ds(0, 256)], wqa.at[dp]),
            ("qb", wq_hbm.at[:, pl.ds(256, 256)], wqb.at[dp]),
            ("tab", tab_hbm, tab_ref),
            ("fmw", fmw_hbm, fmw_ref),
            ("fmb", fmb_hbm, fmb_ref),
        )
    ):
        local[name] = pltpu.make_async_copy(src, dst, loc_sem.at[n])
        local[name].start()

    def chip_at(dy, dx):
        return ((y + dy + 4) % 4) * 2 + (xl + dx) % 2

    def slot_of(dy, dx, c):
        return chip_at(dy, dx) * 2 + c

    with scope("barrier"):
        pl.semaphore_wait(barrier, len(peers))

    steps = [[{"dp": xp}], [{"dp": ym}]] + [[above, below]] * 4

    def tell(n):
        for p in steps[n]:
            pl.semaphore_signal(here_sem.at[n], inc=1, device_id=p, device_id_type=MESH)

    def hear(n):
        with scope("hear%d" % n):
            pl.semaphore_wait(here_sem.at[n], len(steps[n]))

    kinds = {
        "kv": (0, wkv, lambda lo, hi: wkv_hbm.at[pl.ds(lo, hi - lo)], CUTS),
        "qa": (1, wqa, lambda lo, hi: wq_hbm.at[pl.ds(lo, hi - lo), pl.ds(0, 256)], CUTS),
        "qb": (2, wqb, lambda lo, hi: wq_hbm.at[pl.ds(lo, hi - lo), pl.ds(256, 256)], CUTS),
        "o": (3, wo, None, CUTS_OUT),
    }

    def move(kind, stage_name, which):
        index, buf, own, cuts = kinds[kind]
        direction, dy, dx, lo, hi = STAGE_MOVES[stage_name][which]
        lo, hi = cuts[lo], cuts[hi]
        slot = slot_of(dy, dx, core)
        dst = buf.at[slot, pl.ds(lo, hi - lo)]
        src = own(lo, hi) if (own is not None and dy == 0 and dx == 0) else dst
        recv_sem = g_recv.at[index, STAGE_INDEX[stage_name]]
        return remote(src, dst, g_send.at[index], recv_sem, {"dp": peer[direction]})

    def send(kind, *names):
        for name in names:
            for which in range(len(STAGE_MOVES[name])):
                move(kind, name, which).start()

    def recv(kind, *names):
        index, buf, _, cuts = kinds[kind]
        with scope("W_%s_%s" % (kind, "_".join(names))):
            for name in names:
                rows = sum(cuts[m[4]] - cuts[m[3]] for m in STAGE_MOVES[name])
                ref = buf.at[pl.ds(0, 2)] if rows > cuts[4] else buf.at[0, pl.ds(0, rows)]
                landed(ref, g_recv.at[index, STAGE_INDEX[name]])

    def first(kind):
        send(kind, "1a", "1x", "1b", "1o", "1s")

    def wz(p, k):
        dst_dp = chip * 2 + k
        return remote(
            wo_hbm.at[pl.ds(k * 256, 256), pl.ds(p * 128, 128)],
            wo.at[dst_dp, pl.ds(pl.multiple_of(t * 256, 256), 256)],
            wz_send,
            wz_recv,
            {"dp": dst_dp, "tensor": 2 * p + core},
        )

    def wz_local(p, k):
        return pltpu.make_async_copy(
            wo_hbm.at[pl.ds(k * 256, 256), pl.ds(p * 128, 128)],
            wo.at[chip * 2 + k, pl.ds(pl.multiple_of(t * 256, 256), 256)],
            loc_sem.at[8],
        )

    def is_self(p, k):
        return jnp.logical_and(t == 2 * p + core, core == k)

    send("kv", "1a", "1x")
    tell(0)

    def norm_rows(r, carry):
        rows = pl.ds(pl.multiple_of(r * 16, 16), 16)
        total = jnp.zeros((16, 512), F32)
        for j in range(16):
            v = x_ref[rows, j * 512 : (j + 1) * 512].astype(F32)
            total = total + v * v
        inv = lax.rsqrt(jnp.sum(total, axis=-1, keepdims=True) * (1.0 / D) + EPSILON)
        for j in range(16):
            v = x_ref[rows, j * 512 : (j + 1) * 512].astype(F32)
            nrm[j, rows, :] = (v * inv * gain_ref[:, j * 512 : (j + 1) * 512]).astype(BF16)
        return carry

    local["x"].wait()
    local["gain"].wait()
    with scope("norm1"):
        lax.fori_loop(0, 2, norm_rows, 0)
    send("kv", "1b", "1o", "1s")
    hear(0)
    tell(1)
    with scope("norm1"):
        lax.fori_loop(2, 6, norm_rows, 0)
    first("qa")
    hear(1)
    tell(2)
    recv("kv", "1a")
    send("kv", "2a", "2xa")
    recv("kv", "1x")
    send("kv", "2b", "2c")
    hear(2)
    tell(3)
    with scope("norm2"):
        lax.fori_loop(6, 16, norm_rows, 0)
    recv("kv", "1b")
    send("kv", "2xb", "2s")
    hear(3)
    tell(4)
    recv("qa", "1a")
    send("qa", "2a", "2xa")
    recv("qa", "1x")
    send("qa", "2b")
    hear(4)
    tell(5)

    def eat(name, acc, buf, cols, start, wave):
        def add(n, carry):
            if wave == 1:
                dy, dx = n + 3, 0
            elif wave == 2:
                dy, dx = n + 3, 1 - n // 3
            else:
                dy, dx = n + 2, 1
            slot = slot_of(dy, dx, 0)
            acc[:, cols[0] : cols[1]] += mm(nrm[slot], buf[slot]) + mm(nrm[slot + 1], buf[slot + 1])
            return carry

        with scope("eat_%s%d" % (name, wave)):
            if start:
                acc[:, cols[0] : cols[1]] = jnp.zeros((SEQ, cols[1] - cols[0]), F32)
            lax.fori_loop(0, {1: 3, 2: 4, 3: 1}[wave], add, 0)

    def fourth(kind):
        recv(kind, "3y", "3x")
        send(kind, "4s")

    def done2(kind):
        recv(kind, "2c", "2xa", "2xb", "1o")
        send(kind, "3sb", "3sa", "3sc")

    hear(5)
    for p in range(4):
        for k in range(2):

            @pl.when(jnp.logical_not(is_self(p, k)))
            def _(p=p, k=k):
                wz(p, k).start()

            @pl.when(is_self(p, k))
            def _(p=p, k=k):
                wz_local(p, k).start()

    recv("kv", "2a")
    send("kv", "3x")
    recv("kv", "2b")
    send("kv", "3y")
    send("qa", "2c")
    recv("qa", "1b")
    send("qa", "2xb", "2s")
    send("qb", "1a", "1x")
    done2("kv")
    local["kv"].wait()
    recv("kv", "1s", "2s")
    eat("kv", kvacc, wkv, (0, 128), True, 1)
    recv("qa", "2a")
    send("qa", "3x")
    recv("qa", "2b")
    send("qa", "3y")
    fourth("kv")
    recv("kv", "3sa", "3sb", "3sc")
    eat("kv", kvacc, wkv, (0, 128), False, 2)
    done2("qa")
    send("qb", "1b", "1o", "1s")
    recv("kv", "4s")
    eat("kv", kvacc, wkv, (0, 128), False, 3)

    r_i = lax.broadcasted_iota(jnp.int32, (128, 128), 0)
    c_i = lax.broadcasted_iota(jnp.int32, (128, 128), 1)
    pick = (c_i == (r_i & 31) * 4 + (r_i >> 5)).astype(BF16)
    kvs[...] = mm_nt(pick, kvacc[...].astype(BF16)).astype(BF16)

    def kz(d):
        dest = (t + d) % 8
        return remote(
            kvs.at[pl.ds(pl.multiple_of((dest // 2) * 32, 32), 32)],
            kvt.at[t],
            kz_send,
            kz_recv,
            {"tensor": dest},
        )

    for d in range(1, 8):
        kz(d).start()
    kvt[t] = kvs[pl.ds(pl.multiple_of((t // 2) * 32, 32), 32), :]

    recv("qb", "1a")
    send("qb", "2a", "2xa")
    recv("qb", "1x")
    send("qb", "2b", "2c")
    local["qa"].wait()
    recv("qa", "1s", "2s")
    eat("qa", qacc, wqa, (0, 256), True, 1)
    fourth("qa")
    recv("qa", "3sa", "3sb", "3sc")
    eat("qa", qacc, wqa, (0, 256), False, 2)
    local["tab"].wait()
    with scope("Wkz"):
        landed(kvt.at[pl.ds(0, 7)], kz_recv)
    kall = kvt[0:4].reshape(128, SEQ).astype(F32)
    k1, k2 = kall[0:64], kall[64:128]
    ct, st = tab_ref[0].T[0:64], tab_ref[1].T[64:128]
    krot = jnp.concatenate([k1 * ct - k2 * st, k2 * ct + k1 * st], axis=0)
    kt_ref[...] = krot.astype(BF16)
    k_ref[...] = krot.T.astype(BF16)
    v_ref[...] = kvt[4:8].reshape(128, SEQ).astype(F32).T.astype(BF16)

    recv("qa", "4s")
    eat("qa", qacc, wqa, (0, 256), False, 3)

    row_i = lax.broadcasted_iota(jnp.int32, (SEQ, SEQ), 0)
    col_i = lax.broadcasted_iota(jnp.int32, (SEQ, SEQ), 1)
    mask = row_i >= col_i

    def attend(h):
        with scope("attend%d" % h):
            q = qacc[:, h * 128 : (h + 1) * 128]
            q = (q * tab_ref[0] + pltpu.roll(q, 64, 1) * tab_ref[1]).astype(BF16)
            qrot[h] = q
            scores = mm(q, kt_ref[...]) * SCALE
            scores = jnp.where(mask, scores, -jnp.inf)
            lifted = jnp.exp(scores - jnp.max(scores, axis=-1, keepdims=True))
            prob = (lifted / jnp.sum(lifted, axis=-1, keepdims=True)).astype(BF16)
            c0 = (h % 2) * 128
            cols = pl.ds(pl.multiple_of(t * 256 + c0, 128), 128)
            attb[h // 2, :, cols] = mm(prob, v_ref[...]).astype(BF16)

    def ag(k, s, up, half):
        slot = (t + 8 - s) % 8 if up else (t + s) % 8
        ref = attb.at[k, pl.ds(half * 128, 128), pl.ds(pl.multiple_of(slot * 256, 256), 256)]
        dest = (t + 1) % 8 if up else (t + 7) % 8
        return remote(ref, ref, ag_send.at[k], ag_recv.at[k, 2 * s + half], {"tensor": dest})

    def ag_step(k, s, half):
        if s > 0:
            with scope("Wag%d_%d_%d" % (k, s, half)):
                landed(attb.at[k, :, pl.ds(0, 256)], ag_recv.at[k, 2 * s - 2 + half])
        if s < 3 or half == 0:
            ag(k, s, True, half).start()
        if s < 3 or half == 1:
            ag(k, s, False, half).start()

    def ag_end(k, *halves):
        for half in halves:
            with scope("Wag%d_end%d" % (k, half)):
                landed(attb.at[k, pl.ds(0, 128), pl.ds(0, 256)], ag_recv.at[k, 6 + half])

    lead = (lax.broadcasted_iota(jnp.int32, (16, 128), 0) == 0).astype(F32)

    def feature(z):
        e = jnp.exp(jnp.minimum(z, 0.0))
        pos = z > 0
        return jnp.where(pos, z + 1.0, e).astype(BF16), jnp.where(pos, 1.0, e)

    def pre(a, m, h):
        w = fmw_ref[m, h]
        hi = w.astype(BF16)
        low = (w - hi.astype(F32)).astype(BF16)
        return mm(a, hi) + mm(a, low) + fmb_ref[m, pl.ds(h, 1), :]

    def put(m, h, weight, bias):
        gf[m, 2 * h, 0:64, :] = weight[0:64]
        gf[m, 2 * h + 1, 0:64, :] = weight[64:128]
        gf[m, 2 * h, 64:80, :] = bias * lead
        gf[m, 2 * h + 1, 64:80, :] = jnp.zeros((16, 128), F32)

    def student(h):
        with scope("student%d" % h):
            q, k, v = qrot[h], k_ref[...], v_ref[...]
            cols = pl.ds(pl.multiple_of(t * 256 + (h % 2) * 128, 128), 128)
            att = attb[h // 2, :, cols].astype(F32)
            qf, qd = feature(pre(q, 0, h))
            kf, kd = feature(pre(k, 1, h))
            aff = jnp.where(mask, mm_nt(qf, kf), 0.0)
            den = jnp.sum(aff, axis=-1, keepdims=True)
            out = mm(aff.astype(BF16), v) / den
            dnum = ((out - att) * (2.0 / TOKENS) / den).astype(BF16)
            dden = jnp.sum(dnum.astype(F32) * out, axis=-1, keepdims=True)
            daff = jnp.where(mask, mm_nt(dnum, v) - dden, 0.0).astype(BF16)
            dzq = mm(daff, kf) * qd
            dzk = mm_tn(daff, qf) * kd
            put(0, h, mm_tn(q, dzq.astype(BF16)), jnp.sum(dzq, axis=0, keepdims=True))
            put(1, h, mm_tn(k, dzk.astype(BF16)), jnp.sum(dzk, axis=0, keepdims=True))

    attend(0)
    attend(1)
    ag_step(0, 0, 0)
    ag_step(0, 0, 1)
    recv("qb", "1b")
    send("qb", "2xb", "2s")
    local["fmw"].wait()
    local["fmb"].wait()
    student(0)
    recv("qb", "2a")
    send("qb", "3x")
    recv("qb", "2b")
    send("qb", "3y")
    ag_step(0, 1, 0)
    ag_step(0, 1, 1)

    own_column = core == t % 2

    with scope("Wwz"):

        @pl.when(own_column)
        def _():
            wz_local(0, 0).wait()
            landed(wo.at[0, pl.ds(0, 7 * 256)], wz_recv)

        @pl.when(jnp.logical_not(own_column))
        def _():
            landed(wo.at[0], wz_recv)

    def column(plane, c):
        return pl.multiple_of((2 * c + plane % 2) * 512 + (plane // 2) * 128, 128)

    def ship(n, dy, dx, dest):
        return remote(
            stage.at[n, pl.ds(pl.multiple_of(dest * 32, 32), 32)],
            hand_hbm.at[:, pl.ds(column(t, chip_at(dy, dx)), 128)],
            o_send,
            o_recv,
            {"segment": 1 - seg, "tensor": dest},
        )

    def early(n, dy, dx, own=False):
        with scope("early%d" % n):
            c = chip_at(dy, dx)
            k = core if own else 0
            part[n] = x_ref[:, pl.ds(column(t, c), 128)].astype(F32) + mm(attb[k], wo[2 * c + k])

    def late(n, dy, dx, halves=(0, 1), own=False):
        with scope("late%d" % n):
            c = chip_at(dy, dx)
            k = 1 - core if own else 1
            lo, hi = halves[0] * 128, halves[-1] * 128 + 128
            product = mm(attb[k, lo:hi], wo[2 * c + k])
            stage[n, lo:hi] = (part[n, lo:hi] + product).astype(BF16)
            for half in halves:
                for j in (2, 1, 3, 0):
                    ship(n, dy, dx, half * 4 + (t + j) % 4).start()

    def grad_move(n, src, dst, dev):
        return remote(src, dst, gr_send.at[n], gr_recv.at[n], {"dp": dev})

    def chip_n(n):
        return chip_at(n % 4, n // 4)

    done2("qb")
    local["qb"].wait()
    recv("qb", "1s", "2s")
    eat("qb", qacc, wqb, (256, 512), True, 1)
    send("o", "1a", "1x")
    student(1)
    fourth("qb")
    recv("qb", "3sa", "3sb", "3sc")
    send("o", "1b", "1o", "1s")
    ag_step(0, 2, 0)
    ag_step(0, 2, 1)
    eat("qb", qacc, wqb, (256, 512), False, 2)
    recv("qb", "4s")
    eat("qb", qacc, wqb, (256, 512), False, 3)
    attend(2)
    attend(3)
    ag_step(1, 0, 0)
    student(2)
    ag_step(1, 0, 1)
    recv("o", "1a")
    send("o", "2a", "2xa")
    ag_step(0, 3, 0)
    ag_step(0, 3, 1)
    student(3)
    gs0[...] = gf[1 - core].astype(BF16)
    g0 = grad_move(0, gs0, gr0, sib)
    g0.start()
    ag_step(1, 1, 0)
    recv("o", "1x")
    send("o", "2b")
    ag_step(1, 1, 1)
    send("o", "2c")
    ag_end(0, 0, 1)
    recv("o", "1s")
    early(0, 0, 0)
    ag_step(1, 2, 0)
    recv("o", "1b")
    send("o", "2xb", "2s")
    with scope("Wg0"):
        g0.wait_recv()
    gf[core] = gf[core] + gr0[...].astype(F32)
    gs1[...] = gf[core].astype(BF16)
    for n in range(1, 8):
        grad_move(1, gs1.at[chip_n(n)], gr1.at[n - 1], chip_n(n) * 2 + core).start()
    ag_step(1, 2, 1)
    recv("o", "1o")
    send("o", "3sa")
    ag_step(1, 3, 0)
    recv("o", "2s")
    early(1, 1, 0)
    early(2, -1, 0)
    ag_step(1, 3, 1)
    recv("o", "2a")
    send("o", "3x", "3sb")
    ag_end(1, 0)
    late(0, 0, 0, (0,))
    late(1, 1, 0, (0,))
    late(2, -1, 0, (0,))
    recv("o", "2b")
    send("o", "3y")
    recv("o", "3sa")
    early(3, 0, 1)
    late(3, 0, 1, (0,))
    ag_end(1, 1)
    late(0, 0, 0, (1,))
    late(1, 1, 0, (1,))
    late(2, -1, 0, (1,))
    late(3, 0, 1, (1,))
    recv("o", "3sb")
    early(4, 2, 0)
    late(4, 2, 0)
    recv("o", "2c", "2xa", "2xb")
    send("o", "3sc")
    early(5, 1, 1, True)
    early(6, -1, 1, True)

    with scope("Wgs"):
        landed(gr1, gr_recv.at[1])
    total = gf[core, chip]
    for n in range(1, 8):
        total = total + gr1[n - 1].astype(F32)
    ga[chip] = total.astype(BF16)
    for n in range(1, 8):
        grad_move(2, ga.at[chip], ga.at[chip], chip_n(n) * 2 + core).start()

    recv("o", "3sc")
    late(5, 1, 1, own=True)
    late(6, -1, 1, own=True)
    fourth("o")
    early(7, 2, 1, True)
    recv("o", "4s")
    late(7, 2, 1, own=True)

    with scope("Wga"):
        landed(ga.at[pl.ds(0, 7)], gr_recv.at[2])
    g6 = grad_move(3, ga, gfin.at[core], sib)
    g6.start()
    keep = pltpu.make_async_copy(ga, gfin.at[core], loc_sem.at[8])
    keep.start()
    with scope("Wg6"):
        landed(ga, gr_recv.at[3])
    with scope("Wship"):
        landed(stage, o_recv)

    with scope("Wsend"):

        @pl.when(own_column)
        def _():
            left(wo.at[0, pl.ds(0, 7 * 256)], wz_send)

        @pl.when(jnp.logical_not(own_column))
        def _():
            left(wo.at[0], wz_send)

        for index, buf, _, _ in kinds.values():
            left(buf.at[pl.ds(0, 15)], g_send.at[index])
        left(kvt.at[pl.ds(0, 7)], kz_send)
        for k in range(2):
            left(attb.at[k, :, pl.ds(0, 7 * 256)], ag_send.at[k])
        for n, ref in enumerate((gs0, gs1.at[pl.ds(0, 7)], gs1.at[pl.ds(0, 7)], ga)):
            left(ref, gr_send.at[n])
        left(stage, o_send)
        keep.wait()


def finish(hand_in, g_in, hand_ref, fg_ref, bg_ref):
    hand_ref[...] = hand_in[...]
    for m in range(2):
        for h in range(4):
            fg_ref[m, h, 0:64, :] = g_in[m, 2 * h, 0:64, :].astype(F32)
            fg_ref[m, h, 64:128, :] = g_in[m, 2 * h + 1, 0:64, :].astype(F32)
            bg_ref[m, h : h + 1, :] = g_in[m, 2 * h, 64:80, :].astype(F32)[0:1]


def body(segment_input, attn_gain, query_weight, kv_weight, out_weight, fm_weight, fm_bias):
    cos, sin = rope_tables()
    cos2, sin2 = np.concatenate([cos, cos], axis=1), np.concatenate([-sin, sin], axis=1)
    tables = jnp.asarray(np.stack([cos2, sin2]))
    anywhere = pl.BlockSpec(memory_space=pl.ANY)
    vmem = pl.BlockSpec(memory_space=pltpu.VMEM)
    dma = pltpu.SemaphoreType.DMA
    hand, grads = pl.pallas_call(
        kernel,
        out_shape=(
            jax.ShapeDtypeStruct((32, D), BF16),
            jax.ShapeDtypeStruct((2, 8, 80, 128), BF16),
        ),
        in_specs=[anywhere] * 8,
        out_specs=(anywhere, anywhere),
        scratch_shapes=[
            pltpu.VMEM((SEQ, D), BF16),
            pltpu.VMEM((1, D), F32),
            pltpu.VMEM((2, 4, 128, 128), F32),
            pltpu.VMEM((2, 4, 128), F32),
            pltpu.VMEM((2, SEQ, 128), F32),
            pltpu.VMEM((16, SEQ, 512), BF16),
            pltpu.VMEM((16, 512, 128), BF16),
            pltpu.VMEM((16, 512, 256), BF16),
            pltpu.VMEM((16, 512, 256), BF16),
            pltpu.VMEM((16, 2048, 128), BF16),
            pltpu.VMEM((SEQ, 128), F32),
            pltpu.VMEM((SEQ, 512), F32),
            pltpu.VMEM((128, SEQ), BF16),
            pltpu.VMEM((8, 32, SEQ), BF16),
            pltpu.VMEM((SEQ, 128), BF16),
            pltpu.VMEM((128, SEQ), BF16),
            pltpu.VMEM((SEQ, 128), BF16),
            pltpu.VMEM((4, SEQ, 128), BF16),
            pltpu.VMEM((2, SEQ, 2048), BF16),
            pltpu.VMEM((8, SEQ, 128), F32),
            pltpu.VMEM((8, SEQ, 128), BF16),
            pltpu.VMEM((2, 8, 80, 128), F32),
            pltpu.VMEM((8, 80, 128), BF16),
            pltpu.VMEM((8, 80, 128), BF16),
            pltpu.VMEM((8, 80, 128), BF16),
            pltpu.VMEM((7, 80, 128), BF16),
            pltpu.VMEM((8, 80, 128), BF16),
            pltpu.SemaphoreType.REGULAR((6,)),
            dma((9,)),
            dma(()),
            dma((4,)),
            dma((4, len(STAGE_MOVES))),
            dma(()),
            dma(()),
            dma(()),
            dma(()),
            dma((2,)),
            dma((2, 8)),
            dma((4,)),
            dma((4,)),
            dma(()),
            dma(()),
        ],
        compiler_params=pltpu.CompilerParams(
            collective_id=0,
            has_side_effects=True,
            vmem_limit_bytes=60 * 1024 * 1024,
        ),
    )(
        segment_input[0],
        attn_gain,
        query_weight[0],
        kv_weight[0],
        out_weight[0],
        fm_weight[0],
        fm_bias[0],
        tables,
    )
    handoff, fg, bg = pl.pallas_call(
        finish,
        out_shape=(
            jax.ShapeDtypeStruct((32, D), BF16),
            jax.ShapeDtypeStruct((2, 4, 128, 128), F32),
            jax.ShapeDtypeStruct((2, 4, 128), F32),
        ),
        in_specs=[vmem, vmem],
        out_specs=(vmem, vmem, vmem),
    )(hand, grads)
    return handoff[None], fg[None], bg[None]


def solution(mesh):
    placed = (
        P("segment", "dp", None),
        P("segment", None),
        P("segment", "dp", "tensor"),
        P("segment", "dp", "tensor"),
        P("segment", "tensor", "dp"),
        P("segment", None, "tensor", None, None),
        P("segment", None, "tensor", None),
    )
    return jax.shard_map(
        body,
        mesh=mesh,
        in_specs=placed,
        out_specs=(
            P("segment", ("dp", "tensor"), None),
            P("segment", None, "tensor", None, None),
            P("segment", None, "tensor", None),
        ),
        check_vma=False,
    )
```

```python
import jax
import jax.numpy as jnp
import numpy as np
from jax import lax
from jax.experimental import pallas as pl
from jax.experimental.pallas import tpu as pltpu
from jax.sharding import PartitionSpec as P

MESH = pl.DeviceIdType.MESH
F32 = jnp.float32
BF16 = jnp.bfloat16
D = 8192
SEQ = 256
TOKENS = 4096
EPSILON = 1e-05
ROPE_BASE = 500000.0
SCALE = 128 ** (-0.5)

STAGE_MOVES = {
    "1a": [("yp", 0, 0, 0, 2), ("ym", 0, 0, 2, 4)],
    "1b": [("yp", 0, 0, 2, 4), ("ym", 0, 0, 0, 2)],
    "1x": [("x", 0, 0, 1, 3)],
    "1o": [("x", 0, 0, 0, 1), ("x", 0, 0, 3, 4)],
    "1s": [("s", 0, 0, 0, 4)],
    "2a": [("yp", -1, 0, 0, 2), ("ym", 1, 0, 2, 4)],
    "2b": [("yp", 0, 1, 1, 2), ("ym", 0, 1, 2, 3)],
    "2c": [("yp", 0, 1, 2, 3), ("ym", 0, 1, 1, 2)],
    "2xa": [("x", -1, 0, 0, 1), ("x", 1, 0, 3, 4)],
    "2xb": [("x", -1, 0, 3, 4), ("x", 1, 0, 0, 1)],
    "2s": [("s", -1, 0, 0, 4), ("s", 1, 0, 0, 4)],
    "3y": [("yp", -1, 1, 1, 2), ("ym", 1, 1, 2, 3)],
    "3x": [("x", 2, 0, 0, 1), ("x", 2, 0, 3, 4)],
    "3sa": [("s", 0, 1, 0, 4)],
    "3sb": [("s", 2, 0, 0, 4)],
    "3sc": [("s", -1, 1, 0, 4), ("s", 1, 1, 0, 4)],
    "4s": [("s", 2, 1, 0, 4)],
}
STAGE_INDEX = {name: n for n, name in enumerate(STAGE_MOVES)}
CUTS = (0, 112, 256, 400, 512)
CUTS_OUT = (0, 304, 1024, 1744, 2048)


def rope_tables():
    half = 64
    frequency = ROPE_BASE ** (-(np.arange(half, dtype=np.float64) * (2.0 / 128)))
    angles = np.arange(SEQ, dtype=np.float64)[:, None] * frequency[None, :]
    return np.cos(angles).astype(np.float32), np.sin(angles).astype(np.float32)


def mm(a, b):
    return jnp.dot(a, b, preferred_element_type=F32)


def mm_nt(a, b):
    return lax.dot_general(a, b, (((1,), (1,)), ((), ())), preferred_element_type=F32)


def mm_tn(a, b):
    return lax.dot_general(a, b, (((0,), (0,)), ((), ())), preferred_element_type=F32)


def kernel(
    x_hbm,
    gain_hbm,
    wq_hbm,
    wkv_hbm,
    wo_hbm,
    fmw_hbm,
    fmb_hbm,
    tab_hbm,
    hand_hbm,
    gfin,
    x_ref,
    gain_ref,
    fmw_ref,
    fmb_ref,
    tab_ref,
    nrm,
    wkv,
    wqa,
    wqb,
    wo,
    kvacc,
    qacc,
    kvs,
    kvt,
    k_ref,
    kt_ref,
    v_ref,
    qrot,
    attb,
    part,
    stage,
    gf,
    gs0,
    gr0,
    gs1,
    gr1,
    ga,
    here_sem,
    loc_sem,
    idle_sem,
    g_send,
    g_recv,
    wz_send,
    wz_recv,
    kz_send,
    kz_recv,
    ag_send,
    ag_recv,
    gr_send,
    gr_recv,
    o_send,
    o_recv,
):
    dp = lax.axis_index("dp")
    seg = lax.axis_index("segment")
    t = lax.axis_index("tensor")
    core = dp % 2
    chip = dp // 2
    xl = chip % 2
    y = chip // 2
    sib = chip * 2 + (1 - core)
    xp = (y * 2 + (1 - xl)) * 2 + core
    yp = (dp + 4) % 16
    ym = (dp + 12) % 16
    peer = {"yp": yp, "ym": ym, "x": xp, "s": sib}

    def scope(name):
        return jax.named_scope(name)

    def remote(src, dst, ssem, rsem, dev):
        return pltpu.make_async_remote_copy(
            src_ref=src,
            dst_ref=dst,
            send_sem=ssem,
            recv_sem=rsem,
            device_id=dev,
            device_id_type=MESH,
        )

    def landed(ref, sem):
        remote(ref, ref, idle_sem, sem, {"dp": sib}).wait_recv()

    def left(ref, sem):
        remote(ref, ref, sem, idle_sem, {"dp": sib}).wait_send()

    barrier = pltpu.get_barrier_semaphore()
    above, below = {"tensor": (t + 1) % 8}, {"tensor": (t + 7) % 8}
    peers = [{"segment": 1 - seg, "dp": xp}, above, below, {"dp": yp}, {"dp": ym}, {"dp": xp}]
    peers.append({"dp": sib})
    for p in peers:
        pl.semaphore_signal(barrier, inc=1, device_id=p, device_id_type=MESH)

    local = {}
    for n, (name, src, dst) in enumerate(
        (
            ("x", x_hbm, x_ref),
            ("gain", gain_hbm, gain_ref),
            ("kv", wkv_hbm, wkv.at[dp]),
            ("qa", wq_hbm.at[:, pl.ds(0, 256)], wqa.at[dp]),
            ("qb", wq_hbm.at[:, pl.ds(256, 256)], wqb.at[dp]),
            ("tab", tab_hbm, tab_ref),
            ("fmw", fmw_hbm, fmw_ref),
            ("fmb", fmb_hbm, fmb_ref),
        )
    ):
        local[name] = pltpu.make_async_copy(src, dst, loc_sem.at[n])
        local[name].start()

    def chip_at(dy, dx):
        return ((y + dy + 4) % 4) * 2 + (xl + dx) % 2

    def slot_of(dy, dx, c):
        return chip_at(dy, dx) * 2 + c

    with scope("barrier"):
        pl.semaphore_wait(barrier, len(peers))

    steps = [[{"dp": xp}], [{"dp": ym}]] + [[above, below]] * 4

    def tell(n):
        for p in steps[n]:
            pl.semaphore_signal(here_sem.at[n], inc=1, device_id=p, device_id_type=MESH)

    def hear(n):
        with scope("hear%d" % n):
            pl.semaphore_wait(here_sem.at[n], len(steps[n]))

    kinds = {
        "kv": (0, wkv, lambda lo, hi: wkv_hbm.at[pl.ds(lo, hi - lo)], CUTS),
        "qa": (1, wqa, lambda lo, hi: wq_hbm.at[pl.ds(lo, hi - lo), pl.ds(0, 256)], CUTS),
        "qb": (2, wqb, lambda lo, hi: wq_hbm.at[pl.ds(lo, hi - lo), pl.ds(256, 256)], CUTS),
        "o": (3, wo, None, CUTS_OUT),
    }

    def move(kind, stage_name, which):
        index, buf, own, cuts = kinds[kind]
        direction, dy, dx, lo, hi = STAGE_MOVES[stage_name][which]
        lo, hi = cuts[lo], cuts[hi]
        slot = slot_of(dy, dx, core)
        dst = buf.at[slot, pl.ds(lo, hi - lo)]
        src = own(lo, hi) if (own is not None and dy == 0 and dx == 0) else dst
        recv_sem = g_recv.at[index, STAGE_INDEX[stage_name]]
        return remote(src, dst, g_send.at[index], recv_sem, {"dp": peer[direction]})

    def send(kind, *names):
        for name in names:
            for which in range(len(STAGE_MOVES[name])):
                move(kind, name, which).start()

    def recv(kind, *names):
        index, buf, _, cuts = kinds[kind]
        with scope("W_%s_%s" % (kind, "_".join(names))):
            for name in names:
                rows = sum(cuts[m[4]] - cuts[m[3]] for m in STAGE_MOVES[name])
                ref = buf.at[pl.ds(0, 2)] if rows > cuts[4] else buf.at[0, pl.ds(0, rows)]
                landed(ref, g_recv.at[index, STAGE_INDEX[name]])

    def first(kind):
        send(kind, "1a", "1x", "1b", "1o", "1s")

    def wz(p, k):
        dst_dp = chip * 2 + k
        return remote(
            wo_hbm.at[pl.ds(k * 256, 256), pl.ds(p * 128, 128)],
            wo.at[dst_dp, pl.ds(pl.multiple_of(t * 256, 256), 256)],
            wz_send,
            wz_recv,
            {"dp": dst_dp, "tensor": 2 * p + core},
        )

    def wz_local(p, k):
        return pltpu.make_async_copy(
            wo_hbm.at[pl.ds(k * 256, 256), pl.ds(p * 128, 128)],
            wo.at[chip * 2 + k, pl.ds(pl.multiple_of(t * 256, 256), 256)],
            loc_sem.at[8],
        )

    def is_self(p, k):
        return jnp.logical_and(t == 2 * p + core, core == k)

    send("kv", "1a", "1x")
    tell(0)

    def norm_rows(r, carry):
        rows = pl.ds(pl.multiple_of(r * 16, 16), 16)
        total = jnp.zeros((16, 512), F32)
        for j in range(16):
            v = x_ref[rows, j * 512 : (j + 1) * 512].astype(F32)
            total = total + v * v
        inv = lax.rsqrt(jnp.sum(total, axis=-1, keepdims=True) * (1.0 / D) + EPSILON)
        for j in range(16):
            v = x_ref[rows, j * 512 : (j + 1) * 512].astype(F32)
            nrm[j, rows, :] = (v * inv * gain_ref[:, j * 512 : (j + 1) * 512]).astype(BF16)
        return carry

    local["x"].wait()
    local["gain"].wait()
    with scope("norm1"):
        lax.fori_loop(0, 2, norm_rows, 0)
    send("kv", "1b", "1o", "1s")
    hear(0)
    tell(1)
    with scope("norm1"):
        lax.fori_loop(2, 6, norm_rows, 0)
    first("qa")
    hear(1)
    tell(2)
    recv("kv", "1a")
    send("kv", "2a", "2xa")
    recv("kv", "1x")
    send("kv", "2b", "2c")
    hear(2)
    tell(3)
    with scope("norm2"):
        lax.fori_loop(6, 16, norm_rows, 0)
    recv("kv", "1b")
    send("kv", "2xb", "2s")
    hear(3)
    tell(4)
    recv("qa", "1a")
    send("qa", "2a", "2xa")
    recv("qa", "1x")
    send("qa", "2b")
    hear(4)
    tell(5)

    def eat(name, acc, buf, cols, start, wave):
        def add(n, carry):
            if wave == 1:
                dy, dx = n + 3, 0
            elif wave == 2:
                dy, dx = n + 3, 1 - n // 3
            else:
                dy, dx = n + 2, 1
            slot = slot_of(dy, dx, 0)
            acc[:, cols[0] : cols[1]] += mm(nrm[slot], buf[slot]) + mm(nrm[slot + 1], buf[slot + 1])
            return carry

        with scope("eat_%s%d" % (name, wave)):
            if start:
                acc[:, cols[0] : cols[1]] = jnp.zeros((SEQ, cols[1] - cols[0]), F32)
            lax.fori_loop(0, {1: 3, 2: 4, 3: 1}[wave], add, 0)

    def fourth(kind):
        recv(kind, "3y", "3x")
        send(kind, "4s")

    def done2(kind):
        recv(kind, "2c", "2xa", "2xb", "1o")
        send(kind, "3sb", "3sa", "3sc")

    hear(5)
    for p in range(4):
        for k in range(2):

            @pl.when(jnp.logical_not(is_self(p, k)))
            def _(p=p, k=k):
                wz(p, k).start()

            @pl.when(is_self(p, k))
            def _(p=p, k=k):
                wz_local(p, k).start()

    recv("kv", "2a")
    send("kv", "3x")
    recv("kv", "2b")
    send("kv", "3y")
    send("qa", "2c")
    recv("qa", "1b")
    send("qa", "2xb", "2s")
    send("qb", "1a", "1x")
    done2("kv")
    local["kv"].wait()
    recv("kv", "1s", "2s")
    eat("kv", kvacc, wkv, (0, 128), True, 1)
    recv("qa", "2a")
    send("qa", "3x")
    recv("qa", "2b")
    send("qa", "3y")
    fourth("kv")
    recv("kv", "3sa", "3sb", "3sc")
    eat("kv", kvacc, wkv, (0, 128), False, 2)
    done2("qa")
    send("qb", "1b", "1o", "1s")
    recv("kv", "4s")
    eat("kv", kvacc, wkv, (0, 128), False, 3)

    r_i = lax.broadcasted_iota(jnp.int32, (128, 128), 0)
    c_i = lax.broadcasted_iota(jnp.int32, (128, 128), 1)
    pick = (c_i == (r_i & 31) * 4 + (r_i >> 5)).astype(BF16)
    kvs[...] = mm_nt(pick, kvacc[...].astype(BF16)).astype(BF16)

    def kz(d):
        dest = (t + d) % 8
        return remote(
            kvs.at[pl.ds(pl.multiple_of((dest // 2) * 32, 32), 32)],
            kvt.at[t],
            kz_send,
            kz_recv,
            {"tensor": dest},
        )

    for d in range(1, 8):
        kz(d).start()
    kvt[t] = kvs[pl.ds(pl.multiple_of((t // 2) * 32, 32), 32), :]

    recv("qb", "1a")
    send("qb", "2a", "2xa")
    recv("qb", "1x")
    send("qb", "2b", "2c")
    local["qa"].wait()
    recv("qa", "1s", "2s")
    eat("qa", qacc, wqa, (0, 256), True, 1)
    fourth("qa")
    recv("qa", "3sa", "3sb", "3sc")
    eat("qa", qacc, wqa, (0, 256), False, 2)
    local["tab"].wait()
    with scope("Wkz"):
        landed(kvt.at[pl.ds(0, 7)], kz_recv)
    kall = kvt[0:4].reshape(128, SEQ).astype(F32)
    k1, k2 = kall[0:64], kall[64:128]
    ct, st = tab_ref[0].T[0:64], tab_ref[1].T[64:128]
    krot = jnp.concatenate([k1 * ct - k2 * st, k2 * ct + k1 * st], axis=0)
    kt_ref[...] = krot.astype(BF16)
    k_ref[...] = krot.T.astype(BF16)
    v_ref[...] = kvt[4:8].reshape(128, SEQ).astype(F32).T.astype(BF16)

    recv("qa", "4s")
    eat("qa", qacc, wqa, (0, 256), False, 3)

    row_i = lax.broadcasted_iota(jnp.int32, (SEQ, SEQ), 0)
    col_i = lax.broadcasted_iota(jnp.int32, (SEQ, SEQ), 1)
    mask = row_i >= col_i

    def attend(h):
        with scope("attend%d" % h):
            q = qacc[:, h * 128 : (h + 1) * 128]
            q = (q * tab_ref[0] + pltpu.roll(q, 64, 1) * tab_ref[1]).astype(BF16)
            qrot[h] = q
            scores = mm(q, kt_ref[...]) * SCALE
            scores = jnp.where(mask, scores, -jnp.inf)
            lifted = jnp.exp(scores - jnp.max(scores, axis=-1, keepdims=True))
            prob = (lifted / jnp.sum(lifted, axis=-1, keepdims=True)).astype(BF16)
            c0 = (h % 2) * 128
            cols = pl.ds(pl.multiple_of(t * 256 + c0, 128), 128)
            attb[h // 2, :, cols] = mm(prob, v_ref[...]).astype(BF16)

    def ag(k, s, up, half):
        slot = (t + 8 - s) % 8 if up else (t + s) % 8
        ref = attb.at[k, pl.ds(half * 128, 128), pl.ds(pl.multiple_of(slot * 256, 256), 256)]
        dest = (t + 1) % 8 if up else (t + 7) % 8
        return remote(ref, ref, ag_send.at[k], ag_recv.at[k, 2 * s + half], {"tensor": dest})

    def ag_step(k, s, half):
        if s > 0:
            with scope("Wag%d_%d_%d" % (k, s, half)):
                landed(attb.at[k, :, pl.ds(0, 256)], ag_recv.at[k, 2 * s - 2 + half])
        if s < 3 or half == 0:
            ag(k, s, True, half).start()
        if s < 3 or half == 1:
            ag(k, s, False, half).start()

    def ag_end(k, *halves):
        for half in halves:
            with scope("Wag%d_end%d" % (k, half)):
                landed(attb.at[k, pl.ds(0, 128), pl.ds(0, 256)], ag_recv.at[k, 6 + half])

    lead = (lax.broadcasted_iota(jnp.int32, (16, 128), 0) == 0).astype(F32)

    def feature(z):
        e = jnp.exp(jnp.minimum(z, 0.0))
        pos = z > 0
        return jnp.where(pos, z + 1.0, e).astype(BF16), jnp.where(pos, 1.0, e)

    def pre(a, m, h):
        w = fmw_ref[m, h]
        hi = w.astype(BF16)
        low = (w - hi.astype(F32)).astype(BF16)
        return mm(a, hi) + mm(a, low) + fmb_ref[m, pl.ds(h, 1), :]

    def put(m, h, weight, bias):
        gf[m, 2 * h, 0:64, :] = weight[0:64]
        gf[m, 2 * h + 1, 0:64, :] = weight[64:128]
        gf[m, 2 * h, 64:80, :] = bias * lead
        gf[m, 2 * h + 1, 64:80, :] = jnp.zeros((16, 128), F32)

    def student(h):
        with scope("student%d" % h):
            q, k, v = qrot[h], k_ref[...], v_ref[...]
            cols = pl.ds(pl.multiple_of(t * 256 + (h % 2) * 128, 128), 128)
            att = attb[h // 2, :, cols].astype(F32)
            qf, qd = feature(pre(q, 0, h))
            kf, kd = feature(pre(k, 1, h))
            aff = jnp.where(mask, mm_nt(qf, kf), 0.0)
            den = jnp.sum(aff, axis=-1, keepdims=True)
            out = mm(aff.astype(BF16), v) / den
            dnum = ((out - att) * (2.0 / TOKENS) / den).astype(BF16)
            dden = jnp.sum(dnum.astype(F32) * out, axis=-1, keepdims=True)
            daff = jnp.where(mask, mm_nt(dnum, v) - dden, 0.0).astype(BF16)
            dzq = mm(daff, kf) * qd
            dzk = mm_tn(daff, qf) * kd
            put(0, h, mm_tn(q, dzq.astype(BF16)), jnp.sum(dzq, axis=0, keepdims=True))
            put(1, h, mm_tn(k, dzk.astype(BF16)), jnp.sum(dzk, axis=0, keepdims=True))

    attend(0)
    attend(1)
    ag_step(0, 0, 0)
    ag_step(0, 0, 1)
    recv("qb", "1b")
    send("qb", "2xb", "2s")
    local["fmw"].wait()
    local["fmb"].wait()
    student(0)
    recv("qb", "2a")
    send("qb", "3x")
    recv("qb", "2b")
    send("qb", "3y")

    own_column = core == t % 2

    with scope("Wwz"):

        @pl.when(own_column)
        def _():
            wz_local(0, 0).wait()
            landed(wo.at[0, pl.ds(0, 7 * 256)], wz_recv)

        @pl.when(jnp.logical_not(own_column))
        def _():
            landed(wo.at[0], wz_recv)

    send("o", "1a", "1x")
    ag_step(0, 1, 0)
    ag_step(0, 1, 1)

    def column(plane, c):
        return pl.multiple_of((2 * c + plane % 2) * 512 + (plane // 2) * 128, 128)

    def ship(n, dy, dx, dest):
        return remote(
            stage.at[n, pl.ds(pl.multiple_of(dest * 32, 32), 32)],
            hand_hbm.at[:, pl.ds(column(t, chip_at(dy, dx)), 128)],
            o_send,
            o_recv,
            {"segment": 1 - seg, "tensor": dest},
        )

    def early(n, dy, dx, own=False):
        with scope("early%d" % n):
            c = chip_at(dy, dx)
            k = core if own else 0
            part[n] = x_ref[:, pl.ds(column(t, c), 128)].astype(F32) + mm(attb[k], wo[2 * c + k])

    def late(n, dy, dx, halves=(0, 1), own=False):
        with scope("late%d" % n):
            c = chip_at(dy, dx)
            k = 1 - core if own else 1
            lo, hi = halves[0] * 128, halves[-1] * 128 + 128
            product = mm(attb[k, lo:hi], wo[2 * c + k])
            stage[n, lo:hi] = (part[n, lo:hi] + product).astype(BF16)
            for half in halves:
                for j in (2, 1, 3, 0):
                    ship(n, dy, dx, half * 4 + (t + j) % 4).start()

    def grad_move(n, src, dst, dev):
        return remote(src, dst, gr_send.at[n], gr_recv.at[n], {"dp": dev})

    def chip_n(n):
        return chip_at(n % 4, n // 4)

    done2("qb")
    local["qb"].wait()
    recv("qb", "1s", "2s")
    eat("qb", qacc, wqb, (256, 512), True, 1)
    student(1)
    fourth("qb")
    recv("qb", "3sa", "3sb", "3sc")
    send("o", "1b", "1o", "1s")
    ag_step(0, 2, 0)
    ag_step(0, 2, 1)
    eat("qb", qacc, wqb, (256, 512), False, 2)
    recv("qb", "4s")
    eat("qb", qacc, wqb, (256, 512), False, 3)
    attend(2)
    attend(3)
    ag_step(1, 0, 0)
    student(2)
    ag_step(1, 0, 1)
    recv("o", "1a")
    send("o", "2a", "2xa")
    ag_step(0, 3, 0)
    ag_step(0, 3, 1)
    student(3)
    gs0[...] = gf[1 - core].astype(BF16)
    g0 = grad_move(0, gs0, gr0, sib)
    g0.start()
    ag_step(1, 1, 0)
    recv("o", "1x")
    send("o", "2b")
    ag_step(1, 1, 1)
    with scope("Wg0"):
        g0.wait_recv()
    gf[core] = gf[core] + gr0[...].astype(F32)
    gs1[...] = gf[core].astype(BF16)
    for n in range(1, 8):
        grad_move(1, gs1.at[chip_n(n)], gr1.at[n - 1], chip_n(n) * 2 + core).start()
    send("o", "2c")
    ag_end(0, 0, 1)
    recv("o", "1s")
    early(0, 0, 0)
    ag_step(1, 2, 0)
    recv("o", "1b")
    send("o", "2xb", "2s")
    ag_step(1, 2, 1)
    recv("o", "1o")
    send("o", "3sa")
    ag_step(1, 3, 0)
    recv("o", "2s")
    early(1, 1, 0)
    early(2, -1, 0)
    ag_step(1, 3, 1)
    recv("o", "2a")
    send("o", "3x", "3sb")
    ag_end(1, 0)
    late(0, 0, 0, (0,))
    late(1, 1, 0, (0,))
    late(2, -1, 0, (0,))
    recv("o", "2b")
    send("o", "3y")
    recv("o", "3sa")
    early(3, 0, 1)
    late(3, 0, 1, (0,))

    ag_end(1, 1)
    late(0, 0, 0, (1,))
    late(1, 1, 0, (1,))
    late(2, -1, 0, (1,))
    late(3, 0, 1, (1,))
    recv("o", "3sb")
    early(4, 2, 0)
    late(4, 2, 0)
    with scope("Wgs"):
        landed(gr1, gr_recv.at[1])
    total = gf[core, chip]
    for n in range(1, 8):
        total = total + gr1[n - 1].astype(F32)
    ga[chip] = total.astype(BF16)
    for n in range(1, 8):
        grad_move(2, ga.at[chip], ga.at[chip], chip_n(n) * 2 + core).start()

    recv("o", "2c", "2xa", "2xb")
    send("o", "3sc")
    early(5, 1, 1, True)
    early(6, -1, 1, True)

    recv("o", "3sc")
    late(5, 1, 1, own=True)
    late(6, -1, 1, own=True)
    fourth("o")

    early(7, 2, 1, True)
    recv("o", "4s")
    late(7, 2, 1, own=True)

    with scope("Wga"):
        landed(ga.at[pl.ds(0, 7)], gr_recv.at[2])
    g6 = grad_move(3, ga, gfin.at[core], sib)
    g6.start()
    keep = pltpu.make_async_copy(ga, gfin.at[core], loc_sem.at[8])
    keep.start()
    with scope("Wg6"):
        landed(ga, gr_recv.at[3])
    with scope("Wship"):
        landed(stage, o_recv)

    with scope("Wsend"):

        @pl.when(own_column)
        def _():
            left(wo.at[0, pl.ds(0, 7 * 256)], wz_send)

        @pl.when(jnp.logical_not(own_column))
        def _():
            left(wo.at[0], wz_send)

        for index, buf, _, _ in kinds.values():
            left(buf.at[pl.ds(0, 15)], g_send.at[index])
        left(kvt.at[pl.ds(0, 7)], kz_send)
        for k in range(2):
            left(attb.at[k, :, pl.ds(0, 7 * 256)], ag_send.at[k])
        for n, ref in enumerate((gs0, gs1.at[pl.ds(0, 7)], gs1.at[pl.ds(0, 7)], ga)):
            left(ref, gr_send.at[n])
        left(stage, o_send)
        keep.wait()


def finish(hand_in, g_in, hand_ref, fg_ref, bg_ref, fg_v, bg_v, sem):
    hand_copy = pltpu.make_async_copy(hand_in, hand_ref, sem.at[0])
    hand_copy.start()
    copies = []
    for m in range(2):
        for h in range(4):
            fg_v[m, h, 0:64, :] = g_in[m, 2 * h, 0:64, :].astype(F32)
            fg_v[m, h, 64:128, :] = g_in[m, 2 * h + 1, 0:64, :].astype(F32)
            bg_v[m, h : h + 1, :] = g_in[m, 2 * h, 64:80, :].astype(F32)[0:1]
        copies.append(pltpu.make_async_copy(fg_v.at[m], fg_ref.at[m], sem.at[1 + m]))
        copies[m].start()
    copies.append(pltpu.make_async_copy(bg_v, bg_ref, sem.at[3]))
    copies[2].start()
    hand_copy.wait()
    for c in copies:
        c.wait()


def body(segment_input, attn_gain, query_weight, kv_weight, out_weight, fm_weight, fm_bias):
    cos, sin = rope_tables()
    cos2, sin2 = np.concatenate([cos, cos], axis=1), np.concatenate([-sin, sin], axis=1)
    tables = jnp.asarray(np.stack([cos2, sin2]))
    anywhere = pl.BlockSpec(memory_space=pl.ANY)
    vmem = pl.BlockSpec(memory_space=pltpu.VMEM)
    dma = pltpu.SemaphoreType.DMA
    hand, grads = pl.pallas_call(
        kernel,
        out_shape=(
            pltpu.VMEM((32, D), BF16),
            pltpu.VMEM((2, 8, 80, 128), BF16),
        ),
        in_specs=[anywhere] * 8,
        out_specs=(anywhere, anywhere),
        scratch_shapes=[
            pltpu.VMEM((SEQ, D), BF16),
            pltpu.VMEM((1, D), F32),
            pltpu.VMEM((2, 4, 128, 128), F32),
            pltpu.VMEM((2, 4, 128), F32),
            pltpu.VMEM((2, SEQ, 128), F32),
            pltpu.VMEM((16, SEQ, 512), BF16),
            pltpu.VMEM((16, 512, 128), BF16),
            pltpu.VMEM((16, 512, 256), BF16),
            pltpu.VMEM((16, 512, 256), BF16),
            pltpu.VMEM((16, 2048, 128), BF16),
            pltpu.VMEM((SEQ, 128), F32),
            pltpu.VMEM((SEQ, 512), F32),
            pltpu.VMEM((128, SEQ), BF16),
            pltpu.VMEM((8, 32, SEQ), BF16),
            pltpu.VMEM((SEQ, 128), BF16),
            pltpu.VMEM((128, SEQ), BF16),
            pltpu.VMEM((SEQ, 128), BF16),
            pltpu.VMEM((4, SEQ, 128), BF16),
            pltpu.VMEM((2, SEQ, 2048), BF16),
            pltpu.VMEM((8, SEQ, 128), F32),
            pltpu.VMEM((8, SEQ, 128), BF16),
            pltpu.VMEM((2, 8, 80, 128), F32),
            pltpu.VMEM((8, 80, 128), BF16),
            pltpu.VMEM((8, 80, 128), BF16),
            pltpu.VMEM((8, 80, 128), BF16),
            pltpu.VMEM((7, 80, 128), BF16),
            pltpu.VMEM((8, 80, 128), BF16),
            pltpu.SemaphoreType.REGULAR((6,)),
            dma((9,)),
            dma(()),
            dma((4,)),
            dma((4, len(STAGE_MOVES))),
            dma(()),
            dma(()),
            dma(()),
            dma(()),
            dma((2,)),
            dma((2, 8)),
            dma((4,)),
            dma((4,)),
            dma(()),
            dma(()),
        ],
        compiler_params=pltpu.CompilerParams(
            collective_id=0,
            has_side_effects=True,
            vmem_limit_bytes=60 * 1024 * 1024,
        ),
    )(
        segment_input[0],
        attn_gain,
        query_weight[0],
        kv_weight[0],
        out_weight[0],
        fm_weight[0],
        fm_bias[0],
        tables,
    )
    handoff, fg, bg = pl.pallas_call(
        finish,
        out_shape=(
            jax.ShapeDtypeStruct((32, D), BF16),
            jax.ShapeDtypeStruct((2, 4, 128, 128), F32),
            jax.ShapeDtypeStruct((2, 4, 128), F32),
        ),
        in_specs=[vmem, vmem],
        out_specs=(anywhere, anywhere, anywhere),
        scratch_shapes=[
            pltpu.VMEM((2, 4, 128, 128), F32),
            pltpu.VMEM((2, 4, 128), F32),
            dma((4,)),
        ],
    )(
        pltpu.with_memory_space_constraint(hand, pltpu.MemorySpace.VMEM),
        pltpu.with_memory_space_constraint(grads, pltpu.MemorySpace.VMEM),
    )
    return handoff[None], fg[None], bg[None]


def solution(mesh):
    placed = (
        P("segment", "dp", None),
        P("segment", None),
        P("segment", "dp", "tensor"),
        P("segment", "dp", "tensor"),
        P("segment", "tensor", "dp"),
        P("segment", None, "tensor", None, None),
        P("segment", None, "tensor", None),
    )
    return jax.shard_map(
        body,
        mesh=mesh,
        in_specs=placed,
        out_specs=(
            P("segment", ("dp", "tensor"), None),
            P("segment", None, "tensor", None, None),
            P("segment", None, "tensor", None),
        ),
        check_vma=False,
    )
```

```python
import jax
import jax.numpy as jnp
import numpy as np
from jax import lax
from jax.experimental import pallas as pl
from jax.experimental.pallas import tpu as pltpu
from jax.sharding import PartitionSpec as P

MESH = pl.DeviceIdType.MESH
F32 = jnp.float32
BF16 = jnp.bfloat16
D = 8192
SEQ = 256
TOKENS = 4096
EPSILON = 1e-05
ROPE_BASE = 500000.0
SCALE = 128 ** (-0.5)

STAGE_MOVES = {
    "1a": [("yp", 0, 0, 0, 2), ("ym", 0, 0, 2, 4)],
    "1b": [("yp", 0, 0, 2, 4), ("ym", 0, 0, 0, 2)],
    "1x": [("x", 0, 0, 1, 3)],
    "1o": [("x", 0, 0, 0, 1), ("x", 0, 0, 3, 4)],
    "1s": [("s", 0, 0, 0, 4)],
    "2a": [("yp", -1, 0, 0, 2), ("ym", 1, 0, 2, 4)],
    "2b": [("yp", 0, 1, 1, 2), ("ym", 0, 1, 2, 3)],
    "2c": [("yp", 0, 1, 2, 3), ("ym", 0, 1, 1, 2)],
    "2xa": [("x", -1, 0, 0, 1), ("x", 1, 0, 3, 4)],
    "2xb": [("x", -1, 0, 3, 4), ("x", 1, 0, 0, 1)],
    "2s": [("s", -1, 0, 0, 4), ("s", 1, 0, 0, 4)],
    "3y": [("yp", -1, 1, 1, 2), ("ym", 1, 1, 2, 3)],
    "3x": [("x", 2, 0, 0, 1), ("x", 2, 0, 3, 4)],
    "3sa": [("s", 0, 1, 0, 4)],
    "3sb": [("s", 2, 0, 0, 4)],
    "3sc": [("s", -1, 1, 0, 4), ("s", 1, 1, 0, 4)],
    "4s": [("s", 2, 1, 0, 4)],
}
STAGE_INDEX = {name: n for n, name in enumerate(STAGE_MOVES)}
CUTS = (0, 112, 256, 400, 512)
CUTS_OUT = (0, 304, 1024, 1744, 2048)


def rope_tables():
    half = 64
    frequency = ROPE_BASE ** (-(np.arange(half, dtype=np.float64) * (2.0 / 128)))
    angles = np.arange(SEQ, dtype=np.float64)[:, None] * frequency[None, :]
    return np.cos(angles).astype(np.float32), np.sin(angles).astype(np.float32)


def mm(a, b):
    return jnp.dot(a, b, preferred_element_type=F32)


def mm_nt(a, b):
    return lax.dot_general(a, b, (((1,), (1,)), ((), ())), preferred_element_type=F32)


def mm_tn(a, b):
    return lax.dot_general(a, b, (((0,), (0,)), ((), ())), preferred_element_type=F32)


def kernel(
    x_hbm,
    gain_hbm,
    wq_hbm,
    wkv_hbm,
    wo_hbm,
    fmw_hbm,
    fmb_hbm,
    tab_hbm,
    hand_hbm,
    gfin,
    x_ref,
    gain_ref,
    fmw_ref,
    fmb_ref,
    tab_ref,
    nrm,
    wkv,
    wqa,
    wqb,
    wo,
    kvacc,
    qacc,
    kvs,
    kvt,
    k_ref,
    kt_ref,
    v_ref,
    qrot,
    attb,
    part,
    stage,
    gf,
    gs0,
    gr0,
    gs1,
    gr1,
    ga,
    here_sem,
    loc_sem,
    idle_sem,
    g_send,
    g_recv,
    wz_send,
    wz_recv,
    kz_send,
    kz_recv,
    ag_send,
    ag_recv,
    gr_send,
    gr_recv,
    o_send,
    o_recv,
):
    dp = lax.axis_index("dp")
    seg = lax.axis_index("segment")
    t = lax.axis_index("tensor")
    core = dp % 2
    chip = dp // 2
    xl = chip % 2
    y = chip // 2
    sib = chip * 2 + (1 - core)
    xp = (y * 2 + (1 - xl)) * 2 + core
    yp = (dp + 4) % 16
    ym = (dp + 12) % 16
    peer = {"yp": yp, "ym": ym, "x": xp, "s": sib}

    def scope(name):
        return jax.named_scope(name)

    def remote(src, dst, ssem, rsem, dev):
        return pltpu.make_async_remote_copy(
            src_ref=src,
            dst_ref=dst,
            send_sem=ssem,
            recv_sem=rsem,
            device_id=dev,
            device_id_type=MESH,
        )

    def landed(ref, sem):
        remote(ref, ref, idle_sem, sem, {"dp": sib}).wait_recv()

    def left(ref, sem):
        remote(ref, ref, sem, idle_sem, {"dp": sib}).wait_send()

    barrier = pltpu.get_barrier_semaphore()
    above, below = {"tensor": (t + 1) % 8}, {"tensor": (t + 7) % 8}
    peers = [{"segment": 1 - seg, "dp": xp}, above, below, {"dp": yp}, {"dp": ym}, {"dp": xp}]
    peers.append({"dp": sib})
    for p in peers:
        pl.semaphore_signal(barrier, inc=1, device_id=p, device_id_type=MESH)

    local = {}
    for n, (name, src, dst) in enumerate(
        (
            ("x", x_hbm, x_ref),
            ("gain", gain_hbm, gain_ref),
            ("kv", wkv_hbm, wkv.at[dp]),
            ("qa", wq_hbm.at[:, pl.ds(0, 256)], wqa.at[dp]),
            ("qb", wq_hbm.at[:, pl.ds(256, 256)], wqb.at[dp]),
            ("tab", tab_hbm, tab_ref),
            ("fmw", fmw_hbm, fmw_ref),
            ("fmb", fmb_hbm, fmb_ref),
        )
    ):
        local[name] = pltpu.make_async_copy(src, dst, loc_sem.at[n])
        local[name].start()

    def chip_at(dy, dx):
        return ((y + dy + 4) % 4) * 2 + (xl + dx) % 2

    def slot_of(dy, dx, c):
        return chip_at(dy, dx) * 2 + c

    with scope("barrier"):
        pl.semaphore_wait(barrier, len(peers))

    steps = [[{"dp": xp}], [{"dp": ym}]] + [[above, below]] * 4

    def tell(n):
        for p in steps[n]:
            pl.semaphore_signal(here_sem.at[n], inc=1, device_id=p, device_id_type=MESH)

    def hear(n):
        with scope("hear%d" % n):
            pl.semaphore_wait(here_sem.at[n], len(steps[n]))

    kinds = {
        "kv": (0, wkv, lambda lo, hi: wkv_hbm.at[pl.ds(lo, hi - lo)], CUTS),
        "qa": (1, wqa, lambda lo, hi: wq_hbm.at[pl.ds(lo, hi - lo), pl.ds(0, 256)], CUTS),
        "qb": (2, wqb, lambda lo, hi: wq_hbm.at[pl.ds(lo, hi - lo), pl.ds(256, 256)], CUTS),
        "o": (3, wo, None, CUTS_OUT),
    }

    def move(kind, stage_name, which):
        index, buf, own, cuts = kinds[kind]
        direction, dy, dx, lo, hi = STAGE_MOVES[stage_name][which]
        lo, hi = cuts[lo], cuts[hi]
        slot = slot_of(dy, dx, core)
        dst = buf.at[slot, pl.ds(lo, hi - lo)]
        src = own(lo, hi) if (own is not None and dy == 0 and dx == 0) else dst
        recv_sem = g_recv.at[index, STAGE_INDEX[stage_name]]
        return remote(src, dst, g_send.at[index], recv_sem, {"dp": peer[direction]})

    def send(kind, *names):
        for name in names:
            for which in range(len(STAGE_MOVES[name])):
                move(kind, name, which).start()

    def recv(kind, *names):
        index, buf, _, cuts = kinds[kind]
        with scope("W_%s_%s" % (kind, "_".join(names))):
            for name in names:
                rows = sum(cuts[m[4]] - cuts[m[3]] for m in STAGE_MOVES[name])
                ref = buf.at[pl.ds(0, 2)] if rows > cuts[4] else buf.at[0, pl.ds(0, rows)]
                landed(ref, g_recv.at[index, STAGE_INDEX[name]])

    def first(kind):
        send(kind, "1a", "1x", "1b", "1o", "1s")

    def wz(p, k):
        dst_dp = chip * 2 + k
        return remote(
            wo_hbm.at[pl.ds(k * 256, 256), pl.ds(p * 128, 128)],
            wo.at[dst_dp, pl.ds(pl.multiple_of(t * 256, 256), 256)],
            wz_send,
            wz_recv,
            {"dp": dst_dp, "tensor": 2 * p + core},
        )

    def wz_local(p, k):
        return pltpu.make_async_copy(
            wo_hbm.at[pl.ds(k * 256, 256), pl.ds(p * 128, 128)],
            wo.at[chip * 2 + k, pl.ds(pl.multiple_of(t * 256, 256), 256)],
            loc_sem.at[8],
        )

    def is_self(p, k):
        return jnp.logical_and(t == 2 * p + core, core == k)

    send("kv", "1a", "1x")
    tell(0)

    def norm_rows(r, carry):
        rows = pl.ds(pl.multiple_of(r * 16, 16), 16)
        total = jnp.zeros((16, 512), F32)
        for j in range(16):
            v = x_ref[rows, j * 512 : (j + 1) * 512].astype(F32)
            total = total + v * v
        inv = lax.rsqrt(jnp.sum(total, axis=-1, keepdims=True) * (1.0 / D) + EPSILON)
        for j in range(16):
            v = x_ref[rows, j * 512 : (j + 1) * 512].astype(F32)
            nrm[j, rows, :] = (v * inv * gain_ref[:, j * 512 : (j + 1) * 512]).astype(BF16)
        return carry

    local["x"].wait()
    local["gain"].wait()
    with scope("norm1"):
        lax.fori_loop(0, 2, norm_rows, 0)
    send("kv", "1b", "1o", "1s")
    hear(0)
    tell(1)
    with scope("norm1"):
        lax.fori_loop(2, 6, norm_rows, 0)
    first("qa")
    hear(1)
    tell(2)
    recv("kv", "1a")
    send("kv", "2a", "2xa")
    recv("kv", "1x")
    send("kv", "2b", "2c")
    hear(2)
    tell(3)
    with scope("norm2"):
        lax.fori_loop(6, 16, norm_rows, 0)
    recv("kv", "1b")
    send("kv", "2xb", "2s")
    hear(3)
    tell(4)
    recv("qa", "1a")
    send("qa", "2a", "2xa")
    recv("qa", "1x")
    send("qa", "2b")
    hear(4)
    tell(5)

    def eat(name, acc, buf, cols, start, wave):
        def add(n, carry):
            if wave == 1:
                dy, dx = n + 3, 0
            elif wave == 2:
                dy, dx = n + 3, 1 - n // 3
            else:
                dy, dx = n + 2, 1
            slot = slot_of(dy, dx, 0)
            acc[:, cols[0] : cols[1]] += mm(nrm[slot], buf[slot]) + mm(nrm[slot + 1], buf[slot + 1])
            return carry

        with scope("eat_%s%d" % (name, wave)):
            if start:
                acc[:, cols[0] : cols[1]] = jnp.zeros((SEQ, cols[1] - cols[0]), F32)
            lax.fori_loop(0, {1: 3, 2: 4, 3: 1}[wave], add, 0)

    def fourth(kind):
        recv(kind, "3y", "3x")
        send(kind, "4s")

    def done2(kind):
        recv(kind, "2c", "2xa", "2xb", "1o")
        send(kind, "3sb", "3sa", "3sc")

    hear(5)
    for p in range(4):
        for k in range(2):

            @pl.when(jnp.logical_not(is_self(p, k)))
            def _(p=p, k=k):
                wz(p, k).start()

            @pl.when(is_self(p, k))
            def _(p=p, k=k):
                wz_local(p, k).start()

    recv("kv", "2a")
    send("kv", "3x")
    recv("kv", "2b")
    send("kv", "3y")
    send("qa", "2c")
    recv("qa", "1b")
    send("qa", "2xb", "2s")
    send("qb", "1a", "1x")
    done2("kv")
    local["kv"].wait()
    recv("kv", "1s", "2s")
    eat("kv", kvacc, wkv, (0, 128), True, 1)
    recv("qa", "2a")
    send("qa", "3x")
    recv("qa", "2b")
    send("qa", "3y")
    fourth("kv")
    recv("kv", "3sa", "3sb", "3sc")
    eat("kv", kvacc, wkv, (0, 128), False, 2)
    done2("qa")
    send("qb", "1b", "1o", "1s")
    recv("kv", "4s")
    eat("kv", kvacc, wkv, (0, 128), False, 3)

    r_i = lax.broadcasted_iota(jnp.int32, (128, 128), 0)
    c_i = lax.broadcasted_iota(jnp.int32, (128, 128), 1)
    pick = (c_i == (r_i & 31) * 4 + (r_i >> 5)).astype(BF16)
    kvs[...] = mm_nt(pick, kvacc[...].astype(BF16)).astype(BF16)

    def kz(d):
        dest = (t + d) % 8
        return remote(
            kvs.at[pl.ds(pl.multiple_of((dest // 2) * 32, 32), 32)],
            kvt.at[t],
            kz_send,
            kz_recv,
            {"tensor": dest},
        )

    for d in range(1, 8):
        kz(d).start()
    kvt[t] = kvs[pl.ds(pl.multiple_of((t // 2) * 32, 32), 32), :]

    recv("qb", "1a")
    send("qb", "2a", "2xa")
    recv("qb", "1x")
    send("qb", "2b", "2c")
    local["qa"].wait()
    recv("qa", "1s", "2s")
    eat("qa", qacc, wqa, (0, 256), True, 1)
    fourth("qa")
    recv("qa", "3sa", "3sb", "3sc")
    eat("qa", qacc, wqa, (0, 256), False, 2)
    local["tab"].wait()
    with scope("Wkz"):
        landed(kvt.at[pl.ds(0, 7)], kz_recv)
    kall = kvt[0:4].reshape(128, SEQ).astype(F32)
    k1, k2 = kall[0:64], kall[64:128]
    ct, st = tab_ref[0].T[0:64], tab_ref[1].T[64:128]
    krot = jnp.concatenate([k1 * ct - k2 * st, k2 * ct + k1 * st], axis=0)
    kt_ref[...] = krot.astype(BF16)
    k_ref[...] = krot.T.astype(BF16)
    v_ref[...] = kvt[4:8].reshape(128, SEQ).astype(F32).T.astype(BF16)

    recv("qa", "4s")
    eat("qa", qacc, wqa, (0, 256), False, 3)

    row_i = lax.broadcasted_iota(jnp.int32, (SEQ, SEQ), 0)
    col_i = lax.broadcasted_iota(jnp.int32, (SEQ, SEQ), 1)
    mask = row_i >= col_i

    def attend(h):
        with scope("attend%d" % h):
            q = qacc[:, h * 128 : (h + 1) * 128]
            q = (q * tab_ref[0] + pltpu.roll(q, 64, 1) * tab_ref[1]).astype(BF16)
            qrot[h] = q
            scores = mm(q, kt_ref[...]) * SCALE
            scores = jnp.where(mask, scores, -jnp.inf)
            lifted = jnp.exp(scores - jnp.max(scores, axis=-1, keepdims=True))
            prob = (lifted / jnp.sum(lifted, axis=-1, keepdims=True)).astype(BF16)
            c0 = (h % 2) * 128
            cols = pl.ds(pl.multiple_of(t * 256 + c0, 128), 128)
            attb[h // 2, :, cols] = mm(prob, v_ref[...]).astype(BF16)

    def ag(k, s, up, half):
        slot = (t + 8 - s) % 8 if up else (t + s) % 8
        ref = attb.at[k, pl.ds(half * 128, 128), pl.ds(pl.multiple_of(slot * 256, 256), 256)]
        dest = (t + 1) % 8 if up else (t + 7) % 8
        return remote(ref, ref, ag_send.at[k], ag_recv.at[k, 2 * s + half], {"tensor": dest})

    def ag_step(k, s, half):
        if s > 0:
            with scope("Wag%d_%d_%d" % (k, s, half)):
                landed(attb.at[k, :, pl.ds(0, 256)], ag_recv.at[k, 2 * s - 2 + half])
        if s < 3 or half == 0:
            ag(k, s, True, half).start()
        if s < 3 or half == 1:
            ag(k, s, False, half).start()

    def ag_end(k, *halves):
        for half in halves:
            with scope("Wag%d_end%d" % (k, half)):
                landed(attb.at[k, pl.ds(0, 128), pl.ds(0, 256)], ag_recv.at[k, 6 + half])

    lead = (lax.broadcasted_iota(jnp.int32, (8, 128), 0) == 0).astype(F32)

    def feature(z):
        e = jnp.exp(jnp.minimum(z, 0.0))
        pos = z > 0
        return jnp.where(pos, z + 1.0, e).astype(BF16), jnp.where(pos, 1.0, e)

    def pre(a, m, h):
        w = fmw_ref[m, h]
        hi = w.astype(BF16)
        low = (w - hi.astype(F32)).astype(BF16)
        return mm(a, hi) + mm(a, low) + fmb_ref[m, pl.ds(h, 1), :]

    def put(m, h, weight, bias):
        gf[m, 2 * h, 0:64, :] = weight[0:64]
        gf[m, 2 * h + 1, 0:64, :] = weight[64:128]
        gf[m, 2 * h, 64:72, :] = bias * lead
        gf[m, 2 * h + 1, 64:72, :] = jnp.zeros((8, 128), F32)

    def student(h):
        with scope("student%d" % h):
            q, k, v = qrot[h], k_ref[...], v_ref[...]
            cols = pl.ds(pl.multiple_of(t * 256 + (h % 2) * 128, 128), 128)
            att = attb[h // 2, :, cols].astype(F32)
            qf, qd = feature(pre(q, 0, h))
            kf, kd = feature(pre(k, 1, h))
            aff = jnp.where(mask, mm_nt(qf, kf), 0.0)
            den = jnp.sum(aff, axis=-1, keepdims=True)
            out = mm(aff.astype(BF16), v) / den
            dnum = ((out - att) * (2.0 / TOKENS) / den).astype(BF16)
            dden = jnp.sum(dnum.astype(F32) * out, axis=-1, keepdims=True)
            daff = jnp.where(mask, mm_nt(dnum, v) - dden, 0.0).astype(BF16)
            dzq = mm(daff, kf) * qd
            dzk = mm_tn(daff, qf) * kd
            put(0, h, mm_tn(q, dzq.astype(BF16)), jnp.sum(dzq, axis=0, keepdims=True))
            put(1, h, mm_tn(k, dzk.astype(BF16)), jnp.sum(dzk, axis=0, keepdims=True))

    attend(0)
    attend(1)
    ag_step(0, 0, 0)
    ag_step(0, 0, 1)
    recv("qb", "1b")
    send("qb", "2xb", "2s")
    local["fmw"].wait()
    local["fmb"].wait()
    student(0)
    recv("qb", "2a")
    send("qb", "3x")
    recv("qb", "2b")
    send("qb", "3y")

    own_column = core == t % 2

    with scope("Wwz"):

        @pl.when(own_column)
        def _():
            wz_local(0, 0).wait()
            landed(wo.at[0, pl.ds(0, 7 * 256)], wz_recv)

        @pl.when(jnp.logical_not(own_column))
        def _():
            landed(wo.at[0], wz_recv)

    send("o", "1a", "1x")
    ag_step(0, 1, 0)
    ag_step(0, 1, 1)

    def column(plane, c):
        return pl.multiple_of((2 * c + plane % 2) * 512 + (plane // 2) * 128, 128)

    def ship(n, dy, dx, dest):
        return remote(
            stage.at[n, pl.ds(pl.multiple_of(dest * 32, 32), 32)],
            hand_hbm.at[:, pl.ds(column(t, chip_at(dy, dx)), 128)],
            o_send,
            o_recv,
            {"segment": 1 - seg, "tensor": dest},
        )

    def early(n, dy, dx, own=False):
        with scope("early%d" % n):
            c = chip_at(dy, dx)
            k = core if own else 0
            part[n] = x_ref[:, pl.ds(column(t, c), 128)].astype(F32) + mm(attb[k], wo[2 * c + k])

    def late(n, dy, dx, halves=(0, 1), own=False):
        with scope("late%d" % n):
            c = chip_at(dy, dx)
            k = 1 - core if own else 1
            lo, hi = halves[0] * 128, halves[-1] * 128 + 128
            product = mm(attb[k, lo:hi], wo[2 * c + k])
            stage[n, lo:hi] = (part[n, lo:hi] + product).astype(BF16)
            for half in halves:
                for j in (2, 1, 3, 0):
                    ship(n, dy, dx, half * 4 + (t + j) % 4).start()

    def grad_move(n, src, dst, dev):
        return remote(src, dst, gr_send.at[n], gr_recv.at[n], {"dp": dev})

    def chip_n(n):
        return chip_at(n % 4, n // 4)

    done2("qb")
    local["qb"].wait()
    recv("qb", "1s", "2s")
    eat("qb", qacc, wqb, (256, 512), True, 1)
    student(1)
    fourth("qb")
    recv("qb", "3sa", "3sb", "3sc")
    send("o", "1b", "1o", "1s")
    ag_step(0, 2, 0)
    ag_step(0, 2, 1)
    eat("qb", qacc, wqb, (256, 512), False, 2)
    recv("qb", "4s")
    eat("qb", qacc, wqb, (256, 512), False, 3)
    attend(2)
    attend(3)
    ag_step(1, 0, 0)
    student(2)
    ag_step(1, 0, 1)
    recv("o", "1a")
    send("o", "2a", "2xa")
    ag_step(0, 3, 0)
    ag_step(0, 3, 1)
    student(3)
    gs0[...] = gf[1 - core].astype(BF16)
    g0 = grad_move(0, gs0, gr0, sib)
    g0.start()
    ag_step(1, 1, 0)
    recv("o", "1x")
    send("o", "2b")
    ag_step(1, 1, 1)
    with scope("Wg0"):
        g0.wait_recv()
    gf[core] = gf[core] + gr0[...].astype(F32)
    gs1[...] = gf[core].astype(BF16)
    for n in range(1, 8):
        grad_move(1, gs1.at[chip_n(n)], gr1.at[n - 1], chip_n(n) * 2 + core).start()
    send("o", "2c")
    ag_end(0, 0, 1)
    recv("o", "1s")
    early(0, 0, 0)
    ag_step(1, 2, 0)
    recv("o", "1b")
    send("o", "2xb", "2s")
    ag_step(1, 2, 1)
    recv("o", "1o")
    send("o", "3sa")
    ag_step(1, 3, 0)
    recv("o", "2s")
    early(1, 1, 0)
    early(2, -1, 0)
    ag_step(1, 3, 1)
    recv("o", "2a")
    send("o", "3x", "3sb")
    ag_end(1, 0)
    late(0, 0, 0, (0,))
    late(1, 1, 0, (0,))
    late(2, -1, 0, (0,))
    recv("o", "2b")
    send("o", "3y")
    recv("o", "3sa")
    early(3, 0, 1)
    late(3, 0, 1, (0,))

    ag_end(1, 1)
    late(0, 0, 0, (1,))
    late(1, 1, 0, (1,))
    late(2, -1, 0, (1,))
    late(3, 0, 1, (1,))
    recv("o", "3sb")
    early(4, 2, 0)
    late(4, 2, 0)
    with scope("Wgs"):
        landed(gr1, gr_recv.at[1])
    total = gf[core, chip]
    for n in range(1, 8):
        total = total + gr1[n - 1].astype(F32)
    ga[chip] = total.astype(BF16)
    for n in range(1, 8):
        grad_move(2, ga.at[chip], ga.at[chip], chip_n(n) * 2 + core).start()

    recv("o", "2c", "2xa", "2xb")
    send("o", "3sc")
    early(5, 1, 1, True)
    early(6, -1, 1, True)

    recv("o", "3sc")
    late(5, 1, 1, own=True)
    late(6, -1, 1, own=True)
    fourth("o")

    early(7, 2, 1, True)
    recv("o", "4s")
    late(7, 2, 1, own=True)

    with scope("Wga"):
        landed(ga.at[pl.ds(0, 7)], gr_recv.at[2])
    g6 = grad_move(3, ga, gfin.at[core], sib)
    g6.start()
    keep = pltpu.make_async_copy(ga, gfin.at[core], loc_sem.at[8])
    keep.start()
    with scope("Wg6"):
        landed(ga, gr_recv.at[3])
    with scope("Wship"):
        landed(stage, o_recv)

    with scope("Wsend"):

        @pl.when(own_column)
        def _():
            left(wo.at[0, pl.ds(0, 7 * 256)], wz_send)

        @pl.when(jnp.logical_not(own_column))
        def _():
            left(wo.at[0], wz_send)

        for index, buf, _, _ in kinds.values():
            left(buf.at[pl.ds(0, 15)], g_send.at[index])
        left(kvt.at[pl.ds(0, 7)], kz_send)
        for k in range(2):
            left(attb.at[k, :, pl.ds(0, 7 * 256)], ag_send.at[k])
        for n, ref in enumerate((gs0, gs1.at[pl.ds(0, 7)], gs1.at[pl.ds(0, 7)], ga)):
            left(ref, gr_send.at[n])
        left(stage, o_send)
        keep.wait()


def finish(hand_in, g_in, hand_ref, fg_ref, bg_ref, fg_v, bg_v, sem):
    hand_copy = pltpu.make_async_copy(hand_in, hand_ref, sem.at[0])
    hand_copy.start()
    copies = []
    for m in range(2):
        for h in range(4):
            fg_v[m, h, 0:64, :] = g_in[m, 2 * h, 0:64, :].astype(F32)
            fg_v[m, h, 64:128, :] = g_in[m, 2 * h + 1, 0:64, :].astype(F32)
            bg_v[m, h : h + 1, :] = g_in[m, 2 * h, 64:72, :].astype(F32)[0:1]
        copies.append(pltpu.make_async_copy(fg_v.at[m], fg_ref.at[m], sem.at[1 + m]))
        copies[m].start()
    copies.append(pltpu.make_async_copy(bg_v, bg_ref, sem.at[3]))
    copies[2].start()
    hand_copy.wait()
    for c in copies:
        c.wait()


def body(segment_input, attn_gain, query_weight, kv_weight, out_weight, fm_weight, fm_bias):
    cos, sin = rope_tables()
    cos2, sin2 = np.concatenate([cos, cos], axis=1), np.concatenate([-sin, sin], axis=1)
    tables = jnp.asarray(np.stack([cos2, sin2]))
    anywhere = pl.BlockSpec(memory_space=pl.ANY)
    vmem = pl.BlockSpec(memory_space=pltpu.VMEM)
    dma = pltpu.SemaphoreType.DMA
    hand, grads = pl.pallas_call(
        kernel,
        out_shape=(
            pltpu.VMEM((32, D), BF16),
            pltpu.VMEM((2, 8, 72, 128), BF16),
        ),
        in_specs=[anywhere] * 8,
        out_specs=(anywhere, anywhere),
        scratch_shapes=[
            pltpu.VMEM((SEQ, D), BF16),
            pltpu.VMEM((1, D), F32),
            pltpu.VMEM((2, 4, 128, 128), F32),
            pltpu.VMEM((2, 4, 128), F32),
            pltpu.VMEM((2, SEQ, 128), F32),
            pltpu.VMEM((16, SEQ, 512), BF16),
            pltpu.VMEM((16, 512, 128), BF16),
            pltpu.VMEM((16, 512, 256), BF16),
            pltpu.VMEM((16, 512, 256), BF16),
            pltpu.VMEM((16, 2048, 128), BF16),
            pltpu.VMEM((SEQ, 128), F32),
            pltpu.VMEM((SEQ, 512), F32),
            pltpu.VMEM((128, SEQ), BF16),
            pltpu.VMEM((8, 32, SEQ), BF16),
            pltpu.VMEM((SEQ, 128), BF16),
            pltpu.VMEM((128, SEQ), BF16),
            pltpu.VMEM((SEQ, 128), BF16),
            pltpu.VMEM((4, SEQ, 128), BF16),
            pltpu.VMEM((2, SEQ, 2048), BF16),
            pltpu.VMEM((8, SEQ, 128), F32),
            pltpu.VMEM((8, SEQ, 128), BF16),
            pltpu.VMEM((2, 8, 72, 128), F32),
            pltpu.VMEM((8, 72, 128), BF16),
            pltpu.VMEM((8, 72, 128), BF16),
            pltpu.VMEM((8, 72, 128), BF16),
            pltpu.VMEM((7, 72, 128), BF16),
            pltpu.VMEM((8, 72, 128), BF16),
            pltpu.SemaphoreType.REGULAR((6,)),
            dma((9,)),
            dma(()),
            dma((4,)),
            dma((4, len(STAGE_MOVES))),
            dma(()),
            dma(()),
            dma(()),
            dma(()),
            dma((2,)),
            dma((2, 8)),
            dma((4,)),
            dma((4,)),
            dma(()),
            dma(()),
        ],
        compiler_params=pltpu.CompilerParams(
            collective_id=0,
            has_side_effects=True,
            vmem_limit_bytes=60 * 1024 * 1024,
        ),
    )(
        segment_input[0],
        attn_gain,
        query_weight[0],
        kv_weight[0],
        out_weight[0],
        fm_weight[0],
        fm_bias[0],
        tables,
    )
    handoff, fg, bg = pl.pallas_call(
        finish,
        out_shape=(
            jax.ShapeDtypeStruct((32, D), BF16),
            jax.ShapeDtypeStruct((2, 4, 128, 128), F32),
            jax.ShapeDtypeStruct((2, 4, 128), F32),
        ),
        in_specs=[vmem, vmem],
        out_specs=(anywhere, anywhere, anywhere),
        scratch_shapes=[
            pltpu.VMEM((2, 4, 128, 128), F32),
            pltpu.VMEM((2, 4, 128), F32),
            dma((4,)),
        ],
    )(
        pltpu.with_memory_space_constraint(hand, pltpu.MemorySpace.VMEM),
        pltpu.with_memory_space_constraint(grads, pltpu.MemorySpace.VMEM),
    )
    return handoff[None], fg[None], bg[None]


def solution(mesh):
    placed = (
        P("segment", "dp", None),
        P("segment", None),
        P("segment", "dp", "tensor"),
        P("segment", "dp", "tensor"),
        P("segment", "tensor", "dp"),
        P("segment", None, "tensor", None, None),
        P("segment", None, "tensor", None),
    )
    return jax.shard_map(
        body,
        mesh=mesh,
        in_specs=placed,
        out_specs=(
            P("segment", ("dp", "tensor"), None),
            P("segment", None, "tensor", None, None),
            P("segment", None, "tensor", None),
        ),
        check_vma=False,
    )
```
